32 devices in a mesh: grp: 2 (over y), gz: 4 (over z), ma: 2 (over x), dev: 2 (over core).
Axes of the slice: x: 2, y: 2, z: 4, core: 2. Of those that a mesh axis runs over, the one named last changes fastest.
Arguments:
- patches: bfloat16 [128, 512, 768], P(('grp', 'gz', 'dev')), parts along dimension 0, may hold values from -6 to 6
- cls_rows: bfloat16 [128, 768], P(('grp', 'gz', 'dev')), parts along dimension 0, may hold values from -6 to 6
- w_query: bfloat16 [768, 768], P(None, 'ma'), may hold values from -0.21875 to 0.21875
- w_key: bfloat16 [768, 768], P(None, 'ma'), may hold values from -0.21875 to 0.21875
- w_value: bfloat16 [768, 768], P(None, 'ma'), may hold values from -0.21875 to 0.21875
- w_out: bfloat16 [768, 768], P('ma'), may hold values from -0.21875 to 0.21875
- a_query: bfloat16 [768, 768], P(None, 'ma'), may hold values from -0.21875 to 0.21875
- a_key: bfloat16 [768, 768], P(None, 'ma'), may hold values from -0.21875 to 0.21875
- a_value: bfloat16 [768, 768], P(None, 'ma'), may hold values from -0.21875 to 0.21875
- a_out: bfloat16 [768, 768], P('ma'), may hold values from -0.21875 to 0.21875
- upstream: bfloat16 [16, 16, 768], P(('grp', 'gz', 'dev')), parts along dimension 0, may hold values from -6 to 6
- slice_to_scan: int32 [128], P('grp'), parts along dimension 0, may hold values from 0 to 3, never falling along the last dimension, each value on 1 to 32 neighbouring positions
Outputs:
- grad_query: float32 [1536, 768], P(('grp', 'gz', 'dev'), 'ma'), parts along dimension 0
- grad_key: float32 [1536, 768], P(('grp', 'gz', 'dev'), 'ma'), parts along dimension 0
- grad_value: float32 [1536, 768], P(('grp', 'gz', 'dev'), 'ma'), parts along dimension 0
- grad_out_t: float32 [1536, 768], P(('grp', 'gz', 'dev'), 'ma'), parts along dimension 0
The draws below stay inside these ranges and needn't reach their ends.
There are 2 independent parts, one for each index of `grp`. The reference program is written for one: setup_inputs(seed, part) draws one part's arguments, and reference() takes and returns one part's arrays. A program takes and returns all parts, laid end to end along the dimension named above; an argument that names none is the same for every part. Nothing has to cross between parts.
Inputs may be any that keep to these rules, and one draw needn't show every extreme that they name: `slice_to_scan`: scan numbers never fall along the slices; each of the 4 scans covers 1 to 32 consecutive slices.
All inputs are finite; a program needn't handle non-finite values.
Results may differ from the reference program's by a relative error of at most 0.017.
Values may be sent and summed in bfloat16 or wider, within the bound.
No kernel may reach another device: no remote copies, remote signals or barrier semaphores. Data moves between devices by JAX's collectives and lax.ppermute only.
A program may use at most 128 MiB of HBM per device.

```python
import math
import jax
import jax.numpy as jnp
import numpy as np
from jax import lax

MODEL_DIM = 768
H = 12
HD = 64
P_SIZE = 512
SLICES_PER_DEVICE = 8
SLICE_TOTAL = 64
WINDOW_COUNT = 8
WROWS = 16
SCANS = 4
SCAN_MOST = 32


def block_levels(stream_key, extent, shards, least, largest):
    factor_of = 1.0
    for position, parts in shards:
        draws = jax.random.uniform(jax.random.fold_in(jax.random.fold_in(stream_key, 6), position), (parts,), jnp.float32, least / len(shards), largest / len(shards))
        factor_of = factor_of * jnp.repeat(jnp.exp(draws), extent[position] // parts).reshape((-1,) + (1,) * (len(extent) - 1 - position))
    return factor_of


def split_up(amount, total, bound, slope):
    weights = [(1 << 20) // math.isqrt(standing ** slope) + 1 for standing in range(2, amount + 1)]
    spare, given = total - bound - (amount - 1), [1] * (amount - 1)
    while spare > 0:
        movable = [i for i in range(amount - 1) if given[i] < bound]
        mass, remaining = sum([weights[i] for i in movable]), spare
        for i in movable:
            more = min(bound - given[i], max(1, remaining * weights[i] // mass), spare)
            given[i] = given[i] + more
            spare = spare - more
    return np.array([bound] + given)


def uneven(stream_key, amount, total, reach, lean):
    if amount == 2:
        one = jax.random.randint(stream_key, (), max(1, total - reach), min(reach, total - 1) + 1)
        return jnp.stack([one, total - one])
    lengths = jnp.asarray(split_up(amount, total, reach, lean), jnp.int32)
    twos = (amount - 1) // 2
    source_of, sink = lengths[1:1 + 2 * twos:2], lengths[2:2 + 2 * twos:2]
    slack = jnp.minimum(source_of - 1, reach - sink)
    passed = jax.random.randint(jax.random.fold_in(stream_key, 1), (twos,), 0, 1 << 20) % (slack + 1)
    lengths = lengths.at[1:1 + 2 * twos:2].set(source_of - passed).at[2:2 + 2 * twos:2].set(sink + passed)
    return lengths[jax.random.permutation(jax.random.fold_in(stream_key, 2), amount)]


def normal_values(stream_key, dims, deviation, reach, pieces=(), kind=jnp.bfloat16):
    array = jax.random.normal(stream_key, dims, jnp.float32) * deviation
    if len(pieces) > 0:
        array = block_levels(stream_key, dims, pieces, -0.22, 0.18) * array
    return jnp.clip(array, min=-reach, max=reach).astype(kind)


def setup_inputs(seed: int = 0, part: int = 0) -> dict:
    seeds = jax.random.split(jax.random.key(seed), 13)
    part_splits = jax.random.split(jax.random.fold_in(seeds[12], part), 13)
    return {
        "patches": normal_values(part_splits[0], (SLICE_TOTAL, P_SIZE, MODEL_DIM), 1.0, 6.0, ((0, 8),)),
        "cls_rows": normal_values(part_splits[1], (SLICE_TOTAL, MODEL_DIM), 1.0, 6.0, ((0, 8),)),
        "w_query": normal_values(seeds[2], (MODEL_DIM, MODEL_DIM), MODEL_DIM ** -0.5, 0.21875, ((1, 2),)),
        "w_key": normal_values(seeds[3], (MODEL_DIM, MODEL_DIM), MODEL_DIM ** -0.5, 0.21875, ((1, 2),)),
        "w_value": normal_values(seeds[4], (MODEL_DIM, MODEL_DIM), MODEL_DIM ** -0.5, 0.21875, ((1, 2),)),
        "w_out": normal_values(seeds[5], (MODEL_DIM, MODEL_DIM), MODEL_DIM ** -0.5, 0.21875, ((0, 2),)),
        "a_query": normal_values(seeds[6], (MODEL_DIM, MODEL_DIM), MODEL_DIM ** -0.5, 0.21875, ((1, 2),)),
        "a_key": normal_values(seeds[7], (MODEL_DIM, MODEL_DIM), MODEL_DIM ** -0.5, 0.21875, ((1, 2),)),
        "a_value": normal_values(seeds[8], (MODEL_DIM, MODEL_DIM), MODEL_DIM ** -0.5, 0.21875, ((1, 2),)),
        "a_out": normal_values(seeds[9], (MODEL_DIM, MODEL_DIM), MODEL_DIM ** -0.5, 0.21875, ((0, 2),)),
        "upstream": normal_values(part_splits[10], (WINDOW_COUNT, WROWS, MODEL_DIM), 1.0, 6.0, ((0, 8),)),
        "slice_to_scan": jnp.searchsorted(jnp.cumsum(uneven(part_splits[11], SCANS, SLICE_TOTAL, SCAN_MOST, 2)), jnp.arange(SLICE_TOTAL), side="right").astype(jnp.int32),
    }


def normalize(values):
    row_mean = lax.optimization_barrier(jnp.mean(values, axis=-1, keepdims=True))
    centred = values - row_mean
    variance = lax.optimization_barrier(jnp.mean(centred * centred, axis=-1, keepdims=True))
    inv_std = lax.rsqrt(variance + 1e-05)
    return (centred * inv_std, inv_std)

def score_grad(weights, d_probs, att_scale):
    inner = lax.optimization_barrier(jnp.sum(weights * d_probs, axis=-1, keepdims=True))
    return (weights * (d_probs - inner) * att_scale).astype(jnp.bfloat16)

def reference(patches, cls_rows, w_query, w_key, w_value, w_out, a_query, a_key, a_value, a_out, upstream, slice_to_scan):
    att_scale = float(HD) ** (-0.5)
    highest = lax.Precision.HIGHEST
    normed = normalize(patches.astype(jnp.float32))[0].astype(jnp.bfloat16)
    flat_rows = normed.reshape(SLICE_TOTAL * P_SIZE, MODEL_DIM)
    cls_norm = normalize(cls_rows.astype(jnp.float32))[0].astype(jnp.bfloat16)
    queries = jnp.dot(cls_norm, w_query, preferred_element_type=jnp.float32).astype(jnp.bfloat16).reshape(SLICE_TOTAL, H, HD)
    enc_keys = jnp.dot(flat_rows, w_key, preferred_element_type=jnp.float32).astype(jnp.bfloat16).reshape(SLICE_TOTAL, P_SIZE, H, HD)
    enc_values = jnp.dot(flat_rows, w_value, preferred_element_type=jnp.float32).astype(jnp.bfloat16).reshape(SLICE_TOTAL, P_SIZE, H, HD)
    scores = jnp.einsum('zhe,zphe->zhp', queries.astype(jnp.float32), enc_keys.astype(jnp.float32)) * att_scale
    probs = jax.nn.softmax(scores, axis=-1)
    probs_half = probs.astype(jnp.bfloat16)
    pooled = jnp.einsum('zhp,zphe->zhe', probs_half.astype(jnp.float32), enc_values.astype(jnp.float32))
    pooled = pooled.astype(jnp.bfloat16).reshape(SLICE_TOTAL, MODEL_DIM)
    slice_embeddings = (cls_rows.astype(jnp.float32) + jnp.dot(pooled, w_out, preferred_element_type=jnp.float32)).astype(jnp.bfloat16)
    extended_slices = jnp.concatenate([slice_embeddings, jnp.zeros((SLICES_PER_DEVICE, MODEL_DIM), jnp.bfloat16)], axis=0)
    window_blocks = jnp.concatenate([extended_slices[:SLICE_TOTAL].reshape(WINDOW_COUNT, SLICES_PER_DEVICE, MODEL_DIM), extended_slices[SLICES_PER_DEVICE:].reshape(WINDOW_COUNT, SLICES_PER_DEVICE, MODEL_DIM)], axis=1)
    extended_index = jnp.concatenate([slice_to_scan, jnp.full((SLICES_PER_DEVICE,), -1, jnp.int32)])
    window_index = jnp.concatenate([extended_index[:SLICE_TOTAL].reshape(WINDOW_COUNT, SLICES_PER_DEVICE), extended_index[SLICES_PER_DEVICE:].reshape(WINDOW_COUNT, SLICES_PER_DEVICE)], axis=1)
    allowed = (window_index[:, :, None] == window_index[:, None, :]) & (window_index[:, None, :] >= 0) | jnp.eye(WROWS, dtype=bool)[None]
    win_norm, win_rstd = normalize(window_blocks.astype(jnp.float32))
    win_half = win_norm.astype(jnp.bfloat16).reshape(WINDOW_COUNT * WROWS, MODEL_DIM)

    def project(weight):
        return jnp.dot(win_half, weight, preferred_element_type=jnp.float32).astype(jnp.bfloat16).reshape(WINDOW_COUNT, WROWS, H, HD)
    inner_q = project(a_query)
    inner_k = project(a_key)
    inner_v = project(a_value)
    inner_scores = jnp.einsum('wihe,wjhe->whij', inner_q.astype(jnp.float32), inner_k.astype(jnp.float32)) * att_scale
    inner_scores = jnp.where(allowed[:, None], inner_scores, -1e+30)
    inner_probs = jax.nn.softmax(inner_scores, axis=-1)
    inner_half = inner_probs.astype(jnp.bfloat16)
    up_rows = upstream.reshape(WINDOW_COUNT * WROWS, MODEL_DIM)
    d_pooled = jnp.dot(up_rows, a_out.T, preferred_element_type=jnp.float32).astype(jnp.bfloat16).reshape(WINDOW_COUNT, WROWS, H, HD)
    d_probs = jnp.einsum('wihe,wjhe->whij', d_pooled.astype(jnp.float32), inner_v.astype(jnp.float32))
    d_scores = score_grad(inner_probs, d_probs, att_scale).astype(jnp.float32)
    d_query = jnp.einsum('whij,wjhe->wihe', d_scores, inner_k.astype(jnp.float32)).astype(jnp.bfloat16).reshape(-1, MODEL_DIM)
    d_key = jnp.einsum('whij,wihe->wjhe', d_scores, inner_q.astype(jnp.float32)).astype(jnp.bfloat16).reshape(-1, MODEL_DIM)
    d_value = jnp.einsum('whij,wihe->wjhe', inner_half.astype(jnp.float32), d_pooled.astype(jnp.float32)).astype(jnp.bfloat16).reshape(-1, MODEL_DIM)
    d_normed = (jnp.dot(d_query, a_query.T, preferred_element_type=jnp.float32) + jnp.dot(d_key, a_key.T, preferred_element_type=jnp.float32) + jnp.dot(d_value, a_value.T, preferred_element_type=jnp.float32)).reshape(WINDOW_COUNT, WROWS, MODEL_DIM)
    centred_grad = d_normed - lax.optimization_barrier(jnp.mean(d_normed, axis=-1, keepdims=True)) - win_norm * lax.optimization_barrier(jnp.mean(d_normed * win_norm, axis=-1, keepdims=True))
    window_gradient = upstream.astype(jnp.float32) + win_rstd * centred_grad
    carried_state = jnp.concatenate([jnp.zeros((SLICES_PER_DEVICE, MODEL_DIM), jnp.float32), window_gradient[:-1, SLICES_PER_DEVICE:].reshape(SLICE_TOTAL - SLICES_PER_DEVICE, MODEL_DIM)], axis=0)
    embed_gradient = (window_gradient[:, :SLICES_PER_DEVICE].reshape(SLICE_TOTAL, MODEL_DIM) + carried_state).astype(jnp.bfloat16)
    d_att = jnp.dot(embed_gradient, w_out.T, preferred_element_type=jnp.float32).astype(jnp.bfloat16).reshape(SLICE_TOTAL, H, HD)
    d_enc_probs = jnp.einsum('zhe,zphe->zhp', d_att.astype(jnp.float32), enc_values.astype(jnp.float32))
    d_enc_scores = score_grad(probs, d_enc_probs, att_scale).astype(jnp.float32)
    d_enc_query = jnp.einsum('zhp,zphe->zhe', d_enc_scores, enc_keys.astype(jnp.float32)).astype(jnp.bfloat16).reshape(SLICE_TOTAL, MODEL_DIM)
    normed_wide = normed.astype(jnp.float32)
    key_factor = jnp.einsum('zpd,zhp->zdh', normed_wide, d_enc_scores, precision=highest)
    value_factor = jnp.einsum('zpd,zhp->zdh', normed_wide, probs_half.astype(jnp.float32), precision=highest)
    grad_key = jnp.einsum('zdh,zhe->dhe', key_factor, queries.astype(jnp.float32), precision=highest).reshape(MODEL_DIM, MODEL_DIM)
    grad_value = jnp.einsum('zdh,zhe->dhe', value_factor, d_att.astype(jnp.float32), precision=highest).reshape(MODEL_DIM, MODEL_DIM)
    contract = (((0,), (0,)), ((), ()))
    grad_query = lax.dot_general(cls_norm, d_enc_query, contract, preferred_element_type=jnp.float32)
    grad_out_t = lax.dot_general(embed_gradient, pooled, contract, preferred_element_type=jnp.float32)
    return (grad_query, grad_key, grad_value, grad_out_t)
```

```python
import functools

import jax
import jax.numpy as jnp
from jax import lax
from jax.experimental import pallas as pl
from jax.experimental.pallas import tpu as pltpu
from jax.sharding import PartitionSpec as P

HD = 64
SLOT = 8
LANES = 128
F32 = jnp.float32
BF16 = jnp.bfloat16
BIG_VMEM = 56 * 1024 * 1024


def dot(a, b, dims=((1,), (0,))):
    return lax.dot_general(a, b, (dims, ((), ())), preferred_element_type=F32)


BY_COLS = ((1,), (1,))
BY_ROWS = ((0,), (0,))


def normalize(values):
    row_mean = jnp.mean(values, axis=-1, keepdims=True)
    centred = values - row_mean
    variance = jnp.mean(centred * centred, axis=-1, keepdims=True)
    inv_std = lax.rsqrt(variance + 1e-05)
    return centred * inv_std, inv_std


def head_mask(slices, cols):
    shape = (slices * SLOT, cols)
    row = lax.broadcasted_iota(jnp.int32, shape, 0)
    col = lax.broadcasted_iota(jnp.int32, shape, 1)
    return row % SLOT == col // HD


def slot_rows(rows):
    slices, cols = rows.shape
    wide = jnp.broadcast_to(rows.astype(F32)[:, None, :], (slices, SLOT, cols))
    return wide.reshape(slices * SLOT, cols)


def expand(rows):
    wide = slot_rows(rows)
    return jnp.where(head_mask(rows.shape[0], rows.shape[1]), wide, 0.0).astype(BF16)


def collapse(full):
    rows, cols = full.shape
    kept = jnp.where(head_mask(rows // SLOT, cols), full, 0.0)
    return jnp.sum(kept.reshape(rows // SLOT, SLOT, cols), axis=1)


def forward_kernel(
    per_step,
    patches,
    cls_rows,
    w_query,
    w_key,
    w_value,
    w_out,
    normed,
    probs,
    value_factor,
    queries,
    cls_norm,
    pooled,
    head_terms,
    query_keys,
    factor,
):
    step = pl.program_id(0)
    scale = float(HD) ** (-0.5)

    @pl.when(step == 0)
    def _():
        rows = normalize(cls_rows[...].astype(F32))[0].astype(BF16)
        cls_norm[...] = rows
        q = dot(rows, w_query[...]).astype(BF16)
        queries[...] = q
        query_keys[...] = dot(expand(q), w_key[...], BY_COLS) * scale

    for s in range(per_step):
        here = pl.ds(pl.multiple_of((step * per_step + s) * SLOT, SLOT), SLOT)
        rows = normalize(patches[s].astype(F32))[0].astype(BF16)
        normed[s] = rows
        scores = dot(query_keys[here, :].astype(BF16), rows, BY_COLS)
        top = jnp.max(scores, axis=-1, keepdims=True)
        powers = jnp.exp(scores - top)
        p = powers / jnp.sum(powers, axis=-1, keepdims=True)
        probs[s] = p
        factor[here, :] = dot(p.astype(BF16), rows)

    @pl.when(step == pl.num_programs(0) - 1)
    def _():
        half = factor[...].astype(BF16)
        value_factor[...] = half
        pool = collapse(dot(half, w_value[...])).astype(BF16)
        pooled[...] = pool
        head_terms[...] = dot(pool, w_out[...])


def encoder_forward(patches, cls_rows, w_query, w_key, w_value, w_out, per_step):
    slices, tokens, width = patches.shape
    cols = w_query.shape[1]
    whole = lambda shape: pl.BlockSpec(shape, lambda i: (0,) * len(shape))
    block = pl.BlockSpec((per_step, tokens, width), lambda i: (i, 0, 0))
    return pl.pallas_call(
        functools.partial(forward_kernel, per_step),
        grid=(slices // per_step,),
        in_specs=[
            block,
            whole(cls_rows.shape),
            whole(w_query.shape),
            whole(w_key.shape),
            whole(w_value.shape),
            whole(w_out.shape),
        ],
        out_specs=[
            block,
            pl.BlockSpec((per_step, SLOT, tokens), lambda i: (i, 0, 0)),
            whole((slices * SLOT, width)),
            whole((slices, cols)),
            whole((slices, width)),
            whole((slices, cols)),
            whole((slices, width)),
        ],
        out_shape=[
            jax.ShapeDtypeStruct(patches.shape, BF16),
            jax.ShapeDtypeStruct((slices, SLOT, tokens), F32),
            jax.ShapeDtypeStruct((slices * SLOT, width), BF16),
            jax.ShapeDtypeStruct((slices, cols), BF16),
            jax.ShapeDtypeStruct((slices, width), BF16),
            jax.ShapeDtypeStruct((slices, cols), BF16),
            jax.ShapeDtypeStruct((slices, width), F32),
        ],
        scratch_shapes=[
            pltpu.VMEM((slices * SLOT, width), F32),
            pltpu.VMEM((slices * SLOT, width), F32),
        ],
        compiler_params=pltpu.CompilerParams(vmem_limit_bytes=BIG_VMEM),
        name="encoder_forward",
    )(patches, cls_rows, w_query, w_key, w_value, w_out)


def window_kernel(heads, ids, own, following, a_query, a_key, a_value, a_out, up, d_half):
    scale = float(HD) ** (-0.5)
    slices = own.shape[0]
    rows = 2 * slices
    cols = a_query.shape[1]
    total = ids.shape[0]
    start = (lax.axis_index("gz") * lax.axis_size("dev") + lax.axis_index("dev")) * slices
    window = jnp.concatenate([own[...].astype(F32), following[...].astype(F32)], axis=0)
    half = normalize(window)[0].astype(BF16)
    q = dot(half, a_query[...]).astype(BF16)
    k = dot(half, a_key[...]).astype(BF16)
    v = dot(half, a_value[...]).astype(BF16)
    d_pooled = dot(up[...], a_out[...], BY_COLS).astype(BF16)

    wide = (heads * rows, cols)
    mine = (
        lax.broadcasted_iota(jnp.int32, wide, 0) // rows
        == lax.broadcasted_iota(jnp.int32, wide, 1) // HD
    )

    def by_head(x):
        tall = jnp.broadcast_to(x.astype(F32)[None], (heads, rows, cols)).reshape(wide)
        return jnp.where(mine, tall, 0.0).astype(BF16)

    q_wide = by_head(q)
    d_wide = by_head(d_pooled)

    square = (heads * rows, rows)
    i_of = lax.broadcasted_iota(jnp.int32, square, 0) % rows
    j_of = lax.broadcasted_iota(jnp.int32, square, 1)
    id_i = jnp.full(square, -1, jnp.int32)
    id_j = jnp.full(square, -1, jnp.int32)
    for n in range(rows):
        place = start + n
        scan = jnp.where(place < total, ids[jnp.minimum(place, total - 1)], -1)
        id_i = jnp.where(i_of == n, scan, id_i)
        id_j = jnp.where(j_of == n, scan, id_j)
    allowed = ((id_i == id_j) & (id_j >= 0)) | (i_of == j_of)

    scores = jnp.where(allowed, dot(q_wide, k, BY_COLS) * scale, -1e30)
    powers = jnp.exp(scores - jnp.max(scores, axis=-1, keepdims=True))
    probs = powers / jnp.sum(powers, axis=-1, keepdims=True)
    d_probs = dot(d_wide, v, BY_COLS)
    inner = jnp.sum(probs * d_probs, axis=-1, keepdims=True)
    d_scores = probs * (d_probs - inner) * scale
    d_scores_half = d_scores.astype(BF16)
    d_query = jnp.where(mine, dot(d_scores_half, k), 0.0)
    d_query = jnp.sum(d_query.reshape(heads, rows, cols), axis=0).astype(BF16)
    d_key = dot(d_scores_half, q_wide, BY_ROWS).astype(BF16)
    d_value = dot(probs.astype(BF16), d_wide, BY_ROWS).astype(BF16)
    terms = (
        dot(d_query, a_query[...], BY_COLS)
        + dot(d_key, a_key[...], BY_COLS)
        + dot(d_value, a_value[...], BY_COLS)
    )
    d_half[...] = terms.astype(BF16)


def window_gradients(own, following, a_query, a_key, a_value, a_out, up, ids):
    slices, width = own.shape
    heads = a_query.shape[1] // HD

    def body(ids_ref, own_ref, next_ref, q_ref, k_ref, v_ref, o_ref, up_ref, out_ref):
        window_kernel(heads, ids_ref, own_ref, next_ref, q_ref, k_ref, v_ref, o_ref, up_ref, out_ref)

    vmem = pl.BlockSpec(memory_space=pltpu.VMEM)
    return pl.pallas_call(
        body,
        in_specs=[pl.BlockSpec(memory_space=pltpu.SMEM)] + [vmem] * 7,
        out_specs=vmem,
        out_shape=jax.ShapeDtypeStruct((2 * slices, width), BF16),
        compiler_params=pltpu.CompilerParams(vmem_limit_bytes=BIG_VMEM),
        name="window_gradients",
    )(ids, own, following, a_query, a_key, a_value, a_out, up)


def lane_blocks(rows):
    cols = rows.shape[1]
    spare = -cols % LANES
    if spare:
        rows = jnp.concatenate([rows, jnp.zeros((rows.shape[0], spare), rows.dtype)], axis=1)
    return jnp.concatenate(
        [rows[:, b : b + LANES] for b in range(0, cols + spare, LANES)], axis=0
    )


def backward_kernel(
    per_step,
    normed,
    probs,
    d_own,
    d_other,
    d_carried,
    embedded,
    up,
    up_carried,
    w_key,
    w_value,
    w_out,
    value_factor,
    queries,
    cls_norm,
    pooled,
    *rest,
):
    outs, (d_keys, factor, saved_att, saved_embed, turned) = rest[:-5], rest[-5:]
    step = pl.program_id(0)
    scale = float(HD) ** (-0.5)
    slices = embedded.shape[0]

    @pl.when(step == 0)
    def _():
        win_norm, inv_std = normalize(embedded[...].astype(F32))
        d_normed = d_own[:slices].astype(F32) + d_other[:slices].astype(F32) + d_carried[...]
        centred = (
            d_normed
            - jnp.mean(d_normed, axis=-1, keepdims=True)
            - win_norm * jnp.mean(d_normed * win_norm, axis=-1, keepdims=True)
        )
        total = up[:slices].astype(F32) + up_carried[...].astype(F32) + inv_std * centred
        d_embed = total.astype(BF16)
        saved_embed[...] = d_embed
        d_att = dot(d_embed, w_out[...], BY_COLS).astype(BF16)
        saved_att[...] = d_att
        d_keys[...] = dot(expand(d_att), w_value[...], BY_COLS)

    for s in range(per_step):
        here = pl.ds(pl.multiple_of((step * per_step + s) * SLOT, SLOT), SLOT)
        rows = normed[s]
        p = probs[s]
        d_probs = dot(d_keys[here, :].astype(BF16), rows, BY_COLS)
        inner = jnp.sum(p * d_probs, axis=-1, keepdims=True)
        d_scores = (p * (d_probs - inner) * scale).astype(BF16)
        factor[here, :] = dot(d_scores, rows)

    @pl.when(step == pl.num_programs(0) - 1)
    def _():
        key_factor = factor[...]
        d_query = collapse(dot(key_factor.astype(BF16), w_key[...])).astype(BF16)
        slot = lax.broadcasted_iota(jnp.int32, key_factor.shape, 0) % SLOT
        left = jnp.where(slot == SLOT - 2, slot_rows(cls_norm[...]), key_factor)
        left = jnp.where(slot == SLOT - 1, slot_rows(saved_embed[...]), left)
        both = jnp.concatenate([left, value_factor[...].astype(F32)], axis=0)
        turned[...] = both.T
        right = jnp.concatenate(
            [queries[...], saved_att[...], d_query, pooled[...]], axis=0
        ).astype(F32)
        right = lane_blocks(right).astype(BF16)
        chips = len(outs)
        part = turned.shape[0] // chips
        here = lax.axis_index("gz")
        for shift in range(chips):
            first = pl.multiple_of(lax.rem(here + shift, chips) * part, SLOT)
            outs[shift][:part] = turned[pl.ds(first, part), :].astype(BF16)
            outs[shift][part:] = right


def encoder_backward(
    normed, probs, d_own, d_other, d_carried, embedded, up, up_carried, w_key, w_value, w_out,
    value_factor, queries, cls_norm, pooled, chips, per_step,
):
    slices, tokens, width = normed.shape
    cols = w_key.shape[1]
    blocks = pl.cdiv(cols, LANES)
    whole = lambda a: pl.BlockSpec(a.shape, lambda i: (0,) * a.ndim)
    message = (width // chips + 4 * slices * blocks, LANES)
    rest = (d_own, d_other, d_carried, embedded, up, up_carried, w_key, w_value, w_out,
            value_factor, queries, cls_norm, pooled)
    return pl.pallas_call(
        functools.partial(backward_kernel, per_step),
        grid=(slices // per_step,),
        in_specs=[
            pl.BlockSpec((per_step, tokens, width), lambda i: (i, 0, 0)),
            pl.BlockSpec((per_step, SLOT, tokens), lambda i: (i, 0, 0)),
        ]
        + [whole(a) for a in rest],
        out_specs=[pl.BlockSpec(message, lambda i: (0, 0))] * chips,
        out_shape=[jax.ShapeDtypeStruct(message, BF16)] * chips,
        scratch_shapes=[
            pltpu.VMEM((slices * SLOT, width), F32),
            pltpu.VMEM((slices * SLOT, width), F32),
            pltpu.VMEM((slices, cols), BF16),
            pltpu.VMEM((slices, width), BF16),
            pltpu.VMEM((width, 2 * slices * SLOT), F32),
        ],
        compiler_params=pltpu.CompilerParams(vmem_limit_bytes=BIG_VMEM),
        name="encoder_backward",
    )(normed, probs, *rest)


def assemble_kernel(slices, cols, part, chips, *refs):
    messages, (kept, sent) = refs[:chips], refs[chips:]
    blocks = pl.cdiv(cols, LANES)
    count = 4 * slices
    left = jnp.concatenate([m[:part] for m in messages], axis=1)
    mask = head_mask(slices, cols)
    slot = lax.broadcasted_iota(jnp.int32, mask.shape, 0) % SLOT
    zeros = jnp.zeros(mask.shape, F32)
    rights = [[], [], [], []]
    for m in messages:
        tail = m[part:].astype(F32)
        rows = jnp.concatenate(
            [tail[b * count : (b + 1) * count] for b in range(blocks)], axis=1
        )[:, :cols]
        q, d_att, d_query, pooled = [
            slot_rows(rows[n * slices : (n + 1) * slices]) for n in range(4)
        ]
        rights[0] += [jnp.where(slot == SLOT - 2, d_query, 0.0), zeros]
        rights[1] += [jnp.where(mask, q, 0.0), zeros]
        rights[2] += [zeros, jnp.where(mask, d_att, 0.0)]
        rights[3] += [jnp.where(slot == SLOT - 1, pooled, 0.0), zeros]
    first = lax.axis_index("dev") == 0
    own = part // 2
    for n in range(4):
        right = jnp.concatenate(rights[n], axis=0).astype(BF16)
        total = dot(left, right)
        top, bottom = total[:own], total[own:]
        kept[n] = jnp.where(first, top, bottom)
        sent[n] = jnp.where(first, bottom, top)


def assemble(messages, slices, cols, part):
    vmem = pl.BlockSpec(memory_space=pltpu.VMEM)
    shape = jax.ShapeDtypeStruct((4, part // 2, cols), F32)
    return pl.pallas_call(
        functools.partial(assemble_kernel, slices, cols, part, len(messages)),
        in_specs=[vmem] * len(messages),
        out_specs=[vmem, vmem],
        out_shape=[shape, shape],
        compiler_params=pltpu.CompilerParams(vmem_limit_bytes=BIG_VMEM),
        name="assemble",
    )(*messages)


def ring_shift(x, axis, distance):
    size = lax.axis_size(axis)
    return lax.ppermute(x, axis, [(i, (i + distance) % size) for i in range(size)])


def passed_along(block, axis, distance):
    devices = range(lax.axis_size(axis))
    route = [(i - distance, i) for i in devices if i - distance in devices]
    return lax.ppermute(block, axis, route)


def others(x):
    return [ring_shift(x, "ma", d) for d in range(1, lax.axis_size("ma"))]


def local(
    patches,
    cls_rows,
    w_query,
    w_key,
    w_value,
    w_out,
    a_query,
    a_key,
    a_value,
    a_out,
    upstream,
    slice_to_scan,
):
    line = ("gz", "dev")
    slices, _, width = patches.shape
    cols = w_query.shape[1]
    chips = lax.axis_size("gz")
    up = upstream[0]
    up_carried = passed_along(up[slices:], line, 1)
    normed, probs, value_factor, queries, cls_norm, pooled, head_terms = encoder_forward(
        patches, cls_rows, w_query, w_key, w_value, w_out, 2
    )
    total = head_terms
    for term in others(head_terms):
        total = total + term
    embedded = (cls_rows.astype(F32) + total).astype(BF16)
    following = passed_along(embedded, line, -1)
    d_own = window_gradients(
        embedded, following, a_query, a_key, a_value, a_out, up, slice_to_scan
    )
    parts = [part.astype(F32) for part in others(d_own)]
    d_other = parts[0]
    for part in parts[1:]:
        d_other = d_other + part
    d_carried = passed_along(d_own[slices:].astype(F32) + d_other[slices:], line, 1)
    messages = encoder_backward(
        normed, probs, d_own, d_other, d_carried, embedded, up, up_carried, w_key, w_value, w_out,
        value_factor, queries, cls_norm, pooled, chips, 2,
    )
    arrived = [messages[0]] + [
        ring_shift(messages[shift], "gz", shift) for shift in range(1, chips)
    ]
    kept, sent = assemble(arrived, slices, cols, width // chips)
    grads = kept + ring_shift(sent, "dev", 1)
    return tuple(grads[n] for n in range(4))


def solution(mesh):
    return jax.shard_map(
        local,
        mesh=mesh,
        in_specs=(
            P(("grp", "gz", "dev"), None, None),
            P(("grp", "gz", "dev"), None),
            P(None, "ma"),
            P(None, "ma"),
            P(None, "ma"),
            P("ma", None),
            P(None, "ma"),
            P(None, "ma"),
            P(None, "ma"),
            P("ma", None),
            P(("grp", "gz", "dev"), None, None),
            P("grp"),
        ),
        out_specs=(
            P(("grp", "gz", "dev"), "ma"),
            P(("grp", "gz", "dev"), "ma"),
            P(("grp", "gz", "dev"), "ma"),
            P(("grp", "gz", "dev"), "ma"),
        ),
        check_vma=False,
    )
```

```python
import functools

import jax
import jax.numpy as jnp
from jax import lax
from jax.experimental import pallas as pl
from jax.experimental.pallas import tpu as pltpu
from jax.sharding import PartitionSpec as P

HD = 64
SLOT = 8
LANES = 128
F32 = jnp.float32
BF16 = jnp.bfloat16
VMEM_LIMIT = 16 * 1024 * 1024


def dot(a, b, dims=((1,), (0,))):
    return lax.dot_general(a, b, (dims, ((), ())), preferred_element_type=F32)


BY_COLS = ((1,), (1,))
BY_ROWS = ((0,), (0,))


def normalize(values):
    row_mean = jnp.mean(values, axis=-1, keepdims=True)
    centred = values - row_mean
    variance = jnp.mean(centred * centred, axis=-1, keepdims=True)
    inv_std = lax.rsqrt(variance + 1e-05)
    return centred * inv_std, inv_std


def head_mask(slices, cols):
    shape = (slices * SLOT, cols)
    row = lax.broadcasted_iota(jnp.int32, shape, 0)
    col = lax.broadcasted_iota(jnp.int32, shape, 1)
    return row % SLOT == col // HD


def slot_rows(rows):
    slices, cols = rows.shape
    wide = jnp.broadcast_to(rows.astype(F32)[:, None, :], (slices, SLOT, cols))
    return wide.reshape(slices * SLOT, cols)


def expand(rows):
    wide = slot_rows(rows)
    return jnp.where(head_mask(rows.shape[0], rows.shape[1]), wide, 0.0).astype(BF16)


def collapse(full):
    rows, cols = full.shape
    kept = jnp.where(head_mask(rows // SLOT, cols), full, 0.0)
    return jnp.sum(kept.reshape(rows // SLOT, SLOT, cols), axis=1)


def in_vmem(shape, dtype):
    return pltpu.VMEM(shape, dtype)


def lane_blocks(rows):
    cols = rows.shape[1]
    spare = -cols % LANES
    if spare:
        rows = jnp.concatenate([rows, jnp.zeros((rows.shape[0], spare), rows.dtype)], axis=1)
    return jnp.concatenate(
        [rows[:, b : b + LANES] for b in range(0, cols + spare, LANES)], axis=0
    )


def from_lane_blocks(rows, cols):
    count = rows.shape[0] // pl.cdiv(cols, LANES)
    blocks = [rows[b : b + count] for b in range(0, rows.shape[0], count)]
    return jnp.concatenate(blocks, axis=1)[:, :cols]


def write_messages(outs, factor, rows, turned):
    turned[:, : factor.shape[0]] = factor.T
    right = lane_blocks(rows.astype(F32)).astype(BF16)
    chips = len(outs)
    half = turned.shape[0] // chips // 2
    here = lax.axis_index("gz")
    for shift in range(chips):
        first = lax.rem(here + shift, chips) * (2 * half)
        block = turned[pl.ds(pl.multiple_of(first, SLOT), 2 * half), : factor.shape[0]]
        both = jnp.concatenate([block[:half], block[half:]], axis=1)
        outs[shift][:half] = both.astype(BF16)
        outs[shift][half:] = right


def forward_kernel(
    chunk,
    chips,
    patches_hbm,
    w_query_hbm,
    w_key_hbm,
    w_value_hbm,
    w_out_hbm,
    cls_rows,
    patches,
    w_key,
    w_value,
    w_out,
    probs,
    stats,
    cls_norm,
    head_terms,
    *rest,
):
    outs, (w_query, turned, query_keys, factor, sems, patch_sems) = rest[:chips], rest[chips:]
    slices, tokens, width = patches.shape
    scale = float(HD) ** (-0.5)

    def fetch(source, target, n):
        copy = pltpu.make_async_copy(source, target, sems.at[n])
        copy.start()
        return copy

    get_query = fetch(w_query_hbm, w_query, 0)
    get_key = fetch(w_key_hbm, w_key, 1)
    get_patches = []
    for c in range(slices // chunk):
        part = pl.ds(c * chunk, chunk)
        copy = pltpu.make_async_copy(patches_hbm.at[part], patches.at[part], patch_sems.at[c])
        copy.start()
        get_patches.append(copy)
    get_value = fetch(w_value_hbm, w_value, 2)
    get_out = fetch(w_out_hbm, w_out, 3)

    rows = normalize(cls_rows[...].astype(F32))[0].astype(BF16)
    cls_norm[...] = rows
    get_query.wait()
    q = dot(rows, w_query[...]).astype(BF16)
    get_key.wait()
    keys = (dot(expand(q), w_key[...], BY_COLS) * scale).astype(BF16).astype(F32)
    key_sums = jnp.sum(keys, axis=-1, keepdims=True)
    place = lax.broadcasted_iota(jnp.int32, (SLOT, width), 0)
    entry = lax.broadcasted_iota(jnp.int32, (SLOT, width), 1)
    picks = jnp.where((place == 0) | ((place == 1) & (entry == 0)), 1.0, 0.0)
    for z in range(slices):
        query_keys[z] = jnp.concatenate(
            [keys[z * SLOT : (z + 1) * SLOT], picks], axis=0
        ).astype(BF16)

    def measure(z):
        x = patches[z]
        raw = dot(query_keys[z], x, BY_COLS)
        wide = x.astype(F32)
        first = wide[:, 0:1]
        squares = None
        for b in range(0, width, LANES):
            off = wide[:, b : b + LANES] - first
            squares = off * off if squares is None else squares + off * off
        total = jnp.sum(squares.T, axis=0, keepdims=True)
        return raw, total

    def attend(z, raw, total):
        mean = raw[SLOT : SLOT + 1] * (1.0 / width)
        off = mean - raw[SLOT + 1 : SLOT + 2]
        inv_std = lax.rsqrt(jnp.maximum(total * (1.0 / width) - off * off, 0.0) + 1e-05)
        stats[z : z + 1] = mean
        stats[slices + z : slices + z + 1] = inv_std
        here = slice(z * SLOT, (z + 1) * SLOT)
        scores = inv_std * (raw[:SLOT] - mean * key_sums[here])
        powers = jnp.exp(scores - jnp.max(scores, axis=-1, keepdims=True))
        p = powers / jnp.sum(powers, axis=-1, keepdims=True)
        probs[z] = p
        weights = (p.astype(BF16).astype(F32) * inv_std).astype(BF16)
        shift = jnp.sum(weights.astype(F32) * mean, axis=-1, keepdims=True)
        factor[here] = dot(weights, patches[z]) - shift

    waiting = []
    for c in range(slices // chunk):
        get_patches[c].wait()
        ready = [(z,) + measure(z) for z in range(c * chunk, (c + 1) * chunk)]
        for item in waiting:
            attend(*item)
        waiting = ready
    for item in waiting:
        attend(*item)

    get_value.wait()
    value_factor = factor[...]
    pool = collapse(dot(value_factor.astype(BF16), w_value[...])).astype(BF16)
    get_out.wait()
    head_terms[...] = dot(pool, w_out[...])
    write_messages(outs, value_factor, jnp.concatenate([q.astype(F32), pool.astype(F32)], 0), turned)


def encoder_forward(patches, cls_rows, w_query, w_key, w_value, w_out, chips):
    slices, tokens, width = patches.shape
    cols = w_query.shape[1]
    chunk = 2
    hbm = pl.BlockSpec(memory_space=pl.ANY)
    vmem = pl.BlockSpec(memory_space=pltpu.VMEM)
    message = (width // chips // 2 + 2 * slices * pl.cdiv(cols, LANES), LANES)
    out_shape = [
        in_vmem(patches.shape, BF16),
        in_vmem(w_key.shape, BF16),
        in_vmem(w_value.shape, BF16),
        in_vmem(w_out.shape, BF16),
        in_vmem((slices, SLOT, tokens), F32),
        in_vmem((2 * slices, tokens), F32),
        in_vmem((slices, width), BF16),
        in_vmem((slices, width), F32),
    ] + [in_vmem(message, BF16)] * chips
    return pl.pallas_call(
        functools.partial(forward_kernel, chunk, chips),
        in_specs=[hbm] * 5 + [vmem],
        out_specs=[vmem] * len(out_shape),
        out_shape=out_shape,
        scratch_shapes=[
            pltpu.VMEM(w_query.shape, BF16),
            pltpu.VMEM((width, LANES), F32),
            pltpu.VMEM((slices, 2 * SLOT, width), BF16),
            pltpu.VMEM((slices * SLOT, width), F32),
            pltpu.SemaphoreType.DMA((4,)),
            pltpu.SemaphoreType.DMA((slices // chunk,)),
        ],
        compiler_params=pltpu.CompilerParams(vmem_limit_bytes=VMEM_LIMIT),
        name="encoder_forward",
    )(patches, w_query, w_key, w_value, w_out, cls_rows)


def head_rows(x, heads):
    rows, cols = x.shape
    wide = (heads * rows, cols)
    mine = (
        lax.broadcasted_iota(jnp.int32, wide, 0) // rows
        == lax.broadcasted_iota(jnp.int32, wide, 1) // HD
    )
    tall = jnp.broadcast_to(x.astype(F32)[None], (heads, rows, cols)).reshape(wide)
    return jnp.where(mine, tall, 0.0).astype(BF16), mine


def prepare_kernel(heads, slices, ids, up, a_out, d_wide, bias):
    rows = 2 * slices
    total = ids.shape[0]
    start = (lax.axis_index("gz") * lax.axis_size("dev") + lax.axis_index("dev")) * slices
    d_pooled = dot(up[...], a_out[...], BY_COLS).astype(BF16)
    d_wide[...] = head_rows(d_pooled, heads)[0]
    square = (heads * rows, rows)
    i_of = lax.broadcasted_iota(jnp.int32, square, 0) % rows
    j_of = lax.broadcasted_iota(jnp.int32, square, 1)
    id_i = jnp.full(square, -1, jnp.int32)
    id_j = jnp.full(square, -1, jnp.int32)
    for n in range(rows):
        place = start + n
        scan = jnp.where(place < total, ids[jnp.minimum(place, total - 1)], -1)
        id_i = jnp.where(i_of == n, scan, id_i)
        id_j = jnp.where(j_of == n, scan, id_j)
    allowed = ((id_i == id_j) & (id_j >= 0)) | (i_of == j_of)
    bias[...] = jnp.where(allowed, 1.0, 0.0)


def prepare_window(ids, up, a_out, slices):
    cols = a_out.shape[0]
    heads = cols // HD
    rows = 2 * slices
    vmem = pl.BlockSpec(memory_space=pltpu.VMEM)
    return pl.pallas_call(
        functools.partial(prepare_kernel, heads, slices),
        in_specs=[pl.BlockSpec(memory_space=pltpu.SMEM), vmem, vmem],
        out_specs=[vmem, vmem],
        out_shape=[in_vmem((heads * rows, cols), BF16), in_vmem((heads * rows, rows), F32)],
        compiler_params=pltpu.CompilerParams(vmem_limit_bytes=VMEM_LIMIT),
        name="prepare_window",
    )(ids, up, a_out)


def window_kernel(heads, own, following, a_query, a_key, a_value, d_wide, allowed, d_half):
    scale = float(HD) ** (-0.5)
    window = jnp.concatenate([own[...].astype(F32), following[...].astype(F32)], axis=0)
    rows = window.shape[0]
    cols = a_query.shape[1]
    half = normalize(window)[0].astype(BF16)
    q_wide, mine = head_rows(dot(half, a_query[...]).astype(BF16), heads)
    k = dot(half, a_key[...]).astype(BF16)
    v = dot(half, a_value[...]).astype(BF16)
    scores = jnp.where(allowed[...] > 0.5, dot(q_wide, k, BY_COLS) * scale, -1e30)
    d_probs = dot(d_wide[...], v, BY_COLS)
    powers = jnp.exp(scores - jnp.max(scores, axis=-1, keepdims=True))
    probs = powers / jnp.sum(powers, axis=-1, keepdims=True)
    inner = jnp.sum(probs * d_probs, axis=-1, keepdims=True)
    d_scores = (probs * (d_probs - inner) * scale).astype(BF16)
    d_value = dot(probs.astype(BF16), d_wide[...], BY_ROWS).astype(BF16)
    d_query = jnp.where(mine, dot(d_scores, k), 0.0)
    d_query = jnp.sum(d_query.reshape(heads, rows, cols), axis=0).astype(BF16)
    d_key = dot(d_scores, q_wide, BY_ROWS).astype(BF16)
    terms = (
        dot(d_value, a_value[...], BY_COLS)
        + dot(d_query, a_query[...], BY_COLS)
        + dot(d_key, a_key[...], BY_COLS)
    )
    d_half[...] = terms.astype(BF16)


def window_gradients(own, following, a_query, a_key, a_value, d_wide, allowed):
    slices, width = own.shape
    heads = a_query.shape[1] // HD
    vmem = pl.BlockSpec(memory_space=pltpu.VMEM)
    return pl.pallas_call(
        functools.partial(window_kernel, heads),
        in_specs=[vmem] * 7,
        out_specs=vmem,
        out_shape=in_vmem((2 * slices, width), BF16),
        compiler_params=pltpu.CompilerParams(vmem_limit_bytes=VMEM_LIMIT),
        name="window_gradients",
    )(own, following, a_query, a_key, a_value, d_wide, allowed)


def backward_kernel(
    chips,
    patches,
    probs,
    stats,
    d_own,
    d_others,
    carried,
    embedded,
    up,
    w_key,
    w_value,
    w_out,
    cls_norm,
    *rest,
):
    outs, (turned, d_keys, factor) = rest[:chips], rest[chips:]
    scale = float(HD) ** (-0.5)
    slices = embedded.shape[0]

    win_norm, inv_std = normalize(embedded[...].astype(F32))
    d_normed = d_own[:slices].astype(F32) + carried[:slices]
    for n in range(d_others.shape[0]):
        d_normed = d_normed + d_others[n, :slices].astype(F32)
    centred = (
        d_normed
        - jnp.mean(d_normed, axis=-1, keepdims=True)
        - win_norm * jnp.mean(d_normed * win_norm, axis=-1, keepdims=True)
    )
    d_embed = up[:slices].astype(F32) + carried[slices:] + inv_std * centred
    d_embed = d_embed.astype(BF16)
    d_att = dot(d_embed, w_out[...], BY_COLS).astype(BF16)
    keys = dot(expand(d_att), w_value[...], BY_COLS).astype(BF16).astype(F32)
    key_sums = jnp.sum(keys, axis=-1, keepdims=True)
    d_keys[...] = keys

    for z in range(slices):
        here = slice(z * SLOT, (z + 1) * SLOT)
        x = patches[z]
        p = probs[z]
        mean = stats[z : z + 1]
        inv = stats[slices + z : slices + z + 1]
        raw = dot(d_keys[here].astype(BF16), x, BY_COLS)
        d_probs = inv * (raw - mean * key_sums[here])
        inner = jnp.sum(p * d_probs, axis=-1, keepdims=True)
        d_scores = (p * (d_probs - inner) * scale).astype(BF16)
        weights = (d_scores.astype(F32) * inv).astype(BF16)
        shift = jnp.sum(weights.astype(F32) * mean, axis=-1, keepdims=True)
        factor[here] = dot(weights, x) - shift

    key_factor = factor[...]
    d_query = collapse(dot(key_factor.astype(BF16), w_key[...])).astype(BF16)
    slot = lax.broadcasted_iota(jnp.int32, key_factor.shape, 0) % SLOT
    left = jnp.where(slot == SLOT - 2, slot_rows(cls_norm[...]), key_factor)
    left = jnp.where(slot == SLOT - 1, slot_rows(d_embed), left)
    right = jnp.concatenate([d_att.astype(F32), d_query.astype(F32)], axis=0)
    write_messages(outs, left, right, turned)


def encoder_backward(
    patches, probs, stats, d_own, d_others, carried, embedded, up, w_key, w_value, w_out, cls_norm,
    chips,
):
    slices, tokens, width = patches.shape
    cols = w_key.shape[1]
    vmem = pl.BlockSpec(memory_space=pltpu.VMEM)
    message = (width // chips // 2 + 2 * slices * pl.cdiv(cols, LANES), LANES)
    return pl.pallas_call(
        functools.partial(backward_kernel, chips),
        in_specs=[vmem] * 12,
        out_specs=[vmem] * chips,
        out_shape=[in_vmem(message, BF16)] * chips,
        scratch_shapes=[
            pltpu.VMEM((width, LANES), F32),
            pltpu.VMEM((slices * SLOT, width), F32),
            pltpu.VMEM((slices * SLOT, width), F32),
        ],
        compiler_params=pltpu.CompilerParams(vmem_limit_bytes=VMEM_LIMIT),
        name="encoder_backward",
    )(patches, probs, stats, d_own, d_others, carried, embedded, up, w_key, w_value, w_out, cls_norm)


def assemble_kernel(slices, cols, half, chips, *refs):
    early, late, (kept, sent) = refs[:chips], refs[chips : 2 * chips], refs[2 * chips :]
    mask = head_mask(slices, cols)
    slot = lax.broadcasted_iota(jnp.int32, mask.shape, 0) % SLOT
    depth = slices * SLOT

    def stacked(messages):
        top = [m[:half, :depth].astype(F32) for m in messages]
        bottom = [m[:half, depth:].astype(F32) for m in messages]
        return jnp.concatenate(
            [jnp.concatenate(top, axis=1), jnp.concatenate(bottom, axis=1)], axis=0
        ).astype(BF16)

    first, second = [], []
    for messages, into in ((early, first), (late, second)):
        for m in messages:
            rows = from_lane_blocks(m[half:].astype(F32), cols)
            into.append([slot_rows(rows[:slices]), slot_rows(rows[slices:])])
    left_value, left_key = stacked(early), stacked(late)

    def right(blocks):
        return jnp.concatenate(blocks, axis=0).astype(BF16)

    grads = [
        dot(left_key, right([jnp.where(slot == SLOT - 2, b[1], 0.0) for b in second])),
        dot(left_key, right([jnp.where(mask, b[0], 0.0) for b in first])),
        dot(left_value, right([jnp.where(mask, b[0], 0.0) for b in second])),
        dot(left_key, right([jnp.where(slot == SLOT - 1, b[1], 0.0) for b in first])),
    ]
    lower = lax.axis_index("dev") == 0
    for n, total in enumerate(grads):
        top, bottom = total[:half], total[half:]
        kept[n] = jnp.where(lower, top, bottom)
        sent[n] = jnp.where(lower, bottom, top).astype(BF16)


def assemble(early, late, slices, cols, half):
    vmem = pl.BlockSpec(memory_space=pltpu.VMEM)
    shape = (4, half, cols)
    return pl.pallas_call(
        functools.partial(assemble_kernel, slices, cols, half, len(early)),
        in_specs=[vmem] * (2 * len(early)),
        out_specs=[vmem, vmem],
        out_shape=[in_vmem(shape, F32), in_vmem(shape, BF16)],
        compiler_params=pltpu.CompilerParams(vmem_limit_bytes=VMEM_LIMIT),
        name="assemble",
    )(*early, *late)


def finish_kernel(kept, arrived, *outs):
    for n, out in enumerate(outs):
        out[...] = kept[n] + arrived[n].astype(F32)


def finish(kept, arrived):
    vmem = pl.BlockSpec(memory_space=pltpu.VMEM)
    return pl.pallas_call(
        finish_kernel,
        in_specs=[vmem, vmem],
        out_specs=[vmem] * 4,
        out_shape=[jax.ShapeDtypeStruct(kept.shape[1:], F32)] * 4,
        compiler_params=pltpu.CompilerParams(vmem_limit_bytes=VMEM_LIMIT),
        name="finish",
    )(kept, arrived)


def ring_shift(x, axis, distance):
    size = lax.axis_size(axis)
    return lax.ppermute(x, axis, [(i, (i + distance) % size) for i in range(size)])


def passed_along(block, axis, distance):
    devices = range(lax.axis_size(axis))
    route = [(i - distance, i) for i in devices if i - distance in devices]
    return lax.ppermute(block, axis, route)


def others(x):
    return [ring_shift(x, "ma", d) for d in range(1, lax.axis_size("ma"))]


def local(
    patches,
    cls_rows,
    w_query,
    w_key,
    w_value,
    w_out,
    a_query,
    a_key,
    a_value,
    a_out,
    upstream,
    slice_to_scan,
):
    line = ("gz", "dev")
    slices, _, width = patches.shape
    cols = w_query.shape[1]
    chips = lax.axis_size("gz")
    up = upstream[0]
    (
        held, key_held, value_held, out_held, probs, stats, cls_norm, head_terms, *early
    ) = encoder_forward(patches, cls_rows, w_query, w_key, w_value, w_out, chips)
    d_wide, allowed = prepare_window(slice_to_scan, up, a_out, slices)
    total = head_terms
    for term in others(head_terms):
        total = total + term
    embedded = (cls_rows.astype(F32) + total).astype(BF16)
    following = passed_along(embedded, line, -1)
    early_here = early[:1] + [ring_shift(early[n], "gz", n) for n in range(1, chips)]
    d_own = window_gradients(embedded, following, a_query, a_key, a_value, d_wide, allowed)
    d_others = jnp.stack(others(d_own))
    lower = d_own[slices:].astype(F32)
    for n in range(d_others.shape[0]):
        lower = lower + d_others[n, slices:].astype(F32)
    carried = passed_along(
        jnp.concatenate([lower, up[slices:].astype(F32)], axis=0), line, 1
    )
    late = encoder_backward(
        held, probs, stats, d_own, d_others, carried, embedded, up, key_held, value_held, out_held,
        cls_norm, chips,
    )
    late_here = list(late[:1]) + [ring_shift(late[n], "gz", n) for n in range(1, chips)]
    kept, sent = assemble(early_here, late_here, slices, cols, width // chips // 2)
    return tuple(finish(kept, ring_shift(sent, "dev", 1)))


def solution(mesh):
    return jax.shard_map(
        local,
        mesh=mesh,
        in_specs=(
            P(("grp", "gz", "dev"), None, None),
            P(("grp", "gz", "dev"), None),
            P(None, "ma"),
            P(None, "ma"),
            P(None, "ma"),
            P("ma", None),
            P(None, "ma"),
            P(None, "ma"),
            P(None, "ma"),
            P("ma", None),
            P(("grp", "gz", "dev"), None, None),
            P("grp"),
        ),
        out_specs=(
            P(("grp", "gz", "dev"), "ma"),
            P(("grp", "gz", "dev"), "ma"),
            P(("grp", "gz", "dev"), "ma"),
            P(("grp", "gz", "dev"), "ma"),
        ),
        check_vma=False,
    )
```

```python
import functools

import jax
import jax.numpy as jnp
from jax import lax
from jax.experimental import pallas as pl
from jax.experimental.pallas import tpu as pltpu
from jax.sharding import PartitionSpec as P

HD = 64
SLOT = 8
LANES = 128
F32 = jnp.float32
BF16 = jnp.bfloat16
VMEM_LIMIT = 16 * 1024 * 1024


def dot(a, b, dims=((1,), (0,))):
    return lax.dot_general(a, b, (dims, ((), ())), preferred_element_type=F32)


BY_COLS = ((1,), (1,))
BY_ROWS = ((0,), (0,))


def normalize(values):
    row_mean = jnp.mean(values, axis=-1, keepdims=True)
    centred = values - row_mean
    variance = jnp.mean(centred * centred, axis=-1, keepdims=True)
    inv_std = lax.rsqrt(variance + 1e-05)
    return centred * inv_std, inv_std


def head_mask(slices, cols):
    shape = (slices * SLOT, cols)
    row = lax.broadcasted_iota(jnp.int32, shape, 0)
    col = lax.broadcasted_iota(jnp.int32, shape, 1)
    return row % SLOT == col // HD


def slot_rows(rows):
    slices, cols = rows.shape
    wide = jnp.broadcast_to(rows.astype(F32)[:, None, :], (slices, SLOT, cols))
    return wide.reshape(slices * SLOT, cols)


def expand(rows):
    wide = slot_rows(rows)
    return jnp.where(head_mask(rows.shape[0], rows.shape[1]), wide, 0.0).astype(BF16)


def collapse(full):
    rows, cols = full.shape
    kept = jnp.where(head_mask(rows // SLOT, cols), full, 0.0)
    return jnp.sum(kept.reshape(rows // SLOT, SLOT, cols), axis=1)


def in_vmem(shape, dtype):
    return pltpu.VMEM(shape, dtype)


def lane_blocks(rows):
    cols = rows.shape[1]
    spare = -cols % LANES
    if spare:
        rows = jnp.concatenate([rows, jnp.zeros((rows.shape[0], spare), rows.dtype)], axis=1)
    return jnp.concatenate(
        [rows[:, b : b + LANES] for b in range(0, cols + spare, LANES)], axis=0
    )


def from_lane_blocks(rows, cols):
    count = rows.shape[0] // pl.cdiv(cols, LANES)
    blocks = [rows[b : b + count] for b in range(0, rows.shape[0], count)]
    return jnp.concatenate(blocks, axis=1)[:, :cols]


def write_messages(outs, factor, rows, turned):
    turned[:, : factor.shape[0]] = factor.T
    right = lane_blocks(rows.astype(F32)).astype(BF16)
    chips = len(outs)
    half = turned.shape[0] // chips // 2
    here = lax.axis_index("gz")
    for shift in range(chips):
        first = lax.rem(here + shift, chips) * (2 * half)
        block = turned[pl.ds(pl.multiple_of(first, SLOT), 2 * half), : factor.shape[0]]
        both = jnp.concatenate([block[:half], block[half:]], axis=1)
        outs[shift][:half] = both.astype(BF16)
        outs[shift][half:] = right


def forward_kernel(
    chunk,
    patches_hbm,
    w_query_hbm,
    w_key_hbm,
    w_value_hbm,
    w_out_hbm,
    cls_rows,
    patches,
    w_key,
    w_value,
    w_out,
    probs,
    stats,
    cls_norm,
    head_terms,
    factor,
    pooled,
    w_query,
    query_keys,
    sems,
    patch_sems,
):
    slices, tokens, width = patches.shape
    scale = float(HD) ** (-0.5)

    def fetch(source, target, n):
        copy = pltpu.make_async_copy(source, target, sems.at[n])
        copy.start()
        return copy

    get_query = fetch(w_query_hbm, w_query, 0)
    get_key = fetch(w_key_hbm, w_key, 1)
    get_patches = []
    for c in range(slices // chunk):
        part = pl.ds(c * chunk, chunk)
        copy = pltpu.make_async_copy(patches_hbm.at[part], patches.at[part], patch_sems.at[c])
        copy.start()
        get_patches.append(copy)
    get_value = fetch(w_value_hbm, w_value, 2)
    get_out = fetch(w_out_hbm, w_out, 3)

    rows = normalize(cls_rows[...].astype(F32))[0].astype(BF16)
    cls_norm[...] = rows
    get_query.wait()
    q = dot(rows, w_query[...]).astype(BF16)
    get_key.wait()
    keys = (dot(expand(q), w_key[...], BY_COLS) * scale).astype(BF16).astype(F32)
    key_sums = jnp.sum(keys, axis=-1, keepdims=True)
    place = lax.broadcasted_iota(jnp.int32, (SLOT, width), 0)
    entry = lax.broadcasted_iota(jnp.int32, (SLOT, width), 1)
    picks = jnp.where((place == 0) | ((place == 1) & (entry == 0)), 1.0, 0.0)
    for z in range(slices):
        query_keys[z] = jnp.concatenate(
            [keys[z * SLOT : (z + 1) * SLOT], picks], axis=0
        ).astype(BF16)

    def measure(z):
        x = patches[z]
        raw = dot(query_keys[z], x, BY_COLS)
        wide = x.astype(F32)
        first = wide[:, 0:1]
        squares = None
        for b in range(0, width, LANES):
            off = wide[:, b : b + LANES] - first
            squares = off * off if squares is None else squares + off * off
        total = jnp.sum(squares.T, axis=0, keepdims=True)
        return raw, total

    def attend(z, raw, total):
        mean = raw[SLOT : SLOT + 1] * (1.0 / width)
        off = mean - raw[SLOT + 1 : SLOT + 2]
        inv_std = lax.rsqrt(jnp.maximum(total * (1.0 / width) - off * off, 0.0) + 1e-05)
        stats[z : z + 1] = mean
        stats[slices + z : slices + z + 1] = inv_std
        here = slice(z * SLOT, (z + 1) * SLOT)
        scores = inv_std * (raw[:SLOT] - mean * key_sums[here])
        powers = jnp.exp(scores - jnp.max(scores, axis=-1, keepdims=True))
        p = powers / jnp.sum(powers, axis=-1, keepdims=True)
        probs[z] = p
        weights = (p.astype(BF16).astype(F32) * inv_std).astype(BF16)
        shift = jnp.sum(weights.astype(F32) * mean, axis=-1, keepdims=True)
        factor[here] = dot(weights, patches[z]) - shift

    waiting = []
    for c in range(slices // chunk):
        get_patches[c].wait()
        ready = [(z,) + measure(z) for z in range(c * chunk, (c + 1) * chunk)]
        for item in waiting:
            attend(*item)
        waiting = ready
    for item in waiting:
        attend(*item)

    get_value.wait()
    value_factor = factor[...]
    pool = collapse(dot(value_factor.astype(BF16), w_value[...])).astype(BF16)
    get_out.wait()
    head_terms[...] = dot(pool, w_out[...])
    pooled[...] = jnp.concatenate([q.astype(F32), pool.astype(F32)], axis=0)


def encoder_forward(patches, cls_rows, w_query, w_key, w_value, w_out):
    slices, tokens, width = patches.shape
    cols = w_query.shape[1]
    chunk = 2
    far = (patches, w_query, w_key, w_value, w_out)
    hbm = pl.BlockSpec(memory_space=pltpu.HBM)
    vmem = pl.BlockSpec(memory_space=pltpu.VMEM)
    out_shape = [
        in_vmem(patches.shape, BF16),
        in_vmem(w_key.shape, BF16),
        in_vmem(w_value.shape, BF16),
        in_vmem(w_out.shape, BF16),
        in_vmem((slices, SLOT, tokens), F32),
        in_vmem((2 * slices, tokens), F32),
        in_vmem((slices, width), BF16),
        in_vmem((slices, width), F32),
        in_vmem((slices * SLOT, width), F32),
        in_vmem((2 * slices, cols), F32),
    ]
    return pl.pallas_call(
        functools.partial(forward_kernel, chunk),
        in_specs=[hbm] * 5 + [vmem],
        out_specs=[vmem] * len(out_shape),
        out_shape=out_shape,
        scratch_shapes=[
            pltpu.VMEM(w_query.shape, BF16),
            pltpu.VMEM((slices, 2 * SLOT, width), BF16),
            pltpu.SemaphoreType.DMA((4,)),
            pltpu.SemaphoreType.DMA((slices // chunk,)),
        ],
        compiler_params=pltpu.CompilerParams(vmem_limit_bytes=VMEM_LIMIT),
        name="encoder_forward",
    )(*[pltpu.with_memory_space_constraint(a, pltpu.HBM) for a in far], cls_rows)


def head_rows(x, heads):
    rows, cols = x.shape
    wide = (heads * rows, cols)
    mine = (
        lax.broadcasted_iota(jnp.int32, wide, 0) // rows
        == lax.broadcasted_iota(jnp.int32, wide, 1) // HD
    )
    tall = jnp.broadcast_to(x.astype(F32)[None], (heads, rows, cols)).reshape(wide)
    return jnp.where(mine, tall, 0.0).astype(BF16), mine


def prepare_kernel(heads, slices, chips, ids, up, a_out, factor, pooled, d_wide, bias, *rest):
    outs, turned = rest[:chips], rest[chips]
    write_messages(outs, factor[...], pooled[...], turned)
    rows = 2 * slices
    total = ids.shape[0]
    start = (lax.axis_index("gz") * lax.axis_size("dev") + lax.axis_index("dev")) * slices
    d_pooled = dot(up[...], a_out[...], BY_COLS).astype(BF16)
    d_wide[...] = head_rows(d_pooled, heads)[0]
    square = (heads * rows, rows)
    i_of = lax.broadcasted_iota(jnp.int32, square, 0) % rows
    j_of = lax.broadcasted_iota(jnp.int32, square, 1)
    id_i = jnp.full(square, -1, jnp.int32)
    id_j = jnp.full(square, -1, jnp.int32)
    for n in range(rows):
        place = start + n
        scan = jnp.where(place < total, ids[jnp.minimum(place, total - 1)], -1)
        id_i = jnp.where(i_of == n, scan, id_i)
        id_j = jnp.where(j_of == n, scan, id_j)
    allowed = ((id_i == id_j) & (id_j >= 0)) | (i_of == j_of)
    bias[...] = jnp.where(allowed, 1.0, 0.0)


def prepare_window(ids, up, a_out, factor, pooled, slices, chips):
    cols = a_out.shape[0]
    width = a_out.shape[1]
    message = (width // chips // 2 + 2 * slices * pl.cdiv(cols, LANES), LANES)
    heads = cols // HD
    rows = 2 * slices
    vmem = pl.BlockSpec(memory_space=pltpu.VMEM)
    return pl.pallas_call(
        functools.partial(prepare_kernel, heads, slices, chips),
        in_specs=[pl.BlockSpec(memory_space=pltpu.SMEM)] + [vmem] * 4,
        out_specs=[vmem] * (2 + chips),
        out_shape=[in_vmem((heads * rows, cols), BF16), in_vmem((heads * rows, rows), F32)]
        + [in_vmem(message, BF16)] * chips,
        scratch_shapes=[pltpu.VMEM((width, LANES), F32)],
        compiler_params=pltpu.CompilerParams(vmem_limit_bytes=VMEM_LIMIT),
        name="prepare_window",
    )(ids, up, a_out, factor, pooled)


def window_kernel(heads, own, following, a_query, a_key, a_value, d_wide, allowed, d_half):
    scale = float(HD) ** (-0.5)
    window = jnp.concatenate([own[...].astype(F32), following[...].astype(F32)], axis=0)
    rows = window.shape[0]
    cols = a_query.shape[1]
    half = normalize(window)[0].astype(BF16)
    q_wide, mine = head_rows(dot(half, a_query[...]).astype(BF16), heads)
    k = dot(half, a_key[...]).astype(BF16)
    v = dot(half, a_value[...]).astype(BF16)
    scores = jnp.where(allowed[...] > 0.5, dot(q_wide, k, BY_COLS) * scale, -1e30)
    d_probs = dot(d_wide[...], v, BY_COLS)
    powers = jnp.exp(scores - jnp.max(scores, axis=-1, keepdims=True))
    probs = powers / jnp.sum(powers, axis=-1, keepdims=True)
    inner = jnp.sum(probs * d_probs, axis=-1, keepdims=True)
    d_scores = (probs * (d_probs - inner) * scale).astype(BF16)
    d_value = dot(probs.astype(BF16), d_wide[...], BY_ROWS).astype(BF16)
    d_query = jnp.where(mine, dot(d_scores, k), 0.0)
    d_query = jnp.sum(d_query.reshape(heads, rows, cols), axis=0).astype(BF16)
    d_key = dot(d_scores, q_wide, BY_ROWS).astype(BF16)
    terms = (
        dot(d_value, a_value[...], BY_COLS)
        + dot(d_query, a_query[...], BY_COLS)
        + dot(d_key, a_key[...], BY_COLS)
    )
    d_half[...] = terms.astype(BF16)


def window_gradients(own, following, a_query, a_key, a_value, d_wide, allowed):
    slices, width = own.shape
    heads = a_query.shape[1] // HD
    vmem = pl.BlockSpec(memory_space=pltpu.VMEM)
    return pl.pallas_call(
        functools.partial(window_kernel, heads),
        in_specs=[vmem] * 7,
        out_specs=vmem,
        out_shape=in_vmem((2 * slices, width), BF16),
        compiler_params=pltpu.CompilerParams(vmem_limit_bytes=VMEM_LIMIT),
        name="window_gradients",
    )(own, following, a_query, a_key, a_value, d_wide, allowed)


def backward_kernel(
    chips,
    patches,
    probs,
    stats,
    d_own,
    d_others,
    carried,
    embedded,
    up,
    w_key,
    w_value,
    w_out,
    cls_norm,
    *rest,
):
    outs, (turned, d_keys, factor) = rest[:chips], rest[chips:]
    scale = float(HD) ** (-0.5)
    slices = embedded.shape[0]

    win_norm, inv_std = normalize(embedded[...].astype(F32))
    d_normed = d_own[:slices].astype(F32) + carried[:slices]
    for n in range(d_others.shape[0]):
        d_normed = d_normed + d_others[n, :slices].astype(F32)
    centred = (
        d_normed
        - jnp.mean(d_normed, axis=-1, keepdims=True)
        - win_norm * jnp.mean(d_normed * win_norm, axis=-1, keepdims=True)
    )
    d_embed = up[:slices].astype(F32) + carried[slices:] + inv_std * centred
    d_embed = d_embed.astype(BF16)
    d_att = dot(d_embed, w_out[...], BY_COLS).astype(BF16)
    keys = dot(expand(d_att), w_value[...], BY_COLS).astype(BF16).astype(F32)
    key_sums = jnp.sum(keys, axis=-1, keepdims=True)
    d_keys[...] = keys

    for z in range(slices):
        here = slice(z * SLOT, (z + 1) * SLOT)
        x = patches[z]
        p = probs[z]
        mean = stats[z : z + 1]
        inv = stats[slices + z : slices + z + 1]
        raw = dot(d_keys[here].astype(BF16), x, BY_COLS)
        d_probs = inv * (raw - mean * key_sums[here])
        inner = jnp.sum(p * d_probs, axis=-1, keepdims=True)
        d_scores = (p * (d_probs - inner) * scale).astype(BF16)
        weights = (d_scores.astype(F32) * inv).astype(BF16)
        shift = jnp.sum(weights.astype(F32) * mean, axis=-1, keepdims=True)
        factor[here] = dot(weights, x) - shift

    key_factor = factor[...]
    d_query = collapse(dot(key_factor.astype(BF16), w_key[...])).astype(BF16)
    slot = lax.broadcasted_iota(jnp.int32, key_factor.shape, 0) % SLOT
    left = jnp.where(slot == SLOT - 2, slot_rows(cls_norm[...]), key_factor)
    left = jnp.where(slot == SLOT - 1, slot_rows(d_embed), left)
    right = jnp.concatenate([d_att.astype(F32), d_query.astype(F32)], axis=0)
    write_messages(outs, left, right, turned)


def encoder_backward(
    patches, probs, stats, d_own, d_others, carried, embedded, up, w_key, w_value, w_out, cls_norm,
    chips,
):
    slices, tokens, width = patches.shape
    cols = w_key.shape[1]
    vmem = pl.BlockSpec(memory_space=pltpu.VMEM)
    message = (width // chips // 2 + 2 * slices * pl.cdiv(cols, LANES), LANES)
    return pl.pallas_call(
        functools.partial(backward_kernel, chips),
        in_specs=[vmem] * 12,
        out_specs=[vmem] * chips,
        out_shape=[in_vmem(message, BF16)] * chips,
        scratch_shapes=[
            pltpu.VMEM((width, LANES), F32),
            pltpu.VMEM((slices * SLOT, width), F32),
            pltpu.VMEM((slices * SLOT, width), F32),
        ],
        compiler_params=pltpu.CompilerParams(vmem_limit_bytes=VMEM_LIMIT),
        name="encoder_backward",
    )(patches, probs, stats, d_own, d_others, carried, embedded, up, w_key, w_value, w_out, cls_norm)


def assemble_kernel(slices, cols, half, chips, *refs):
    early, late, (kept, sent) = refs[:chips], refs[chips : 2 * chips], refs[2 * chips :]
    mask = head_mask(slices, cols)
    slot = lax.broadcasted_iota(jnp.int32, mask.shape, 0) % SLOT
    depth = slices * SLOT

    def stacked(messages):
        top = [m[:half, :depth].astype(F32) for m in messages]
        bottom = [m[:half, depth:].astype(F32) for m in messages]
        return jnp.concatenate(
            [jnp.concatenate(top, axis=1), jnp.concatenate(bottom, axis=1)], axis=0
        ).astype(BF16)

    first, second = [], []
    for messages, into in ((early, first), (late, second)):
        for m in messages:
            rows = from_lane_blocks(m[half:].astype(F32), cols)
            into.append([slot_rows(rows[:slices]), slot_rows(rows[slices:])])
    left_value, left_key = stacked(early), stacked(late)

    def right(blocks):
        return jnp.concatenate(blocks, axis=0).astype(BF16)

    grads = [
        dot(left_key, right([jnp.where(slot == SLOT - 2, b[1], 0.0) for b in second])),
        dot(left_key, right([jnp.where(mask, b[0], 0.0) for b in first])),
        dot(left_value, right([jnp.where(mask, b[0], 0.0) for b in second])),
        dot(left_key, right([jnp.where(slot == SLOT - 1, b[1], 0.0) for b in first])),
    ]
    lower = lax.axis_index("dev") == 0
    for n, total in enumerate(grads):
        top, bottom = total[:half], total[half:]
        kept[n] = jnp.where(lower, top, bottom)
        sent[n] = jnp.where(lower, bottom, top).astype(BF16)


def assemble(early, late, slices, cols, half):
    vmem = pl.BlockSpec(memory_space=pltpu.VMEM)
    shape = (4, half, cols)
    return pl.pallas_call(
        functools.partial(assemble_kernel, slices, cols, half, len(early)),
        in_specs=[vmem] * (2 * len(early)),
        out_specs=[vmem, vmem],
        out_shape=[in_vmem(shape, F32), in_vmem(shape, BF16)],
        compiler_params=pltpu.CompilerParams(vmem_limit_bytes=VMEM_LIMIT),
        name="assemble",
    )(*early, *late)


def finish_kernel(kept, arrived, *outs):
    for n, out in enumerate(outs):
        out[...] = kept[n] + arrived[n].astype(F32)


def finish(kept, arrived):
    vmem = pl.BlockSpec(memory_space=pltpu.VMEM)
    return pl.pallas_call(
        finish_kernel,
        in_specs=[vmem, vmem],
        out_specs=[vmem] * 4,
        out_shape=[jax.ShapeDtypeStruct(kept.shape[1:], F32)] * 4,
        compiler_params=pltpu.CompilerParams(vmem_limit_bytes=VMEM_LIMIT),
        name="finish",
    )(kept, arrived)


def ring_shift(x, axis, distance):
    size = lax.axis_size(axis)
    return lax.ppermute(x, axis, [(i, (i + distance) % size) for i in range(size)])


def passed_along(block, axis, distance):
    devices = range(lax.axis_size(axis))
    route = [(i - distance, i) for i in devices if i - distance in devices]
    return lax.ppermute(block, axis, route)


def others(x):
    return [ring_shift(x, "ma", d) for d in range(1, lax.axis_size("ma"))]


def local(
    patches,
    cls_rows,
    w_query,
    w_key,
    w_value,
    w_out,
    a_query,
    a_key,
    a_value,
    a_out,
    upstream,
    slice_to_scan,
):
    line = ("gz", "dev")
    slices, _, width = patches.shape
    cols = w_query.shape[1]
    chips = lax.axis_size("gz")
    up = upstream[0]
    (
        held, key_held, value_held, out_held, probs, stats, cls_norm, head_terms, factor, pooled
    ) = encoder_forward(patches, cls_rows, w_query, w_key, w_value, w_out)
    d_wide, allowed, *early = prepare_window(
        slice_to_scan, up, a_out, factor, pooled, slices, chips
    )
    early_here = early[:1] + [ring_shift(early[n], "gz", n) for n in range(1, chips)]
    head_others = others(head_terms)
    total = head_terms
    for term in head_others:
        total = total + term
    embedded = (cls_rows.astype(F32) + total).astype(BF16)
    following = passed_along(embedded, line, -1)
    following, early_here[1] = lax.optimization_barrier((following, early_here[1]))
    d_own = window_gradients(embedded, following, a_query, a_key, a_value, d_wide, allowed)
    d_others = others(d_own)
    d_others, early_here[2] = lax.optimization_barrier((d_others, early_here[2]))
    d_others = jnp.stack(d_others)
    lower = d_own[slices:].astype(F32)
    for n in range(d_others.shape[0]):
        lower = lower + d_others[n, slices:].astype(F32)
    carried = passed_along(
        jnp.concatenate([lower, up[slices:].astype(F32)], axis=0), line, 1
    )
    carried, early_here[3:] = lax.optimization_barrier((carried, early_here[3:]))
    late = encoder_backward(
        held, probs, stats, d_own, d_others, carried, embedded, up, key_held, value_held, out_held,
        cls_norm, chips,
    )
    late_here = list(late[:1]) + [ring_shift(late[n], "gz", n) for n in range(1, chips)]
    kept, sent = assemble(early_here, late_here, slices, cols, width // chips // 2)
    return tuple(finish(kept, ring_shift(sent, "dev", 1)))


def solution(mesh):
    return jax.shard_map(
        local,
        mesh=mesh,
        in_specs=(
            P(("grp", "gz", "dev"), None, None),
            P(("grp", "gz", "dev"), None),
            P(None, "ma"),
            P(None, "ma"),
            P(None, "ma"),
            P("ma", None),
            P(None, "ma"),
            P(None, "ma"),
            P(None, "ma"),
            P("ma", None),
            P(("grp", "gz", "dev"), None, None),
            P("grp"),
        ),
        out_specs=(
            P(("grp", "gz", "dev"), "ma"),
            P(("grp", "gz", "dev"), "ma"),
            P(("grp", "gz", "dev"), "ma"),
            P(("grp", "gz", "dev"), "ma"),
        ),
        check_vma=False,
    )
```

```python
import functools

import jax
import jax.numpy as jnp
from jax import lax
from jax.experimental import pallas as pl
from jax.experimental.pallas import tpu as pltpu
from jax.sharding import PartitionSpec as P

HD = 64
SLOT = 8
LANES = 128
F32 = jnp.float32
BF16 = jnp.bfloat16
CHUNK = 2
VMEM_LIMIT = 16 * 1024 * 1024


def dot(a, b, dims=((1,), (0,))):
    return lax.dot_general(a, b, (dims, ((), ())), preferred_element_type=F32)


BY_COLS = ((1,), (1,))
BY_ROWS = ((0,), (0,))


def normalize(values):
    row_mean = jnp.mean(values, axis=-1, keepdims=True)
    centred = values - row_mean
    variance = jnp.mean(centred * centred, axis=-1, keepdims=True)
    inv_std = lax.rsqrt(variance + 1e-05)
    return centred * inv_std, inv_std


def head_mask(slices, cols):
    shape = (slices * SLOT, cols)
    row = lax.broadcasted_iota(jnp.int32, shape, 0)
    col = lax.broadcasted_iota(jnp.int32, shape, 1)
    return row % SLOT == col // HD


def slot_rows(rows):
    slices, cols = rows.shape
    wide = jnp.broadcast_to(rows.astype(F32)[:, None, :], (slices, SLOT, cols))
    return wide.reshape(slices * SLOT, cols)


def expand(rows):
    wide = slot_rows(rows)
    return jnp.where(head_mask(rows.shape[0], rows.shape[1]), wide, 0.0).astype(BF16)


def collapse(full):
    rows, cols = full.shape
    kept = jnp.where(head_mask(rows // SLOT, cols), full, 0.0)
    return jnp.sum(kept.reshape(rows // SLOT, SLOT, cols), axis=1)


def in_vmem(shape, dtype):
    return pltpu.VMEM(shape, dtype)


def lane_blocks(rows):
    cols = rows.shape[1]
    spare = -cols % LANES
    if spare:
        rows = jnp.concatenate([rows, jnp.zeros((rows.shape[0], spare), rows.dtype)], axis=1)
    return jnp.concatenate(
        [rows[:, b : b + LANES] for b in range(0, cols + spare, LANES)], axis=0
    )


def from_lane_blocks(rows, cols):
    count = rows.shape[0] // pl.cdiv(cols, LANES)
    blocks = [rows[b : b + count] for b in range(0, rows.shape[0], count)]
    return jnp.concatenate(blocks, axis=1)[:, :cols]


def partner(here, shift, chips):
    return here ^ shift if chips & (chips - 1) == 0 else (here + shift) % chips


def forward_kernel(
    chunk,
    patches_hbm,
    w_query_hbm,
    w_key_hbm,
    w_value_hbm,
    w_out_hbm,
    cls_hbm,
    patches,
    w_key,
    w_value,
    w_out,
    probs,
    stats,
    cls_norm,
    head_terms,
    factor,
    pooled,
    cls_rows,
    w_query,
    query_keys,
    sems,
    patch_sems,
):
    slices, tokens, width = patches.shape
    scale = float(HD) ** (-0.5)

    def fetch(source, target, n):
        copy = pltpu.make_async_copy(source, target, sems.at[n])
        copy.start()
        return copy

    get_rows = fetch(cls_hbm, cls_rows, 4)
    get_query = fetch(w_query_hbm, w_query, 0)
    get_key = fetch(w_key_hbm, w_key, 1)
    get_patches = []
    for c in range(slices // chunk):
        part = pl.ds(c * chunk, chunk)
        copy = pltpu.make_async_copy(patches_hbm.at[part], patches.at[part], patch_sems.at[c])
        copy.start()
        get_patches.append(copy)
    get_value = fetch(w_value_hbm, w_value, 2)
    get_out = fetch(w_out_hbm, w_out, 3)

    get_rows.wait()
    rows = normalize(cls_rows[...].astype(F32))[0].astype(BF16)
    cls_norm[...] = rows
    get_query.wait()
    q = dot(rows, w_query[...]).astype(BF16)
    get_key.wait()
    keys = (dot(expand(q), w_key[...], BY_COLS) * scale).astype(BF16).astype(F32)
    key_sums = jnp.sum(keys, axis=-1, keepdims=True)
    place = lax.broadcasted_iota(jnp.int32, (SLOT, width), 0)
    entry = lax.broadcasted_iota(jnp.int32, (SLOT, width), 1)
    picks = jnp.where((place == 0) | ((place == 1) & (entry == 0)), 1.0, 0.0)
    for z in range(slices):
        query_keys[z] = jnp.concatenate(
            [keys[z * SLOT : (z + 1) * SLOT], picks], axis=0
        ).astype(BF16)

    def measure(z):
        x = patches[z]
        raw = dot(query_keys[z], x, BY_COLS)
        wide = x.astype(F32)
        first = wide[:, 0:1]
        squares = None
        for b in range(0, width, LANES):
            off = wide[:, b : b + LANES] - first
            squares = off * off if squares is None else squares + off * off
        total = jnp.sum(squares.T, axis=0, keepdims=True)
        return raw, total

    def attend(z, raw, total):
        mean = raw[SLOT : SLOT + 1] * (1.0 / width)
        off = mean - raw[SLOT + 1 : SLOT + 2]
        inv_std = lax.rsqrt(jnp.maximum(total * (1.0 / width) - off * off, 0.0) + 1e-05)
        stats[z : z + 1] = mean
        stats[slices + z : slices + z + 1] = inv_std
        here = slice(z * SLOT, (z + 1) * SLOT)
        scores = inv_std * (raw[:SLOT] - mean * key_sums[here])
        powers = jnp.exp(scores - jnp.max(scores, axis=-1, keepdims=True))
        p = powers / jnp.sum(powers, axis=-1, keepdims=True)
        probs[z] = p
        weights = (p.astype(BF16).astype(F32) * inv_std).astype(BF16)
        shift = jnp.sum(weights.astype(F32) * mean, axis=-1, keepdims=True)
        factor[here] = dot(weights, patches[z]) - shift

    waiting = []
    for c in range(slices // chunk):
        get_patches[c].wait()
        ready = [(z,) + measure(z) for z in range(c * chunk, (c + 1) * chunk)]
        for item in waiting:
            attend(*item)
        waiting = ready
    for item in waiting:
        attend(*item)

    get_value.wait()
    value_factor = factor[...]
    pool = collapse(dot(value_factor.astype(BF16), w_value[...])).astype(BF16)
    get_out.wait()
    head_terms[...] = dot(pool, w_out[...]).astype(BF16)
    pooled[...] = jnp.concatenate([q.astype(F32), pool.astype(F32)], axis=0)


def encoder_forward(patches, cls_rows, w_query, w_key, w_value, w_out):
    slices, tokens, width = patches.shape
    cols = w_query.shape[1]
    chunk = CHUNK
    far = (patches, w_query, w_key, w_value, w_out, cls_rows)
    hbm = pl.BlockSpec(memory_space=pltpu.HBM)
    vmem = pl.BlockSpec(memory_space=pltpu.VMEM)
    out_shape = [
        in_vmem(patches.shape, BF16),
        in_vmem(w_key.shape, BF16),
        in_vmem(w_value.shape, BF16),
        in_vmem(w_out.shape, BF16),
        in_vmem((slices, SLOT, tokens), F32),
        in_vmem((2 * slices, tokens), F32),
        in_vmem((slices, width), BF16),
        in_vmem((slices, width), BF16),
        in_vmem((slices * SLOT, width), F32),
        in_vmem((2 * slices, cols), F32),
    ]
    return pl.pallas_call(
        functools.partial(forward_kernel, chunk),
        in_specs=[hbm] * len(far),
        out_specs=[vmem] * len(out_shape),
        out_shape=out_shape,
        scratch_shapes=[
            pltpu.VMEM(cls_rows.shape, BF16),
            pltpu.VMEM(w_query.shape, BF16),
            pltpu.VMEM((slices, 2 * SLOT, width), BF16),
            pltpu.SemaphoreType.DMA((5,)),
            pltpu.SemaphoreType.DMA((slices // chunk,)),
        ],
        compiler_params=pltpu.CompilerParams(vmem_limit_bytes=VMEM_LIMIT),
        name="encoder_forward",
    )(*[pltpu.with_memory_space_constraint(a, pltpu.HBM) for a in far])


def head_rows(x, heads):
    rows, cols = x.shape
    wide = (heads * rows, cols)
    mine = (
        lax.broadcasted_iota(jnp.int32, wide, 0) // rows
        == lax.broadcasted_iota(jnp.int32, wide, 1) // HD
    )
    tall = jnp.broadcast_to(x.astype(F32)[None], (heads, rows, cols)).reshape(wide)
    return jnp.where(mine, tall, 0.0).astype(BF16), mine


def prepare_kernel(heads, slices, ids, up, a_out, factor, pooled, d_wide, bias, turned, early):
    value_factor = factor[...]
    turned[...] = jnp.concatenate([jnp.zeros_like(value_factor), value_factor], axis=0).T
    early[...] = lane_blocks(pooled[...]).astype(BF16)
    rows = 2 * slices
    total = ids.shape[0]
    start = (lax.axis_index("gz") * lax.axis_size("dev") + lax.axis_index("dev")) * slices
    d_pooled = dot(up[...], a_out[...], BY_COLS).astype(BF16)
    d_wide[...] = head_rows(d_pooled, heads)[0]
    square = (heads * rows, rows)
    i_of = lax.broadcasted_iota(jnp.int32, square, 0) % rows
    j_of = lax.broadcasted_iota(jnp.int32, square, 1)
    id_i = jnp.full(square, -1, jnp.int32)
    id_j = jnp.full(square, -1, jnp.int32)
    for n in range(rows):
        place = start + n
        scan = jnp.where(place < total, ids[jnp.minimum(place, total - 1)], -1)
        id_i = jnp.where(i_of == n, scan, id_i)
        id_j = jnp.where(j_of == n, scan, id_j)
    allowed = ((id_i == id_j) & (id_j >= 0)) | (i_of == j_of)
    bias[...] = jnp.where(allowed, 1.0, 0.0)


def prepare_window(ids, up, a_out, factor, pooled, slices):
    cols = a_out.shape[0]
    width = a_out.shape[1]
    heads = cols // HD
    rows = 2 * slices
    vmem = pl.BlockSpec(memory_space=pltpu.VMEM)
    return pl.pallas_call(
        functools.partial(prepare_kernel, heads, slices),
        in_specs=[pl.BlockSpec(memory_space=pltpu.SMEM)] + [vmem] * 4,
        out_specs=[vmem] * 4,
        out_shape=[
            in_vmem((heads * rows, cols), BF16),
            in_vmem((heads * rows, rows), F32),
            in_vmem((width, 2 * slices * SLOT), F32),
            in_vmem((2 * slices * pl.cdiv(cols, LANES), LANES), BF16),
        ],
        compiler_params=pltpu.CompilerParams(vmem_limit_bytes=VMEM_LIMIT),
        name="prepare_window",
    )(ids, up, a_out, factor, pooled)


def window_kernel(heads, own, following, a_query, a_key, a_value, d_wide, allowed, d_half):
    scale = float(HD) ** (-0.5)
    window = jnp.concatenate([own[...].astype(F32), following[...].astype(F32)], axis=0)
    rows = window.shape[0]
    cols = a_query.shape[1]
    half = normalize(window)[0].astype(BF16)
    q_wide, mine = head_rows(dot(half, a_query[...]).astype(BF16), heads)
    k = dot(half, a_key[...]).astype(BF16)
    v = dot(half, a_value[...]).astype(BF16)
    scores = jnp.where(allowed[...] > 0.5, dot(q_wide, k, BY_COLS) * scale, -1e30)
    d_probs = dot(d_wide[...], v, BY_COLS)
    powers = jnp.exp(scores - jnp.max(scores, axis=-1, keepdims=True))
    probs = powers / jnp.sum(powers, axis=-1, keepdims=True)
    inner = jnp.sum(probs * d_probs, axis=-1, keepdims=True)
    d_scores = (probs * (d_probs - inner) * scale).astype(BF16)
    d_value = dot(probs.astype(BF16), d_wide[...], BY_ROWS).astype(BF16)
    d_query = jnp.where(mine, dot(d_scores, k), 0.0)
    d_query = jnp.sum(d_query.reshape(heads, rows, cols), axis=0).astype(BF16)
    d_key = dot(d_scores, q_wide, BY_ROWS).astype(BF16)
    terms = (
        dot(d_value, a_value[...], BY_COLS)
        + dot(d_query, a_query[...], BY_COLS)
        + dot(d_key, a_key[...], BY_COLS)
    )
    d_half[...] = terms.astype(BF16)


def window_gradients(own, following, a_query, a_key, a_value, d_wide, allowed):
    slices, width = own.shape
    heads = a_query.shape[1] // HD
    vmem = pl.BlockSpec(memory_space=pltpu.VMEM)
    return pl.pallas_call(
        functools.partial(window_kernel, heads),
        in_specs=[vmem] * 7,
        out_specs=vmem,
        out_shape=in_vmem((2 * slices, width), BF16),
        compiler_params=pltpu.CompilerParams(vmem_limit_bytes=VMEM_LIMIT),
        name="window_gradients",
    )(own, following, a_query, a_key, a_value, d_wide, allowed)


def backward_kernel(
    chips,
    patches,
    probs,
    stats,
    d_own,
    d_others,
    carried,
    embedded,
    up,
    w_key,
    w_value,
    w_out,
    cls_norm,
    turned_value,
    early,
    *rest,
):
    outs, (turned, d_keys, factor) = rest[:chips], rest[chips:]
    scale = float(HD) ** (-0.5)
    slices = embedded.shape[0]

    win_norm, inv_std = normalize(embedded[...].astype(F32))
    d_normed = d_own[:slices].astype(F32) + carried[:slices].astype(F32)
    for n in range(d_others.shape[0]):
        d_normed = d_normed + d_others[n, :slices].astype(F32)
    centred = (
        d_normed
        - jnp.mean(d_normed, axis=-1, keepdims=True)
        - win_norm * jnp.mean(d_normed * win_norm, axis=-1, keepdims=True)
    )
    d_embed = up[:slices].astype(F32) + carried[slices:].astype(F32) + inv_std * centred
    d_embed = d_embed.astype(BF16)
    d_att = dot(d_embed, w_out[...], BY_COLS).astype(BF16)
    keys = dot(expand(d_att), w_value[...], BY_COLS).astype(BF16).astype(F32)
    key_sums = jnp.sum(keys, axis=-1, keepdims=True)
    d_keys[...] = keys

    def score(z):
        return dot(d_keys[z * SLOT : (z + 1) * SLOT].astype(BF16), patches[z], BY_COLS)

    def attend(z, raw):
        here = slice(z * SLOT, (z + 1) * SLOT)
        p = probs[z]
        mean = stats[z : z + 1]
        inv = stats[slices + z : slices + z + 1]
        d_probs = inv * (raw - mean * key_sums[here])
        inner = jnp.sum(p * d_probs, axis=-1, keepdims=True)
        d_scores = (p * (d_probs - inner) * scale).astype(BF16)
        weights = (d_scores.astype(F32) * inv).astype(BF16)
        shift = jnp.sum(weights.astype(F32) * mean, axis=-1, keepdims=True)
        factor[here] = dot(weights, patches[z]) - shift

    waiting = []
    for c in range(0, slices, CHUNK):
        ready = [(z, score(z)) for z in range(c, c + CHUNK)]
        for item in waiting:
            attend(*item)
        waiting = ready
    for item in waiting:
        attend(*item)

    key_factor = factor[...]
    d_query = collapse(dot(key_factor.astype(BF16), w_key[...])).astype(BF16)
    slot = lax.broadcasted_iota(jnp.int32, key_factor.shape, 0) % SLOT
    left = jnp.where(slot == SLOT - 2, slot_rows(cls_norm[...]), key_factor)
    left = jnp.where(slot == SLOT - 1, slot_rows(d_embed), left)
    right = jnp.concatenate([d_att.astype(F32), d_query.astype(F32)], axis=0)
    turned[...] = jnp.concatenate([left, jnp.zeros_like(left)], axis=0).T + turned_value[...]
    late = lane_blocks(right).astype(BF16)
    part = turned.shape[0] // chips
    middle = part + late.shape[0]
    here = lax.axis_index("gz")
    for shift in range(chips):
        first = pl.multiple_of(partner(here, shift, chips) * part, SLOT)
        outs[shift][:part] = turned[pl.ds(first, part), :].astype(BF16)
        outs[shift][part:middle] = late
        outs[shift][middle:] = early[...]


def encoder_backward(
    patches, probs, stats, d_own, d_others, carried, embedded, up, w_key, w_value, w_out, cls_norm,
    turned_value, early, chips,
):
    slices, tokens, width = patches.shape
    cols = w_key.shape[1]
    vmem = pl.BlockSpec(memory_space=pltpu.VMEM)
    message = (width // chips + 4 * slices * pl.cdiv(cols, LANES), LANES)
    return pl.pallas_call(
        functools.partial(backward_kernel, chips),
        in_specs=[vmem] * 14,
        out_specs=[vmem] * chips,
        out_shape=[in_vmem(message, BF16)] * chips,
        scratch_shapes=[
            pltpu.VMEM((width, LANES), F32),
            pltpu.VMEM((slices * SLOT, width), F32),
            pltpu.VMEM((slices * SLOT, width), F32),
        ],
        compiler_params=pltpu.CompilerParams(vmem_limit_bytes=VMEM_LIMIT),
        name="encoder_backward",
    )(
        patches, probs, stats, d_own, d_others, carried, embedded, up, w_key, w_value, w_out, cls_norm,
        turned_value, early,
    )


def assemble_kernel(slices, cols, part, chips, *refs):
    messages, (kept, sent) = refs[:chips], refs[chips:]
    mask = head_mask(slices, cols)
    slot = lax.broadcasted_iota(jnp.int32, mask.shape, 0) % SLOT
    depth = slices * SLOT
    rows = 2 * slices * pl.cdiv(cols, LANES)

    def stacked(columns):
        blocks = [m[:part, columns].astype(F32) for m in messages]
        return jnp.concatenate(blocks, axis=1).astype(BF16)

    first, second = [], []
    for m in messages:
        for start, into in ((part, second), (part + rows, first)):
            block = from_lane_blocks(m[start : start + rows].astype(F32), cols)
            into.append([slot_rows(block[:slices]), slot_rows(block[slices:])])
    left_key, left_value = stacked(slice(0, depth)), stacked(slice(depth, 2 * depth))

    def right(blocks):
        return jnp.concatenate(blocks, axis=0).astype(BF16)

    grads = [
        dot(left_key, right([jnp.where(slot == SLOT - 2, b[1], 0.0) for b in second])),
        dot(left_key, right([jnp.where(mask, b[0], 0.0) for b in first])),
        dot(left_value, right([jnp.where(mask, b[0], 0.0) for b in second])),
        dot(left_key, right([jnp.where(slot == SLOT - 1, b[1], 0.0) for b in first])),
    ]
    lower = lax.axis_index("dev") == 0
    half = part // 2
    for n, total in enumerate(grads):
        top, bottom = total[:half], total[half:]
        kept[n] = jnp.where(lower, top, bottom)
        sent[n] = jnp.where(lower, bottom, top).astype(BF16)


def assemble(messages, slices, cols, part):
    vmem = pl.BlockSpec(memory_space=pltpu.VMEM)
    shape = (4, part // 2, cols)
    return pl.pallas_call(
        functools.partial(assemble_kernel, slices, cols, part, len(messages)),
        in_specs=[vmem] * len(messages),
        out_specs=[vmem, vmem],
        out_shape=[in_vmem(shape, F32), in_vmem(shape, BF16)],
        compiler_params=pltpu.CompilerParams(vmem_limit_bytes=VMEM_LIMIT),
        name="assemble",
    )(*messages)


def finish_kernel(kept, arrived, *refs):
    outs, sums, sems = refs[:4], refs[4], refs[5]
    copies = []
    for n, out in enumerate(outs):
        sums[n] = kept[n] + arrived[n].astype(F32)
        copy = pltpu.make_async_copy(sums.at[n], out, sems.at[n])
        copy.start()
        copies.append(copy)
    for copy in copies:
        copy.wait()


def finish(kept, arrived):
    vmem = pl.BlockSpec(memory_space=pltpu.VMEM)
    return pl.pallas_call(
        finish_kernel,
        in_specs=[vmem, vmem],
        out_specs=[pl.BlockSpec(memory_space=pltpu.HBM)] * 4,
        out_shape=[pltpu.HBM(kept.shape[1:], F32)] * 4,
        scratch_shapes=[pltpu.VMEM(kept.shape, F32), pltpu.SemaphoreType.DMA((4,))],
        compiler_params=pltpu.CompilerParams(vmem_limit_bytes=VMEM_LIMIT),
        name="finish",
    )(kept, arrived)


def ring_shift(x, axis, distance):
    size = lax.axis_size(axis)
    return lax.ppermute(x, axis, [(i, (i + distance) % size) for i in range(size)])


def passed_along(block, axis, distance):
    devices = range(lax.axis_size(axis))
    route = [(i - distance, i) for i in devices if i - distance in devices]
    return lax.ppermute(block, axis, route)


def others(x):
    return [ring_shift(x, "ma", d) for d in range(1, lax.axis_size("ma"))]


def exchanged(x, axis, shift):
    size = lax.axis_size(axis)
    return lax.ppermute(x, axis, [(i, partner(i, shift, size)) for i in range(size)])


def local(
    patches,
    cls_rows,
    w_query,
    w_key,
    w_value,
    w_out,
    a_query,
    a_key,
    a_value,
    a_out,
    upstream,
    slice_to_scan,
):
    line = ("gz", "dev")
    slices, _, width = patches.shape
    cols = w_query.shape[1]
    chips = lax.axis_size("gz")
    up = upstream[0]
    (
        held, key_held, value_held, out_held, probs, stats, cls_norm, head_terms, factor, pooled
    ) = encoder_forward(patches, cls_rows, w_query, w_key, w_value, w_out)
    d_wide, allowed, turned_value, early = prepare_window(
        slice_to_scan, up, a_out, factor, pooled, slices
    )
    total = head_terms.astype(F32)
    for term in others(head_terms):
        total = total + term.astype(F32)
    embedded = (cls_rows.astype(F32) + total).astype(BF16)
    following = passed_along(embedded, line, -1)
    d_own = window_gradients(embedded, following, a_query, a_key, a_value, d_wide, allowed)
    d_others = jnp.stack(others(d_own))
    lower = d_own[slices:].astype(F32)
    for n in range(d_others.shape[0]):
        lower = lower + d_others[n, slices:].astype(F32)
    carried = passed_along(
        jnp.concatenate([lower.astype(BF16), up[slices:]], axis=0), line, 1
    )
    messages = encoder_backward(
        held, probs, stats, d_own, d_others, carried, embedded, up, key_held, value_held, out_held,
        cls_norm, turned_value, early, chips,
    )
    order = range(chips - 1, 0, -1)
    arrived = list(messages[:1]) + [exchanged(messages[n], "gz", n) for n in order]
    kept, sent = assemble(arrived, slices, cols, width // chips)
    return tuple(finish(kept, ring_shift(sent, "dev", 1)))


def solution(mesh):
    return jax.shard_map(
        local,
        mesh=mesh,
        in_specs=(
            P(("grp", "gz", "dev"), None, None),
            P(("grp", "gz", "dev"), None),
            P(None, "ma"),
            P(None, "ma"),
            P(None, "ma"),
            P("ma", None),
            P(None, "ma"),
            P(None, "ma"),
            P(None, "ma"),
            P("ma", None),
            P(("grp", "gz", "dev"), None, None),
            P("grp"),
        ),
        out_specs=(
            P(("grp", "gz", "dev"), "ma"),
            P(("grp", "gz", "dev"), "ma"),
            P(("grp", "gz", "dev"), "ma"),
            P(("grp", "gz", "dev"), "ma"),
        ),
        check_vma=False,
    )
```

```python
import functools

import jax
import jax.numpy as jnp
from jax import lax
from jax.experimental import pallas as pl
from jax.experimental.pallas import tpu as pltpu
from jax.sharding import PartitionSpec as P

HD = 64
SLOT = 8
LANES = 128
F32 = jnp.float32
BF16 = jnp.bfloat16
CHUNK = 2
VMEM_LIMIT = 16 * 1024 * 1024


def dot(a, b, dims=((1,), (0,))):
    return lax.dot_general(a, b, (dims, ((), ())), preferred_element_type=F32)


BY_COLS = ((1,), (1,))
BY_ROWS = ((0,), (0,))


def normalize(values):
    row_mean = jnp.mean(values, axis=-1, keepdims=True)
    centred = values - row_mean
    variance = jnp.mean(centred * centred, axis=-1, keepdims=True)
    inv_std = lax.rsqrt(variance + 1e-05)
    return centred * inv_std, inv_std


def head_mask(slices, cols):
    shape = (slices * SLOT, cols)
    row = lax.broadcasted_iota(jnp.int32, shape, 0)
    col = lax.broadcasted_iota(jnp.int32, shape, 1)
    return row % SLOT == col // HD


def slot_rows(rows):
    slices, cols = rows.shape
    wide = jnp.broadcast_to(rows.astype(F32)[:, None, :], (slices, SLOT, cols))
    return wide.reshape(slices * SLOT, cols)


def expand(rows):
    wide = slot_rows(rows)
    return jnp.where(head_mask(rows.shape[0], rows.shape[1]), wide, 0.0).astype(BF16)


def collapse(full):
    rows, cols = full.shape
    kept = jnp.where(head_mask(rows // SLOT, cols), full, 0.0)
    return jnp.sum(kept.reshape(rows // SLOT, SLOT, cols), axis=1)


def in_vmem(shape, dtype):
    return pltpu.VMEM(shape, dtype)


def lane_blocks(rows):
    cols = rows.shape[1]
    spare = -cols % LANES
    if spare:
        rows = jnp.concatenate([rows, jnp.zeros((rows.shape[0], spare), rows.dtype)], axis=1)
    return jnp.concatenate(
        [rows[:, b : b + LANES] for b in range(0, cols + spare, LANES)], axis=0
    )


def from_lane_blocks(rows, cols):
    count = rows.shape[0] // pl.cdiv(cols, LANES)
    blocks = [rows[b : b + count] for b in range(0, rows.shape[0], count)]
    return jnp.concatenate(blocks, axis=1)[:, :cols]


def partner(here, shift, chips):
    return here ^ shift if chips & (chips - 1) == 0 else (here + shift) % chips


def forward_kernel(
    chunk,
    patches_hbm,
    w_query_hbm,
    w_key_hbm,
    w_value_hbm,
    w_out_hbm,
    cls_hbm,
    patches,
    w_key,
    w_value,
    w_out,
    probs,
    stats,
    cls_norm,
    head_terms,
    factor,
    pooled,
    cls_rows,
    w_query,
    query_keys,
    sems,
    patch_sems,
):
    slices, tokens, width = patches.shape
    scale = float(HD) ** (-0.5)

    def fetch(source, target, n):
        copy = pltpu.make_async_copy(source, target, sems.at[n])
        copy.start()
        return copy

    get_rows = fetch(cls_hbm, cls_rows, 4)
    get_query = fetch(w_query_hbm, w_query, 0)
    get_key = fetch(w_key_hbm, w_key, 1)
    get_patches = []
    for c in range(slices // chunk):
        part = pl.ds(c * chunk, chunk)
        copy = pltpu.make_async_copy(patches_hbm.at[part], patches.at[part], patch_sems.at[c])
        copy.start()
        get_patches.append(copy)
    get_value = fetch(w_value_hbm, w_value, 2)
    get_out = fetch(w_out_hbm, w_out, 3)

    get_rows.wait()
    rows = normalize(cls_rows[...].astype(F32))[0].astype(BF16)
    cls_norm[...] = rows
    get_query.wait()
    q = dot(rows, w_query[...]).astype(BF16)
    get_key.wait()
    keys = (dot(expand(q), w_key[...], BY_COLS) * scale).astype(BF16).astype(F32)
    key_sums = jnp.sum(keys, axis=-1, keepdims=True)
    place = lax.broadcasted_iota(jnp.int32, (SLOT, width), 0)
    entry = lax.broadcasted_iota(jnp.int32, (SLOT, width), 1)
    picks = jnp.where((place == 0) | ((place == 1) & (entry == 0)), 1.0, 0.0)
    for z in range(slices):
        query_keys[z] = jnp.concatenate(
            [keys[z * SLOT : (z + 1) * SLOT], picks], axis=0
        ).astype(BF16)

    def measure(z):
        x = patches[z]
        raw = dot(query_keys[z], x, BY_COLS)
        wide = x.astype(F32)
        first = wide[:, 0:1]
        squares = None
        for b in range(0, width, LANES):
            off = wide[:, b : b + LANES] - first
            squares = off * off if squares is None else squares + off * off
        total = jnp.sum(squares.T, axis=0, keepdims=True)
        return raw, total

    def attend(z, raw, total):
        mean = raw[SLOT : SLOT + 1] * (1.0 / width)
        off = mean - raw[SLOT + 1 : SLOT + 2]
        inv_std = lax.rsqrt(jnp.maximum(total * (1.0 / width) - off * off, 0.0) + 1e-05)
        stats[z : z + 1] = mean
        stats[slices + z : slices + z + 1] = inv_std
        here = slice(z * SLOT, (z + 1) * SLOT)
        scores = inv_std * (raw[:SLOT] - mean * key_sums[here])
        powers = jnp.exp(scores - jnp.max(scores, axis=-1, keepdims=True))
        p = powers / jnp.sum(powers, axis=-1, keepdims=True)
        probs[z] = p
        weights = (p.astype(BF16).astype(F32) * inv_std).astype(BF16)
        shift = jnp.sum(weights.astype(F32) * mean, axis=-1, keepdims=True)
        factor[here] = dot(weights, patches[z]) - shift

    waiting = []
    for c in range(slices // chunk):
        get_patches[c].wait()
        ready = [(z,) + measure(z) for z in range(c * chunk, (c + 1) * chunk)]
        for item in waiting:
            attend(*item)
        waiting = ready
    for item in waiting:
        attend(*item)

    get_value.wait()
    value_factor = factor[...]
    pool = collapse(dot(value_factor.astype(BF16), w_value[...])).astype(BF16)
    get_out.wait()
    head_terms[...] = dot(pool, w_out[...]).astype(BF16)
    pooled[...] = jnp.concatenate([q.astype(F32), pool.astype(F32)], axis=0)


def encoder_forward(patches, cls_rows, w_query, w_key, w_value, w_out):
    slices, tokens, width = patches.shape
    cols = w_query.shape[1]
    chunk = CHUNK
    far = (patches, w_query, w_key, w_value, w_out, cls_rows)
    hbm = pl.BlockSpec(memory_space=pltpu.HBM)
    vmem = pl.BlockSpec(memory_space=pltpu.VMEM)
    out_shape = [
        in_vmem(patches.shape, BF16),
        in_vmem(w_key.shape, BF16),
        in_vmem(w_value.shape, BF16),
        in_vmem(w_out.shape, BF16),
        in_vmem((slices, SLOT, tokens), F32),
        in_vmem((2 * slices, tokens), F32),
        in_vmem((slices, width), BF16),
        in_vmem((slices, width), BF16),
        in_vmem((slices * SLOT, width), F32),
        in_vmem((2 * slices, cols), F32),
    ]
    return pl.pallas_call(
        functools.partial(forward_kernel, chunk),
        in_specs=[hbm] * len(far),
        out_specs=[vmem] * len(out_shape),
        out_shape=out_shape,
        scratch_shapes=[
            pltpu.VMEM(cls_rows.shape, BF16),
            pltpu.VMEM(w_query.shape, BF16),
            pltpu.VMEM((slices, 2 * SLOT, width), BF16),
            pltpu.SemaphoreType.DMA((5,)),
            pltpu.SemaphoreType.DMA((slices // chunk,)),
        ],
        compiler_params=pltpu.CompilerParams(vmem_limit_bytes=VMEM_LIMIT),
        name="encoder_forward",
    )(*[pltpu.with_memory_space_constraint(a, pltpu.HBM) for a in far])


def head_rows(x, heads):
    rows, cols = x.shape
    wide = (heads * rows, cols)
    mine = (
        lax.broadcasted_iota(jnp.int32, wide, 0) // rows
        == lax.broadcasted_iota(jnp.int32, wide, 1) // HD
    )
    tall = jnp.broadcast_to(x.astype(F32)[None], (heads, rows, cols)).reshape(wide)
    return jnp.where(mine, tall, 0.0).astype(BF16), mine


def prepare_kernel(heads, slices, ids, up, a_out, factor, pooled, d_wide, bias, turned, early):
    value_factor = factor[...]
    turned[...] = jnp.concatenate([jnp.zeros_like(value_factor), value_factor], axis=0).T
    early[...] = lane_blocks(pooled[...]).astype(BF16)
    rows = 2 * slices
    total = ids.shape[0]
    start = (lax.axis_index("gz") * lax.axis_size("dev") + lax.axis_index("dev")) * slices
    d_pooled = dot(up[...], a_out[...], BY_COLS).astype(BF16)
    d_wide[...] = head_rows(d_pooled, heads)[0]
    square = (heads * rows, rows)
    i_of = lax.broadcasted_iota(jnp.int32, square, 0) % rows
    j_of = lax.broadcasted_iota(jnp.int32, square, 1)
    id_i = jnp.full(square, -1, jnp.int32)
    id_j = jnp.full(square, -1, jnp.int32)
    for n in range(rows):
        place = start + n
        scan = jnp.where(place < total, ids[jnp.minimum(place, total - 1)], -1)
        id_i = jnp.where(i_of == n, scan, id_i)
        id_j = jnp.where(j_of == n, scan, id_j)
    allowed = ((id_i == id_j) & (id_j >= 0)) | (i_of == j_of)
    bias[...] = jnp.where(allowed, 1.0, 0.0)


def prepare_window(ids, up, a_out, factor, pooled, slices):
    cols = a_out.shape[0]
    width = a_out.shape[1]
    heads = cols // HD
    rows = 2 * slices
    vmem = pl.BlockSpec(memory_space=pltpu.VMEM)
    return pl.pallas_call(
        functools.partial(prepare_kernel, heads, slices),
        in_specs=[pl.BlockSpec(memory_space=pltpu.SMEM)] + [vmem] * 4,
        out_specs=[vmem] * 4,
        out_shape=[
            in_vmem((heads * rows, cols), BF16),
            in_vmem((heads * rows, rows), F32),
            in_vmem((width, 2 * slices * SLOT), F32),
            in_vmem((2 * slices * pl.cdiv(cols, LANES), LANES), BF16),
        ],
        compiler_params=pltpu.CompilerParams(vmem_limit_bytes=VMEM_LIMIT),
        name="prepare_window",
    )(ids, up, a_out, factor, pooled)


def window_kernel(heads, own, following, a_query, a_key, a_value, d_wide, allowed, d_half):
    scale = float(HD) ** (-0.5)
    window = jnp.concatenate([own[...].astype(F32), following[...].astype(F32)], axis=0)
    rows = window.shape[0]
    cols = a_query.shape[1]
    half = normalize(window)[0].astype(BF16)
    q_wide, mine = head_rows(dot(half, a_query[...]).astype(BF16), heads)
    k = dot(half, a_key[...]).astype(BF16)
    v = dot(half, a_value[...]).astype(BF16)
    scores = jnp.where(allowed[...] > 0.5, dot(q_wide, k, BY_COLS) * scale, -1e30)
    d_probs = dot(d_wide[...], v, BY_COLS)
    powers = jnp.exp(scores - jnp.max(scores, axis=-1, keepdims=True))
    probs = powers / jnp.sum(powers, axis=-1, keepdims=True)
    inner = jnp.sum(probs * d_probs, axis=-1, keepdims=True)
    d_scores = (probs * (d_probs - inner) * scale).astype(BF16)
    d_value = dot(probs.astype(BF16), d_wide[...], BY_ROWS).astype(BF16)
    d_query = jnp.where(mine, dot(d_scores, k), 0.0)
    d_query = jnp.sum(d_query.reshape(heads, rows, cols), axis=0).astype(BF16)
    d_key = dot(d_scores, q_wide, BY_ROWS).astype(BF16)
    terms = (
        dot(d_value, a_value[...], BY_COLS)
        + dot(d_query, a_query[...], BY_COLS)
        + dot(d_key, a_key[...], BY_COLS)
    )
    d_half[...] = terms.astype(BF16)


def window_gradients(own, following, a_query, a_key, a_value, d_wide, allowed):
    slices, width = own.shape
    heads = a_query.shape[1] // HD
    vmem = pl.BlockSpec(memory_space=pltpu.VMEM)
    return pl.pallas_call(
        functools.partial(window_kernel, heads),
        in_specs=[vmem] * 7,
        out_specs=vmem,
        out_shape=in_vmem((2 * slices, width), BF16),
        compiler_params=pltpu.CompilerParams(vmem_limit_bytes=VMEM_LIMIT),
        name="window_gradients",
    )(own, following, a_query, a_key, a_value, d_wide, allowed)


def backward_kernel(
    chips,
    patches,
    probs,
    stats,
    d_own,
    d_others,
    carried,
    embedded,
    up,
    w_key,
    w_value,
    w_out,
    cls_norm,
    turned_value,
    early,
    *rest,
):
    outs, (turned, d_keys, factor) = rest[:chips], rest[chips:]
    scale = float(HD) ** (-0.5)
    slices = embedded.shape[0]

    win_norm, inv_std = normalize(embedded[...].astype(F32))
    d_normed = d_own[:slices].astype(F32) + carried[:slices].astype(F32)
    for n in range(d_others.shape[0]):
        d_normed = d_normed + d_others[n, :slices].astype(F32)
    centred = (
        d_normed
        - jnp.mean(d_normed, axis=-1, keepdims=True)
        - win_norm * jnp.mean(d_normed * win_norm, axis=-1, keepdims=True)
    )
    d_embed = up[:slices].astype(F32) + carried[slices:].astype(F32) + inv_std * centred
    d_embed = d_embed.astype(BF16)
    d_att = dot(d_embed, w_out[...], BY_COLS).astype(BF16)
    keys = dot(expand(d_att), w_value[...], BY_COLS).astype(BF16).astype(F32)
    key_sums = jnp.sum(keys, axis=-1, keepdims=True)
    d_keys[...] = keys

    def score(z):
        return dot(d_keys[z * SLOT : (z + 1) * SLOT].astype(BF16), patches[z], BY_COLS)

    def attend(z, raw):
        here = slice(z * SLOT, (z + 1) * SLOT)
        p = probs[z]
        mean = stats[z : z + 1]
        inv = stats[slices + z : slices + z + 1]
        d_probs = inv * (raw - mean * key_sums[here])
        inner = jnp.sum(p * d_probs, axis=-1, keepdims=True)
        d_scores = (p * (d_probs - inner) * scale).astype(BF16)
        weights = (d_scores.astype(F32) * inv).astype(BF16)
        shift = jnp.sum(weights.astype(F32) * mean, axis=-1, keepdims=True)
        factor[here] = dot(weights, patches[z]) - shift

    waiting = []
    for c in range(0, slices, CHUNK):
        ready = [(z, score(z)) for z in range(c, c + CHUNK)]
        for item in waiting:
            attend(*item)
        waiting = ready
    for item in waiting:
        attend(*item)

    key_factor = factor[...]
    d_query = collapse(dot(key_factor.astype(BF16), w_key[...])).astype(BF16)
    slot = lax.broadcasted_iota(jnp.int32, key_factor.shape, 0) % SLOT
    left = jnp.where(slot == SLOT - 2, slot_rows(cls_norm[...]), key_factor)
    left = jnp.where(slot == SLOT - 1, slot_rows(d_embed), left)
    right = jnp.concatenate([d_att.astype(F32), d_query.astype(F32)], axis=0)
    turned[...] = jnp.concatenate([left, jnp.zeros_like(left)], axis=0).T + turned_value[...]
    late = lane_blocks(right).astype(BF16)
    part = turned.shape[0] // chips
    middle = part + late.shape[0]
    here = lax.axis_index("gz")
    for shift in range(chips):
        first = pl.multiple_of(partner(here, shift, chips) * part, SLOT)
        outs[shift][:part] = turned[pl.ds(first, part), :].astype(BF16)
        outs[shift][part:middle] = late
        outs[shift][middle:] = early[...]


def encoder_backward(
    patches, probs, stats, d_own, d_others, carried, embedded, up, w_key, w_value, w_out, cls_norm,
    turned_value, early, chips,
):
    slices, tokens, width = patches.shape
    cols = w_key.shape[1]
    vmem = pl.BlockSpec(memory_space=pltpu.VMEM)
    message = (width // chips + 4 * slices * pl.cdiv(cols, LANES), LANES)
    return pl.pallas_call(
        functools.partial(backward_kernel, chips),
        in_specs=[vmem] * 14,
        out_specs=[vmem] * chips,
        out_shape=[in_vmem(message, BF16)] * chips,
        scratch_shapes=[
            pltpu.VMEM((width, LANES), F32),
            pltpu.VMEM((slices * SLOT, width), F32),
            pltpu.VMEM((slices * SLOT, width), F32),
        ],
        compiler_params=pltpu.CompilerParams(vmem_limit_bytes=VMEM_LIMIT),
        name="encoder_backward",
    )(
        patches, probs, stats, d_own, d_others, carried, embedded, up, w_key, w_value, w_out, cls_norm,
        turned_value, early,
    )


def assemble_kernel(slices, cols, part, chips, *refs):
    messages, (kept, sent) = refs[:chips], refs[chips:]
    mask = head_mask(slices, cols)
    slot = lax.broadcasted_iota(jnp.int32, mask.shape, 0) % SLOT
    depth = slices * SLOT
    rows = 2 * slices * pl.cdiv(cols, LANES)

    def stacked(columns):
        blocks = [m[:part, columns].astype(F32) for m in messages]
        return jnp.concatenate(blocks, axis=1).astype(BF16)

    first, second = [], []
    for m in messages:
        for start, into in ((part, second), (part + rows, first)):
            block = from_lane_blocks(m[start : start + rows].astype(F32), cols)
            into.append([slot_rows(block[:slices]), slot_rows(block[slices:])])
    left_key, left_value = stacked(slice(0, depth)), stacked(slice(depth, 2 * depth))

    def right(blocks):
        return jnp.concatenate(blocks, axis=0).astype(BF16)

    grads = [
        dot(left_key, right([jnp.where(slot == SLOT - 2, b[1], 0.0) for b in second])),
        dot(left_key, right([jnp.where(mask, b[0], 0.0) for b in first])),
        dot(left_value, right([jnp.where(mask, b[0], 0.0) for b in second])),
        dot(left_key, right([jnp.where(slot == SLOT - 1, b[1], 0.0) for b in first])),
    ]
    lower = lax.axis_index("dev") == 0
    half = part // 2
    for n, total in enumerate(grads):
        top, bottom = total[:half], total[half:]
        kept[n] = jnp.where(lower, top, bottom)
        sent[n] = jnp.where(lower, bottom, top).astype(BF16)


def assemble(messages, slices, cols, part):
    vmem = pl.BlockSpec(memory_space=pltpu.VMEM)
    shape = (4, part // 2, cols)
    return pl.pallas_call(
        functools.partial(assemble_kernel, slices, cols, part, len(messages)),
        in_specs=[vmem] * len(messages),
        out_specs=[vmem, vmem],
        out_shape=[in_vmem(shape, F32), in_vmem(shape, BF16)],
        compiler_params=pltpu.CompilerParams(vmem_limit_bytes=VMEM_LIMIT),
        name="assemble",
    )(*messages)


def finish_kernel(kept, arrived, *refs):
    outs, sums, sems = refs[:4], refs[4], refs[5]
    copies = []
    for n, out in enumerate(outs):
        sums[n] = kept[n] + arrived[n].astype(F32)
        copy = pltpu.make_async_copy(sums.at[n], out, sems.at[n])
        copy.start()
        copies.append(copy)
    for copy in copies:
        copy.wait()


def finish(kept, arrived):
    vmem = pl.BlockSpec(memory_space=pltpu.VMEM)
    return pl.pallas_call(
        finish_kernel,
        in_specs=[vmem, vmem],
        out_specs=[pl.BlockSpec(memory_space=pltpu.HBM)] * 4,
        out_shape=[pltpu.HBM(kept.shape[1:], F32)] * 4,
        scratch_shapes=[pltpu.VMEM(kept.shape, F32), pltpu.SemaphoreType.DMA((4,))],
        compiler_params=pltpu.CompilerParams(vmem_limit_bytes=VMEM_LIMIT),
        name="finish",
    )(kept, arrived)


def ring_shift(x, axis, distance):
    size = lax.axis_size(axis)
    return lax.ppermute(x, axis, [(i, (i + distance) % size) for i in range(size)])


def others(x):
    return [ring_shift(x, "ma", d) for d in range(1, lax.axis_size("ma"))]


def pair_route():
    chips, parts, cores = [lax.axis_size(a) for a in ("gz", "ma", "dev")]
    route = []
    for chip in range(chips):
        for part in range(parts):
            for core in range(cores):
                place = chip * cores + core
                other = place + 1 if core else place - 1
                at = part
                if not 0 <= other < chips * cores:
                    other, at = place, part ^ 1
                    if at >= parts:
                        continue
                source = (chip * parts + part) * cores + core
                route.append((source, (other // cores * parts + at) * cores + other % cores))
    return route


def neighbour(block, upward):
    within = ring_shift(block, "dev", 1)
    across = lax.ppermute(block, ("gz", "ma", "dev"), pair_route())
    chip, core = lax.axis_index("gz"), lax.axis_index("dev")
    edge = 0 if upward else lax.axis_size("gz") - 1
    inside = core == (1 if upward else 0)
    return jnp.where(inside, within, jnp.where(chip == edge, jnp.zeros_like(across), across))


def exchanged(x, axis, shift):
    size = lax.axis_size(axis)
    return lax.ppermute(x, axis, [(i, partner(i, shift, size)) for i in range(size)])


def local(
    patches,
    cls_rows,
    w_query,
    w_key,
    w_value,
    w_out,
    a_query,
    a_key,
    a_value,
    a_out,
    upstream,
    slice_to_scan,
):
    slices, _, width = patches.shape
    cols = w_query.shape[1]
    chips = lax.axis_size("gz")
    up = upstream[0]
    (
        held, key_held, value_held, out_held, probs, stats, cls_norm, head_terms, factor, pooled
    ) = encoder_forward(patches, cls_rows, w_query, w_key, w_value, w_out)
    d_wide, allowed, turned_value, early = prepare_window(
        slice_to_scan, up, a_out, factor, pooled, slices
    )
    total = head_terms.astype(F32)
    for term in others(head_terms):
        total = total + term.astype(F32)
    embedded = (cls_rows.astype(F32) + total).astype(BF16)
    following = neighbour(embedded, False)
    d_own = window_gradients(embedded, following, a_query, a_key, a_value, d_wide, allowed)
    d_others = jnp.stack(others(d_own))
    lower = d_own[slices:].astype(F32)
    for n in range(d_others.shape[0]):
        lower = lower + d_others[n, slices:].astype(F32)
    carried = neighbour(jnp.concatenate([lower.astype(BF16), up[slices:]], axis=0), True)
    messages = encoder_backward(
        held, probs, stats, d_own, d_others, carried, embedded, up, key_held, value_held, out_held,
        cls_norm, turned_value, early, chips,
    )
    order = range(chips - 1, 0, -1)
    arrived = list(messages[:1]) + [exchanged(messages[n], "gz", n) for n in order]
    kept, sent = assemble(arrived, slices, cols, width // chips)
    return tuple(finish(kept, ring_shift(sent, "dev", 1)))


def solution(mesh):
    return jax.shard_map(
        local,
        mesh=mesh,
        in_specs=(
            P(("grp", "gz", "dev"), None, None),
            P(("grp", "gz", "dev"), None),
            P(None, "ma"),
            P(None, "ma"),
            P(None, "ma"),
            P("ma", None),
            P(None, "ma"),
            P(None, "ma"),
            P(None, "ma"),
            P("ma", None),
            P(("grp", "gz", "dev"), None, None),
            P("grp"),
        ),
        out_specs=(
            P(("grp", "gz", "dev"), "ma"),
            P(("grp", "gz", "dev"), "ma"),
            P(("grp", "gz", "dev"), "ma"),
            P(("grp", "gz", "dev"), "ma"),
        ),
        check_vma=False,
    )
```

```python
import functools

import jax
import jax.numpy as jnp
from jax import lax
from jax.experimental import pallas as pl
from jax.experimental.pallas import tpu as pltpu
from jax.sharding import PartitionSpec as P

HD = 64
SLOT = 8
LANES = 128
F32 = jnp.float32
BF16 = jnp.bfloat16
CHUNK = 2
VMEM_LIMIT = 16 * 1024 * 1024


def dot(a, b, dims=((1,), (0,))):
    return lax.dot_general(a, b, (dims, ((), ())), preferred_element_type=F32)


BY_COLS = ((1,), (1,))
BY_ROWS = ((0,), (0,))


def normalize(values):
    row_mean = jnp.mean(values, axis=-1, keepdims=True)
    centred = values - row_mean
    variance = jnp.mean(centred * centred, axis=-1, keepdims=True)
    inv_std = lax.rsqrt(variance + 1e-05)
    return centred * inv_std, inv_std


def head_mask(slices, cols):
    shape = (slices * SLOT, cols)
    row = lax.broadcasted_iota(jnp.int32, shape, 0)
    col = lax.broadcasted_iota(jnp.int32, shape, 1)
    return row % SLOT == col // HD


def slot_rows(rows):
    slices, cols = rows.shape
    wide = jnp.broadcast_to(rows.astype(F32)[:, None, :], (slices, SLOT, cols))
    return wide.reshape(slices * SLOT, cols)


def expand(rows):
    wide = slot_rows(rows)
    return jnp.where(head_mask(rows.shape[0], rows.shape[1]), wide, 0.0).astype(BF16)


def collapse(full):
    rows, cols = full.shape
    kept = jnp.where(head_mask(rows // SLOT, cols), full, 0.0)
    return jnp.sum(kept.reshape(rows // SLOT, SLOT, cols), axis=1)


def in_vmem(shape, dtype):
    return pltpu.VMEM(shape, dtype)


def lane_blocks(rows):
    cols = rows.shape[1]
    spare = -cols % LANES
    if spare:
        rows = jnp.concatenate([rows, jnp.zeros((rows.shape[0], spare), rows.dtype)], axis=1)
    return jnp.concatenate(
        [rows[:, b : b + LANES] for b in range(0, cols + spare, LANES)], axis=0
    )


def from_lane_blocks(rows, cols):
    count = rows.shape[0] // pl.cdiv(cols, LANES)
    blocks = [rows[b : b + count] for b in range(0, rows.shape[0], count)]
    return jnp.concatenate(blocks, axis=1)[:, :cols]


def partner(here, shift, chips):
    return here ^ shift if chips & (chips - 1) == 0 else (here + shift) % chips


def forward_kernel(
    chunk,
    patches_hbm,
    w_query_hbm,
    w_key_hbm,
    w_value_hbm,
    w_out_hbm,
    cls_hbm,
    patches,
    w_key,
    w_value,
    w_out,
    probs,
    stats,
    cls_norm,
    head_terms,
    factor,
    pooled,
    cls_rows,
    w_query,
    query_keys,
    sems,
    patch_sems,
):
    slices, tokens, width = patches.shape
    scale = float(HD) ** (-0.5)

    def fetch(source, target, n):
        copy = pltpu.make_async_copy(source, target, sems.at[n])
        copy.start()
        return copy

    get_rows = fetch(cls_hbm, cls_rows, 4)
    get_query = fetch(w_query_hbm, w_query, 0)
    get_key = fetch(w_key_hbm, w_key, 1)
    get_patches = []
    for c in range(slices // chunk):
        part = pl.ds(c * chunk, chunk)
        copy = pltpu.make_async_copy(patches_hbm.at[part], patches.at[part], patch_sems.at[c])
        copy.start()
        get_patches.append(copy)
    get_value = fetch(w_value_hbm, w_value, 2)
    get_out = fetch(w_out_hbm, w_out, 3)

    get_rows.wait()
    rows = normalize(cls_rows[...].astype(F32))[0].astype(BF16)
    cls_norm[...] = rows
    get_query.wait()
    q = dot(rows, w_query[...]).astype(BF16)
    get_key.wait()
    keys = (dot(expand(q), w_key[...], BY_COLS) * scale).astype(BF16).astype(F32)
    key_sums = jnp.sum(keys, axis=-1, keepdims=True)
    place = lax.broadcasted_iota(jnp.int32, (SLOT, width), 0)
    entry = lax.broadcasted_iota(jnp.int32, (SLOT, width), 1)
    picks = jnp.where((place == 0) | ((place == 1) & (entry == 0)), 1.0, 0.0)
    for z in range(slices):
        query_keys[z] = jnp.concatenate(
            [keys[z * SLOT : (z + 1) * SLOT], picks], axis=0
        ).astype(BF16)

    def measure(z):
        x = patches[z]
        raw = dot(query_keys[z], x, BY_COLS)
        wide = x.astype(F32)
        first = wide[:, 0:1]
        squares = None
        for b in range(0, width, LANES):
            off = wide[:, b : b + LANES] - first
            squares = off * off if squares is None else squares + off * off
        total = jnp.sum(squares.T, axis=0, keepdims=True)
        return raw, total

    def attend(z, raw, total):
        mean = raw[SLOT : SLOT + 1] * (1.0 / width)
        off = mean - raw[SLOT + 1 : SLOT + 2]
        inv_std = lax.rsqrt(jnp.maximum(total * (1.0 / width) - off * off, 0.0) + 1e-05)
        stats[z : z + 1] = mean
        stats[slices + z : slices + z + 1] = inv_std
        here = slice(z * SLOT, (z + 1) * SLOT)
        scores = inv_std * (raw[:SLOT] - mean * key_sums[here])
        powers = jnp.exp(scores - jnp.max(scores, axis=-1, keepdims=True))
        p = powers / jnp.sum(powers, axis=-1, keepdims=True)
        probs[z] = p
        weights = (p.astype(BF16).astype(F32) * inv_std).astype(BF16)
        shift = jnp.sum(weights.astype(F32) * mean, axis=-1, keepdims=True)
        factor[here] = dot(weights, patches[z]) - shift

    waiting = []
    for c in range(slices // chunk):
        get_patches[c].wait()
        ready = [(z,) + measure(z) for z in range(c * chunk, (c + 1) * chunk)]
        for item in waiting:
            attend(*item)
        waiting = ready
    for item in waiting:
        attend(*item)

    get_value.wait()
    value_factor = factor[...]
    pool = collapse(dot(value_factor.astype(BF16), w_value[...])).astype(BF16)
    get_out.wait()
    head_terms[...] = dot(pool, w_out[...]).astype(BF16)
    pooled[...] = jnp.concatenate([q.astype(F32), pool.astype(F32)], axis=0)


def encoder_forward(patches, cls_rows, w_query, w_key, w_value, w_out):
    slices, tokens, width = patches.shape
    cols = w_query.shape[1]
    chunk = CHUNK
    far = (patches, w_query, w_key, w_value, w_out, cls_rows)
    hbm = pl.BlockSpec(memory_space=pltpu.HBM)
    vmem = pl.BlockSpec(memory_space=pltpu.VMEM)
    out_shape = [
        in_vmem(patches.shape, BF16),
        in_vmem(w_key.shape, BF16),
        in_vmem(w_value.shape, BF16),
        in_vmem(w_out.shape, BF16),
        in_vmem((slices, SLOT, tokens), F32),
        in_vmem((2 * slices, tokens), F32),
        in_vmem((slices, width), BF16),
        in_vmem((slices, width), BF16),
        in_vmem((slices * SLOT, width), F32),
        in_vmem((2 * slices, cols), F32),
    ]
    return pl.pallas_call(
        functools.partial(forward_kernel, chunk),
        in_specs=[hbm] * len(far),
        out_specs=[vmem] * len(out_shape),
        out_shape=out_shape,
        scratch_shapes=[
            pltpu.VMEM(cls_rows.shape, BF16),
            pltpu.VMEM(w_query.shape, BF16),
            pltpu.VMEM((slices, 2 * SLOT, width), BF16),
            pltpu.SemaphoreType.DMA((5,)),
            pltpu.SemaphoreType.DMA((slices // chunk,)),
        ],
        compiler_params=pltpu.CompilerParams(vmem_limit_bytes=VMEM_LIMIT),
        name="encoder_forward",
    )(*[pltpu.with_memory_space_constraint(a, pltpu.HBM) for a in far])


def head_rows(x, heads):
    rows, cols = x.shape
    wide = (heads * rows, cols)
    mine = (
        lax.broadcasted_iota(jnp.int32, wide, 0) // rows
        == lax.broadcasted_iota(jnp.int32, wide, 1) // HD
    )
    tall = jnp.broadcast_to(x.astype(F32)[None], (heads, rows, cols)).reshape(wide)
    return jnp.where(mine, tall, 0.0).astype(BF16), mine


def prepare_kernel(heads, slices, ids, up, a_out, factor, pooled, d_wide, bias, turned, early):
    value_factor = factor[...]
    turned[...] = jnp.concatenate([jnp.zeros_like(value_factor), value_factor], axis=0).T
    early[...] = lane_blocks(pooled[...]).astype(BF16)
    rows = 2 * slices
    total = ids.shape[0]
    start = (lax.axis_index("gz") * lax.axis_size("dev") + lax.axis_index("dev")) * slices
    d_pooled = dot(up[...], a_out[...], BY_COLS).astype(BF16)
    d_wide[...] = head_rows(d_pooled, heads)[0]
    square = (heads * rows, rows)
    i_of = lax.broadcasted_iota(jnp.int32, square, 0) % rows
    j_of = lax.broadcasted_iota(jnp.int32, square, 1)
    id_i = jnp.full(square, -1, jnp.int32)
    id_j = jnp.full(square, -1, jnp.int32)
    for n in range(rows):
        place = start + n
        scan = jnp.where(place < total, ids[jnp.minimum(place, total - 1)], -1)
        id_i = jnp.where(i_of == n, scan, id_i)
        id_j = jnp.where(j_of == n, scan, id_j)
    allowed = ((id_i == id_j) & (id_j >= 0)) | (i_of == j_of)
    bias[...] = jnp.where(allowed, 1.0, 0.0)


def prepare_window(ids, up, a_out, factor, pooled, slices):
    cols = a_out.shape[0]
    width = a_out.shape[1]
    heads = cols // HD
    rows = 2 * slices
    vmem = pl.BlockSpec(memory_space=pltpu.VMEM)
    return pl.pallas_call(
        functools.partial(prepare_kernel, heads, slices),
        in_specs=[pl.BlockSpec(memory_space=pltpu.SMEM)] + [vmem] * 4,
        out_specs=[vmem] * 4,
        out_shape=[
            in_vmem((heads * rows, cols), BF16),
            in_vmem((heads * rows, rows), F32),
            in_vmem((width, 2 * slices * SLOT), F32),
            in_vmem((2 * slices * pl.cdiv(cols, LANES), LANES), BF16),
        ],
        compiler_params=pltpu.CompilerParams(vmem_limit_bytes=VMEM_LIMIT),
        name="prepare_window",
    )(ids, up, a_out, factor, pooled)


def choose(within, across, inside, edge):
    across = jnp.where(edge, 0.0, across.astype(F32))
    return jnp.where(inside, within.astype(F32), across)


def window_kernel(heads, own, within, across, a_query, a_key, a_value, d_wide, allowed, d_half):
    scale = float(HD) ** (-0.5)
    last = lax.axis_index("gz") == lax.axis_size("gz") - 1
    following = choose(within[...], across[...], lax.axis_index("dev") == 0, last)
    window = jnp.concatenate([own[...].astype(F32), following], axis=0)
    rows = window.shape[0]
    cols = a_query.shape[1]
    half = normalize(window)[0].astype(BF16)
    q_wide, mine = head_rows(dot(half, a_query[...]).astype(BF16), heads)
    k = dot(half, a_key[...]).astype(BF16)
    v = dot(half, a_value[...]).astype(BF16)
    scores = jnp.where(allowed[...] > 0.5, dot(q_wide, k, BY_COLS) * scale, -1e30)
    d_probs = dot(d_wide[...], v, BY_COLS)
    powers = jnp.exp(scores - jnp.max(scores, axis=-1, keepdims=True))
    probs = powers / jnp.sum(powers, axis=-1, keepdims=True)
    inner = jnp.sum(probs * d_probs, axis=-1, keepdims=True)
    d_scores = (probs * (d_probs - inner) * scale).astype(BF16)
    d_value = dot(probs.astype(BF16), d_wide[...], BY_ROWS).astype(BF16)
    d_query = jnp.where(mine, dot(d_scores, k), 0.0)
    d_query = jnp.sum(d_query.reshape(heads, rows, cols), axis=0).astype(BF16)
    d_key = dot(d_scores, q_wide, BY_ROWS).astype(BF16)
    terms = (
        dot(d_value, a_value[...], BY_COLS)
        + dot(d_query, a_query[...], BY_COLS)
        + dot(d_key, a_key[...], BY_COLS)
    )
    d_half[...] = terms.astype(BF16)


def window_gradients(own, within, across, a_query, a_key, a_value, d_wide, allowed):
    slices, width = own.shape
    heads = a_query.shape[1] // HD
    vmem = pl.BlockSpec(memory_space=pltpu.VMEM)
    return pl.pallas_call(
        functools.partial(window_kernel, heads),
        in_specs=[vmem] * 8,
        out_specs=vmem,
        out_shape=in_vmem((2 * slices, width), BF16),
        compiler_params=pltpu.CompilerParams(vmem_limit_bytes=VMEM_LIMIT),
        name="window_gradients",
    )(own, within, across, a_query, a_key, a_value, d_wide, allowed)


def backward_kernel(
    chips,
    patches,
    probs,
    stats,
    d_own,
    d_others,
    within,
    across,
    embedded,
    up,
    w_key,
    w_value,
    w_out,
    cls_norm,
    turned_value,
    early,
    *rest,
):
    outs, (turned, d_keys, factor) = rest[:chips], rest[chips:]
    scale = float(HD) ** (-0.5)
    slices = embedded.shape[0]

    carried = choose(
        within[...], across[...], lax.axis_index("dev") == 1, lax.axis_index("gz") == 0
    )
    win_norm, inv_std = normalize(embedded[...].astype(F32))
    d_normed = d_own[:slices].astype(F32) + carried[:slices]
    for n in range(d_others.shape[0]):
        d_normed = d_normed + d_others[n, :slices].astype(F32)
    centred = (
        d_normed
        - jnp.mean(d_normed, axis=-1, keepdims=True)
        - win_norm * jnp.mean(d_normed * win_norm, axis=-1, keepdims=True)
    )
    d_embed = up[:slices].astype(F32) + carried[slices:] + inv_std * centred
    d_embed = d_embed.astype(BF16)
    d_att = dot(d_embed, w_out[...], BY_COLS).astype(BF16)
    keys = dot(expand(d_att), w_value[...], BY_COLS).astype(BF16).astype(F32)
    key_sums = jnp.sum(keys, axis=-1, keepdims=True)
    d_keys[...] = keys

    def score(z):
        return dot(d_keys[z * SLOT : (z + 1) * SLOT].astype(BF16), patches[z], BY_COLS)

    def attend(z, raw):
        here = slice(z * SLOT, (z + 1) * SLOT)
        p = probs[z]
        mean = stats[z : z + 1]
        inv = stats[slices + z : slices + z + 1]
        d_probs = inv * (raw - mean * key_sums[here])
        inner = jnp.sum(p * d_probs, axis=-1, keepdims=True)
        d_scores = (p * (d_probs - inner) * scale).astype(BF16)
        weights = (d_scores.astype(F32) * inv).astype(BF16)
        shift = jnp.sum(weights.astype(F32) * mean, axis=-1, keepdims=True)
        factor[here] = dot(weights, patches[z]) - shift

    waiting = []
    for c in range(0, slices, CHUNK):
        ready = [(z, score(z)) for z in range(c, c + CHUNK)]
        for item in waiting:
            attend(*item)
        waiting = ready
    for item in waiting:
        attend(*item)

    key_factor = factor[...]
    d_query = collapse(dot(key_factor.astype(BF16), w_key[...])).astype(BF16)
    slot = lax.broadcasted_iota(jnp.int32, key_factor.shape, 0) % SLOT
    left = jnp.where(slot == SLOT - 2, slot_rows(cls_norm[...]), key_factor)
    left = jnp.where(slot == SLOT - 1, slot_rows(d_embed), left)
    right = jnp.concatenate([d_att.astype(F32), d_query.astype(F32)], axis=0)
    turned[...] = jnp.concatenate([left, jnp.zeros_like(left)], axis=0).T + turned_value[...]
    late = lane_blocks(right).astype(BF16)
    part = turned.shape[0] // chips
    middle = part + late.shape[0]
    here = lax.axis_index("gz")
    for shift in range(chips):
        first = pl.multiple_of(partner(here, shift, chips) * part, SLOT)
        outs[shift][:part] = turned[pl.ds(first, part), :].astype(BF16)
        outs[shift][part:middle] = late
        outs[shift][middle:] = early[...]


def encoder_backward(
    patches, probs, stats, d_own, d_others, within, across, embedded, up, w_key, w_value, w_out,
    cls_norm, turned_value, early, chips,
):
    slices, tokens, width = patches.shape
    cols = w_key.shape[1]
    vmem = pl.BlockSpec(memory_space=pltpu.VMEM)
    message = (width // chips + 4 * slices * pl.cdiv(cols, LANES), LANES)
    return pl.pallas_call(
        functools.partial(backward_kernel, chips),
        in_specs=[vmem] * 15,
        out_specs=[vmem] * chips,
        out_shape=[in_vmem(message, BF16)] * chips,
        scratch_shapes=[
            pltpu.VMEM((width, LANES), F32),
            pltpu.VMEM((slices * SLOT, width), F32),
            pltpu.VMEM((slices * SLOT, width), F32),
        ],
        compiler_params=pltpu.CompilerParams(vmem_limit_bytes=VMEM_LIMIT),
        name="encoder_backward",
    )(
        patches, probs, stats, d_own, d_others, within, across, embedded, up, w_key, w_value, w_out,
        cls_norm, turned_value, early,
    )


def assemble_kernel(slices, cols, part, chips, *refs):
    messages, (kept, sent) = refs[:chips], refs[chips:]
    mask = head_mask(slices, cols)
    slot = lax.broadcasted_iota(jnp.int32, mask.shape, 0) % SLOT
    depth = slices * SLOT
    rows = 2 * slices * pl.cdiv(cols, LANES)

    def stacked(columns):
        blocks = [m[:part, columns].astype(F32) for m in messages]
        return jnp.concatenate(blocks, axis=1).astype(BF16)

    first, second = [], []
    for m in messages:
        for start, into in ((part, second), (part + rows, first)):
            block = from_lane_blocks(m[start : start + rows].astype(F32), cols)
            into.append([slot_rows(block[:slices]), slot_rows(block[slices:])])
    left_key, left_value = stacked(slice(0, depth)), stacked(slice(depth, 2 * depth))

    def right(blocks):
        return jnp.concatenate(blocks, axis=0).astype(BF16)

    grads = [
        dot(left_key, right([jnp.where(slot == SLOT - 2, b[1], 0.0) for b in second])),
        dot(left_key, right([jnp.where(mask, b[0], 0.0) for b in first])),
        dot(left_value, right([jnp.where(mask, b[0], 0.0) for b in second])),
        dot(left_key, right([jnp.where(slot == SLOT - 1, b[1], 0.0) for b in first])),
    ]
    lower = lax.axis_index("dev") == 0
    half = part // 2
    for n, total in enumerate(grads):
        top, bottom = total[:half], total[half:]
        kept[n] = jnp.where(lower, top, bottom)
        sent[n] = jnp.where(lower, bottom, top).astype(BF16)


def assemble(messages, slices, cols, part):
    vmem = pl.BlockSpec(memory_space=pltpu.VMEM)
    shape = (4, part // 2, cols)
    return pl.pallas_call(
        functools.partial(assemble_kernel, slices, cols, part, len(messages)),
        in_specs=[vmem] * len(messages),
        out_specs=[vmem, vmem],
        out_shape=[in_vmem(shape, F32), in_vmem(shape, BF16)],
        compiler_params=pltpu.CompilerParams(vmem_limit_bytes=VMEM_LIMIT),
        name="assemble",
    )(*messages)


def finish_kernel(kept, arrived, *refs):
    outs, sums, sems = refs[:4], refs[4], refs[5]
    copies = []
    for n, out in enumerate(outs):
        sums[n] = kept[n] + arrived[n].astype(F32)
        copy = pltpu.make_async_copy(sums.at[n], out, sems.at[n])
        copy.start()
        copies.append(copy)
    for copy in copies:
        copy.wait()


def finish(kept, arrived):
    vmem = pl.BlockSpec(memory_space=pltpu.VMEM)
    return pl.pallas_call(
        finish_kernel,
        in_specs=[vmem, vmem],
        out_specs=[pl.BlockSpec(memory_space=pltpu.HBM)] * 4,
        out_shape=[pltpu.HBM(kept.shape[1:], F32)] * 4,
        scratch_shapes=[pltpu.VMEM(kept.shape, F32), pltpu.SemaphoreType.DMA((4,))],
        compiler_params=pltpu.CompilerParams(vmem_limit_bytes=VMEM_LIMIT),
        name="finish",
    )(kept, arrived)


def ring_shift(x, axis, distance):
    size = lax.axis_size(axis)
    return lax.ppermute(x, axis, [(i, (i + distance) % size) for i in range(size)])


def others(x):
    return [ring_shift(x, "ma", d) for d in range(1, lax.axis_size("ma"))]


def pair_route():
    chips, parts, cores = [lax.axis_size(a) for a in ("gz", "ma", "dev")]
    route = []
    for chip in range(chips):
        for part in range(parts):
            for core in range(cores):
                place = chip * cores + core
                other = place + 1 if core else place - 1
                at = part
                if not 0 <= other < chips * cores:
                    other, at = place, part ^ 1
                    if at >= parts:
                        continue
                source = (chip * parts + part) * cores + core
                route.append((source, (other // cores * parts + at) * cores + other % cores))
    return route


def neighbours(block):
    within = ring_shift(block, "dev", 1)
    return within, lax.ppermute(block, ("gz", "ma", "dev"), pair_route())


def exchanged(x, axis, shift):
    size = lax.axis_size(axis)
    return lax.ppermute(x, axis, [(i, partner(i, shift, size)) for i in range(size)])


def local(
    patches,
    cls_rows,
    w_query,
    w_key,
    w_value,
    w_out,
    a_query,
    a_key,
    a_value,
    a_out,
    upstream,
    slice_to_scan,
):
    slices, _, width = patches.shape
    cols = w_query.shape[1]
    chips = lax.axis_size("gz")
    up = upstream[0]
    (
        held, key_held, value_held, out_held, probs, stats, cls_norm, head_terms, factor, pooled
    ) = encoder_forward(patches, cls_rows, w_query, w_key, w_value, w_out)
    d_wide, allowed, turned_value, early = prepare_window(
        slice_to_scan, up, a_out, factor, pooled, slices
    )
    total = head_terms.astype(F32)
    for term in others(head_terms):
        total = total + term.astype(F32)
    embedded = (cls_rows.astype(F32) + total).astype(BF16)
    following = neighbours(embedded)
    d_own = window_gradients(embedded, *following, a_query, a_key, a_value, d_wide, allowed)
    d_others = jnp.stack(others(d_own))
    lower = d_own[slices:].astype(F32)
    for n in range(d_others.shape[0]):
        lower = lower + d_others[n, slices:].astype(F32)
    carried = neighbours(jnp.concatenate([lower.astype(BF16), up[slices:]], axis=0))
    messages = encoder_backward(
        held, probs, stats, d_own, d_others, *carried, embedded, up, key_held, value_held, out_held,
        cls_norm, turned_value, early, chips,
    )
    order = range(chips - 1, 0, -1)
    arrived = list(messages[:1]) + [exchanged(messages[n], "gz", n) for n in order]
    kept, sent = assemble(arrived, slices, cols, width // chips)
    return tuple(finish(kept, ring_shift(sent, "dev", 1)))


def solution(mesh):
    return jax.shard_map(
        local,
        mesh=mesh,
        in_specs=(
            P(("grp", "gz", "dev"), None, None),
            P(("grp", "gz", "dev"), None),
            P(None, "ma"),
            P(None, "ma"),
            P(None, "ma"),
            P("ma", None),
            P(None, "ma"),
            P(None, "ma"),
            P(None, "ma"),
            P("ma", None),
            P(("grp", "gz", "dev"), None, None),
            P("grp"),
        ),
        out_specs=(
            P(("grp", "gz", "dev"), "ma"),
            P(("grp", "gz", "dev"), "ma"),
            P(("grp", "gz", "dev"), "ma"),
            P(("grp", "gz", "dev"), "ma"),
        ),
        check_vma=False,
    )
```

```python
import functools

import jax
import jax.numpy as jnp
from jax import lax
from jax.experimental import pallas as pl
from jax.experimental.pallas import tpu as pltpu
from jax.sharding import PartitionSpec as P

HD = 64
SLOT = 8
LANES = 128
F32 = jnp.float32
BF16 = jnp.bfloat16
CHUNK = 2
VMEM_LIMIT = 16 * 1024 * 1024


def dot(a, b, dims=((1,), (0,))):
    return lax.dot_general(a, b, (dims, ((), ())), preferred_element_type=F32)


BY_COLS = ((1,), (1,))
BY_ROWS = ((0,), (0,))


def normalize(values):
    row_mean = jnp.mean(values, axis=-1, keepdims=True)
    centred = values - row_mean
    variance = jnp.mean(centred * centred, axis=-1, keepdims=True)
    inv_std = lax.rsqrt(variance + 1e-05)
    return centred * inv_std, inv_std


def head_mask(slices, cols):
    shape = (slices * SLOT, cols)
    row = lax.broadcasted_iota(jnp.int32, shape, 0)
    col = lax.broadcasted_iota(jnp.int32, shape, 1)
    return row % SLOT == col // HD


def slot_rows(rows):
    slices, cols = rows.shape
    wide = jnp.broadcast_to(rows.astype(F32)[:, None, :], (slices, SLOT, cols))
    return wide.reshape(slices * SLOT, cols)


def expand(rows):
    wide = slot_rows(rows)
    return jnp.where(head_mask(rows.shape[0], rows.shape[1]), wide, 0.0).astype(BF16)


def collapse(full):
    rows, cols = full.shape
    kept = jnp.where(head_mask(rows // SLOT, cols), full, 0.0)
    return jnp.sum(kept.reshape(rows // SLOT, SLOT, cols), axis=1)


def in_vmem(shape, dtype):
    return pltpu.VMEM(shape, dtype)


def lane_blocks(rows):
    cols = rows.shape[1]
    spare = -cols % LANES
    if spare:
        rows = jnp.concatenate([rows, jnp.zeros((rows.shape[0], spare), rows.dtype)], axis=1)
    return jnp.concatenate(
        [rows[:, b : b + LANES] for b in range(0, cols + spare, LANES)], axis=0
    )


def from_lane_blocks(rows, cols):
    count = rows.shape[0] // pl.cdiv(cols, LANES)
    blocks = [rows[b : b + count] for b in range(0, rows.shape[0], count)]
    return jnp.concatenate(blocks, axis=1)[:, :cols]


def partner(here, shift, chips):
    return here ^ shift if chips & (chips - 1) == 0 else (here + shift) % chips


def forward_kernel(
    chunk,
    patches_hbm,
    w_query_hbm,
    w_key_hbm,
    w_value_hbm,
    w_out_hbm,
    cls_hbm,
    patches,
    w_key,
    w_value,
    w_out,
    probs,
    stats,
    cls_norm,
    head_terms,
    factor,
    pooled,
    cls_rows,
    w_query,
    query_keys,
    sems,
    patch_sems,
):
    slices, tokens, width = patches.shape
    scale = float(HD) ** (-0.5)

    def fetch(source, target, n):
        copy = pltpu.make_async_copy(source, target, sems.at[n])
        copy.start()
        return copy

    get_rows = fetch(cls_hbm, cls_rows, 4)
    get_query = fetch(w_query_hbm, w_query, 0)
    get_key = fetch(w_key_hbm, w_key, 1)
    get_patches = []
    for c in range(slices // chunk):
        part = pl.ds(c * chunk, chunk)
        copy = pltpu.make_async_copy(patches_hbm.at[part], patches.at[part], patch_sems.at[c])
        copy.start()
        get_patches.append(copy)
    get_value = fetch(w_value_hbm, w_value, 2)
    get_out = fetch(w_out_hbm, w_out, 3)

    def spread(z):
        wide = patches[z].astype(F32)
        first = wide[:, 0:1]
        squares = None
        for b in range(0, width, LANES):
            off = wide[:, b : b + LANES] - first
            squares = off * off if squares is None else squares + off * off
        return jnp.sum(squares.T, axis=0, keepdims=True)

    groups = [range(z, z + chunk) for z in range(0, slices, chunk)]
    get_rows.wait()
    rows = normalize(cls_rows[...].astype(F32))[0].astype(BF16)
    cls_norm[...] = rows
    get_query.wait()
    get_key.wait()
    get_patches[0].wait()
    totals = {z: spread(z) for z in groups[0]}
    q = dot(rows, w_query[...]).astype(BF16)
    keys = (dot(expand(q), w_key[...], BY_COLS) * scale).astype(BF16).astype(F32)
    key_sums = jnp.sum(keys, axis=-1, keepdims=True)
    place = lax.broadcasted_iota(jnp.int32, (SLOT, width), 0)
    entry = lax.broadcasted_iota(jnp.int32, (SLOT, width), 1)
    picks = jnp.where((place == 0) | ((place == 1) & (entry == 0)), 1.0, 0.0)
    for z in range(slices):
        query_keys[z] = jnp.concatenate(
            [keys[z * SLOT : (z + 1) * SLOT], picks], axis=0
        ).astype(BF16)

    def attend(z, raw, total):
        mean = raw[SLOT : SLOT + 1] * (1.0 / width)
        off = mean - raw[SLOT + 1 : SLOT + 2]
        inv_std = lax.rsqrt(jnp.maximum(total * (1.0 / width) - off * off, 0.0) + 1e-05)
        stats[z : z + 1] = mean
        stats[slices + z : slices + z + 1] = inv_std
        here = slice(z * SLOT, (z + 1) * SLOT)
        scores = inv_std * (raw[:SLOT] - mean * key_sums[here])
        powers = jnp.exp(scores - jnp.max(scores, axis=-1, keepdims=True))
        p = powers / jnp.sum(powers, axis=-1, keepdims=True)
        probs[z] = p
        weights = (p.astype(BF16).astype(F32) * inv_std).astype(BF16)
        shift = jnp.sum(weights.astype(F32) * mean, axis=-1, keepdims=True)
        factor[here] = dot(weights, patches[z]) - shift

    waiting = []
    for g, group in enumerate(groups):
        if g + 1 < len(groups):
            get_patches[g + 1].wait()
        ready = [(z, dot(query_keys[z], patches[z], BY_COLS)) for z in group]
        if g + 1 < len(groups):
            totals.update({z: spread(z) for z in groups[g + 1]})
        for z, raw in waiting:
            attend(z, raw, totals[z])
        waiting = ready
    get_value.wait()
    get_out.wait()
    for z, raw in waiting:
        attend(z, raw, totals[z])

    value_factor = factor[...]
    pool = collapse(dot(value_factor.astype(BF16), w_value[...])).astype(BF16)
    head_terms[...] = dot(pool, w_out[...]).astype(BF16)
    pooled[...] = jnp.concatenate([q.astype(F32), pool.astype(F32)], axis=0)


def encoder_forward(patches, cls_rows, w_query, w_key, w_value, w_out):
    slices, tokens, width = patches.shape
    cols = w_query.shape[1]
    chunk = CHUNK
    far = (patches, w_query, w_key, w_value, w_out, cls_rows)
    hbm = pl.BlockSpec(memory_space=pltpu.HBM)
    vmem = pl.BlockSpec(memory_space=pltpu.VMEM)
    out_shape = [
        in_vmem(patches.shape, BF16),
        in_vmem(w_key.shape, BF16),
        in_vmem(w_value.shape, BF16),
        in_vmem(w_out.shape, BF16),
        in_vmem((slices, SLOT, tokens), F32),
        in_vmem((2 * slices, tokens), F32),
        in_vmem((slices, width), BF16),
        in_vmem((slices, width), BF16),
        in_vmem((slices * SLOT, width), F32),
        in_vmem((2 * slices, cols), F32),
    ]
    return pl.pallas_call(
        functools.partial(forward_kernel, chunk),
        in_specs=[hbm] * len(far),
        out_specs=[vmem] * len(out_shape),
        out_shape=out_shape,
        scratch_shapes=[
            pltpu.VMEM(cls_rows.shape, BF16),
            pltpu.VMEM(w_query.shape, BF16),
            pltpu.VMEM((slices, 2 * SLOT, width), BF16),
            pltpu.SemaphoreType.DMA((5,)),
            pltpu.SemaphoreType.DMA((slices // chunk,)),
        ],
        compiler_params=pltpu.CompilerParams(vmem_limit_bytes=VMEM_LIMIT),
        name="encoder_forward",
    )(*[pltpu.with_memory_space_constraint(a, pltpu.HBM) for a in far])


def turn_kernel(patches, turned):
    for z in range(patches.shape[0]):
        turned[z] = patches[z].T


def turn_patches(patches):
    slices, tokens, width = patches.shape
    vmem = pl.BlockSpec(memory_space=pltpu.VMEM)
    return pl.pallas_call(
        turn_kernel,
        in_specs=[vmem],
        out_specs=vmem,
        out_shape=in_vmem((slices, width, tokens), BF16),
        compiler_params=pltpu.CompilerParams(vmem_limit_bytes=VMEM_LIMIT),
        name="turn_patches",
    )(patches)


def head_rows(x, heads):
    rows, cols = x.shape
    wide = (heads * rows, cols)
    mine = (
        lax.broadcasted_iota(jnp.int32, wide, 0) // rows
        == lax.broadcasted_iota(jnp.int32, wide, 1) // HD
    )
    tall = jnp.broadcast_to(x.astype(F32)[None], (heads, rows, cols)).reshape(wide)
    return jnp.where(mine, tall, 0.0).astype(BF16), mine


def prepare_kernel(heads, slices, ids, up, a_out, factor, pooled, d_wide, bias, turned, early):
    value_factor = factor[...]
    turned[...] = jnp.concatenate([jnp.zeros_like(value_factor), value_factor], axis=0).T
    early[...] = lane_blocks(pooled[...]).astype(BF16)
    rows = 2 * slices
    total = ids.shape[0]
    start = (lax.axis_index("gz") * lax.axis_size("dev") + lax.axis_index("dev")) * slices
    d_pooled = dot(up[...], a_out[...], BY_COLS).astype(BF16)
    d_wide[...] = head_rows(d_pooled, heads)[0]
    square = (heads * rows, rows)
    i_of = lax.broadcasted_iota(jnp.int32, square, 0) % rows
    j_of = lax.broadcasted_iota(jnp.int32, square, 1)
    id_i = jnp.full(square, -1, jnp.int32)
    id_j = jnp.full(square, -1, jnp.int32)
    for n in range(rows):
        place = start + n
        scan = jnp.where(place < total, ids[jnp.minimum(place, total - 1)], -1)
        id_i = jnp.where(i_of == n, scan, id_i)
        id_j = jnp.where(j_of == n, scan, id_j)
    allowed = ((id_i == id_j) & (id_j >= 0)) | (i_of == j_of)
    bias[...] = jnp.where(allowed, 1.0, 0.0)


def prepare_window(ids, up, a_out, factor, pooled, slices):
    cols = a_out.shape[0]
    width = a_out.shape[1]
    heads = cols // HD
    rows = 2 * slices
    vmem = pl.BlockSpec(memory_space=pltpu.VMEM)
    return pl.pallas_call(
        functools.partial(prepare_kernel, heads, slices),
        in_specs=[pl.BlockSpec(memory_space=pltpu.SMEM)] + [vmem] * 4,
        out_specs=[vmem] * 4,
        out_shape=[
            in_vmem((heads * rows, cols), BF16),
            in_vmem((heads * rows, rows), F32),
            in_vmem((width, 2 * slices * SLOT), F32),
            in_vmem((2 * slices * pl.cdiv(cols, LANES), LANES), BF16),
        ],
        compiler_params=pltpu.CompilerParams(vmem_limit_bytes=VMEM_LIMIT),
        name="prepare_window",
    )(ids, up, a_out, factor, pooled)


def choose(within, across, inside, edge):
    across = jnp.where(edge, 0.0, across.astype(F32))
    return jnp.where(inside, within.astype(F32), across)


def window_kernel(heads, own, within, across, a_query, a_key, a_value, d_wide, allowed, d_half):
    scale = float(HD) ** (-0.5)
    last = lax.axis_index("gz") == lax.axis_size("gz") - 1
    following = choose(within[...], across[...], lax.axis_index("dev") == 0, last)
    window = jnp.concatenate([own[...].astype(F32), following], axis=0)
    rows = window.shape[0]
    cols = a_query.shape[1]
    half = normalize(window)[0].astype(BF16)
    q_wide, mine = head_rows(dot(half, a_query[...]).astype(BF16), heads)
    k = dot(half, a_key[...]).astype(BF16)
    v = dot(half, a_value[...]).astype(BF16)
    scores = jnp.where(allowed[...] > 0.5, dot(q_wide, k, BY_COLS) * scale, -1e30)
    d_probs = dot(d_wide[...], v, BY_COLS)
    powers = jnp.exp(scores - jnp.max(scores, axis=-1, keepdims=True))
    probs = powers / jnp.sum(powers, axis=-1, keepdims=True)
    inner = jnp.sum(probs * d_probs, axis=-1, keepdims=True)
    d_scores = (probs * (d_probs - inner) * scale).astype(BF16)
    d_value = dot(probs.astype(BF16), d_wide[...], BY_ROWS).astype(BF16)
    d_query = jnp.where(mine, dot(d_scores, k), 0.0)
    d_query = jnp.sum(d_query.reshape(heads, rows, cols), axis=0).astype(BF16)
    d_key = dot(d_scores, q_wide, BY_ROWS).astype(BF16)
    terms = (
        dot(d_value, a_value[...], BY_COLS)
        + dot(d_query, a_query[...], BY_COLS)
        + dot(d_key, a_key[...], BY_COLS)
    )
    d_half[...] = terms.astype(BF16)


def window_gradients(own, within, across, a_query, a_key, a_value, d_wide, allowed):
    slices, width = own.shape
    heads = a_query.shape[1] // HD
    vmem = pl.BlockSpec(memory_space=pltpu.VMEM)
    return pl.pallas_call(
        functools.partial(window_kernel, heads),
        in_specs=[vmem] * 8,
        out_specs=vmem,
        out_shape=in_vmem((2 * slices, width), BF16),
        compiler_params=pltpu.CompilerParams(vmem_limit_bytes=VMEM_LIMIT),
        name="window_gradients",
    )(own, within, across, a_query, a_key, a_value, d_wide, allowed)


def backward_kernel(
    chips,
    patches,
    patches_turned,
    probs,
    stats,
    d_own,
    d_others,
    within,
    across,
    embedded,
    up,
    w_key,
    w_value,
    w_out,
    cls_norm,
    turned_value,
    early,
    *rest,
):
    outs, (turned, d_keys, factor) = rest[:chips], rest[chips:]
    scale = float(HD) ** (-0.5)
    slices = embedded.shape[0]

    carried = choose(
        within[...], across[...], lax.axis_index("dev") == 1, lax.axis_index("gz") == 0
    )
    win_norm, inv_std = normalize(embedded[...].astype(F32))
    d_normed = d_own[:slices].astype(F32) + carried[:slices]
    for n in range(d_others.shape[0]):
        d_normed = d_normed + d_others[n, :slices].astype(F32)
    centred = (
        d_normed
        - jnp.mean(d_normed, axis=-1, keepdims=True)
        - win_norm * jnp.mean(d_normed * win_norm, axis=-1, keepdims=True)
    )
    d_embed = up[:slices].astype(F32) + carried[slices:] + inv_std * centred
    d_embed = d_embed.astype(BF16)
    d_att = dot(d_embed, w_out[...], BY_COLS).astype(BF16)
    keys = dot(expand(d_att), w_value[...], BY_COLS).astype(BF16).astype(F32)
    key_sums = jnp.sum(keys, axis=-1, keepdims=True)
    d_keys[...] = keys

    def score(z):
        return dot(d_keys[z * SLOT : (z + 1) * SLOT].astype(BF16), patches_turned[z])

    def attend(z, raw):
        here = slice(z * SLOT, (z + 1) * SLOT)
        p = probs[z]
        mean = stats[z : z + 1]
        inv = stats[slices + z : slices + z + 1]
        d_probs = inv * (raw - mean * key_sums[here])
        inner = jnp.sum(p * d_probs, axis=-1, keepdims=True)
        d_scores = (p * (d_probs - inner) * scale).astype(BF16)
        weights = (d_scores.astype(F32) * inv).astype(BF16)
        shift = jnp.sum(weights.astype(F32) * mean, axis=-1, keepdims=True)
        factor[here] = dot(weights, patches[z]) - shift

    waiting = []
    for c in range(0, slices, CHUNK):
        ready = [(z, score(z)) for z in range(c, c + CHUNK)]
        for item in waiting:
            attend(*item)
        waiting = ready
    for item in waiting:
        attend(*item)

    key_factor = factor[...]
    d_query = collapse(dot(key_factor.astype(BF16), w_key[...])).astype(BF16)
    slot = lax.broadcasted_iota(jnp.int32, key_factor.shape, 0) % SLOT
    left = jnp.where(slot == SLOT - 2, slot_rows(cls_norm[...]), key_factor)
    left = jnp.where(slot == SLOT - 1, slot_rows(d_embed), left)
    right = jnp.concatenate([d_att.astype(F32), d_query.astype(F32)], axis=0)
    turned[...] = jnp.concatenate([left, jnp.zeros_like(left)], axis=0).T + turned_value[...]
    late = lane_blocks(right).astype(BF16)
    part = turned.shape[0] // chips
    middle = part + late.shape[0]
    here = lax.axis_index("gz")
    for shift in range(chips):
        first = pl.multiple_of(partner(here, shift, chips) * part, SLOT)
        outs[shift][:part] = turned[pl.ds(first, part), :].astype(BF16)
        outs[shift][part:middle] = late
        outs[shift][middle:] = early[...]


def encoder_backward(
    patches, patches_turned, probs, stats, d_own, d_others, within, across, embedded, up, w_key, w_value, w_out,
    cls_norm, turned_value, early, chips,
):
    slices, tokens, width = patches.shape
    cols = w_key.shape[1]
    vmem = pl.BlockSpec(memory_space=pltpu.VMEM)
    message = (width // chips + 4 * slices * pl.cdiv(cols, LANES), LANES)
    return pl.pallas_call(
        functools.partial(backward_kernel, chips),
        in_specs=[vmem] * 16,
        out_specs=[vmem] * chips,
        out_shape=[in_vmem(message, BF16)] * chips,
        scratch_shapes=[
            pltpu.VMEM((width, LANES), F32),
            pltpu.VMEM((slices * SLOT, width), F32),
            pltpu.VMEM((slices * SLOT, width), F32),
        ],
        compiler_params=pltpu.CompilerParams(vmem_limit_bytes=VMEM_LIMIT),
        name="encoder_backward",
    )(
        patches, patches_turned, probs, stats, d_own, d_others, within, across, embedded, up, w_key, w_value, w_out,
        cls_norm, turned_value, early,
    )


def assemble_kernel(slices, cols, part, chips, *refs):
    messages, (kept, sent) = refs[:chips], refs[chips:]
    mask = head_mask(slices, cols)
    slot = lax.broadcasted_iota(jnp.int32, mask.shape, 0) % SLOT
    depth = slices * SLOT
    rows = 2 * slices * pl.cdiv(cols, LANES)

    def stacked(columns):
        blocks = [m[:part, columns].astype(F32) for m in messages]
        return jnp.concatenate(blocks, axis=1).astype(BF16)

    first, second = [], []
    for m in messages:
        for start, into in ((part, second), (part + rows, first)):
            block = from_lane_blocks(m[start : start + rows].astype(F32), cols)
            into.append([slot_rows(block[:slices]), slot_rows(block[slices:])])
    left_key, left_value = stacked(slice(0, depth)), stacked(slice(depth, 2 * depth))

    def right(blocks):
        return jnp.concatenate(blocks, axis=0).astype(BF16)

    grads = [
        dot(left_key, right([jnp.where(slot == SLOT - 2, b[1], 0.0) for b in second])),
        dot(left_key, right([jnp.where(mask, b[0], 0.0) for b in first])),
        dot(left_value, right([jnp.where(mask, b[0], 0.0) for b in second])),
        dot(left_key, right([jnp.where(slot == SLOT - 1, b[1], 0.0) for b in first])),
    ]
    lower = lax.axis_index("dev") == 0
    half = part // 2
    for n, total in enumerate(grads):
        top, bottom = total[:half], total[half:]
        kept[n] = jnp.where(lower, top, bottom)
        sent[n] = jnp.where(lower, bottom, top).astype(BF16)


def assemble(messages, slices, cols, part):
    vmem = pl.BlockSpec(memory_space=pltpu.VMEM)
    shape = (4, part // 2, cols)
    return pl.pallas_call(
        functools.partial(assemble_kernel, slices, cols, part, len(messages)),
        in_specs=[vmem] * len(messages),
        out_specs=[vmem, vmem],
        out_shape=[in_vmem(shape, F32), in_vmem(shape, BF16)],
        compiler_params=pltpu.CompilerParams(vmem_limit_bytes=VMEM_LIMIT),
        name="assemble",
    )(*messages)


def finish_kernel(kept, arrived, *refs):
    outs, sums, sems = refs[:4], refs[4], refs[5]
    copies = []
    for n, out in enumerate(outs):
        sums[n] = kept[n] + arrived[n].astype(F32)
        copy = pltpu.make_async_copy(sums.at[n], out, sems.at[n])
        copy.start()
        copies.append(copy)
    for copy in copies:
        copy.wait()


def finish(kept, arrived):
    vmem = pl.BlockSpec(memory_space=pltpu.VMEM)
    return pl.pallas_call(
        finish_kernel,
        in_specs=[vmem, vmem],
        out_specs=[pl.BlockSpec(memory_space=pltpu.HBM)] * 4,
        out_shape=[pltpu.HBM(kept.shape[1:], F32)] * 4,
        scratch_shapes=[pltpu.VMEM(kept.shape, F32), pltpu.SemaphoreType.DMA((4,))],
        compiler_params=pltpu.CompilerParams(vmem_limit_bytes=VMEM_LIMIT),
        name="finish",
    )(kept, arrived)


def ring_shift(x, axis, distance):
    size = lax.axis_size(axis)
    return lax.ppermute(x, axis, [(i, (i + distance) % size) for i in range(size)])


def others(x):
    return [ring_shift(x, "ma", d) for d in range(1, lax.axis_size("ma"))]


def pair_route():
    chips, parts, cores = [lax.axis_size(a) for a in ("gz", "ma", "dev")]
    route = []
    for chip in range(chips):
        for part in range(parts):
            for core in range(cores):
                place = chip * cores + core
                other = place + 1 if core else place - 1
                at = part
                if not 0 <= other < chips * cores:
                    other, at = place, part ^ 1
                    if at >= parts:
                        continue
                source = (chip * parts + part) * cores + core
                route.append((source, (other // cores * parts + at) * cores + other % cores))
    return route


def neighbours(block):
    within = ring_shift(block, "dev", 1)
    return within, lax.ppermute(block, ("gz", "ma", "dev"), pair_route())


def exchanged(x, axis, shift):
    size = lax.axis_size(axis)
    return lax.ppermute(x, axis, [(i, partner(i, shift, size)) for i in range(size)])


def local(
    patches,
    cls_rows,
    w_query,
    w_key,
    w_value,
    w_out,
    a_query,
    a_key,
    a_value,
    a_out,
    upstream,
    slice_to_scan,
):
    slices, _, width = patches.shape
    cols = w_query.shape[1]
    chips = lax.axis_size("gz")
    up = upstream[0]
    (
        held, key_held, value_held, out_held, probs, stats, cls_norm, head_terms, factor, pooled
    ) = encoder_forward(patches, cls_rows, w_query, w_key, w_value, w_out)
    held_turned = turn_patches(held)
    d_wide, allowed, turned_value, early = prepare_window(
        slice_to_scan, up, a_out, factor, pooled, slices
    )
    total = head_terms.astype(F32)
    for term in others(head_terms):
        total = total + term.astype(F32)
    embedded = (cls_rows.astype(F32) + total).astype(BF16)
    following = neighbours(embedded)
    d_own = window_gradients(embedded, *following, a_query, a_key, a_value, d_wide, allowed)
    d_others = jnp.stack(others(d_own))
    lower = d_own[slices:].astype(F32)
    for n in range(d_others.shape[0]):
        lower = lower + d_others[n, slices:].astype(F32)
    carried = neighbours(jnp.concatenate([lower.astype(BF16), up[slices:]], axis=0))
    messages = encoder_backward(
        held, held_turned, probs, stats, d_own, d_others, *carried, embedded, up, key_held, value_held, out_held,
        cls_norm, turned_value, early, chips,
    )
    order = range(chips - 1, 0, -1)
    arrived = list(messages[:1]) + [exchanged(messages[n], "gz", n) for n in order]
    kept, sent = assemble(arrived, slices, cols, width // chips)
    return tuple(finish(kept, ring_shift(sent, "dev", 1)))


def solution(mesh):
    return jax.shard_map(
        local,
        mesh=mesh,
        in_specs=(
            P(("grp", "gz", "dev"), None, None),
            P(("grp", "gz", "dev"), None),
            P(None, "ma"),
            P(None, "ma"),
            P(None, "ma"),
            P("ma", None),
            P(None, "ma"),
            P(None, "ma"),
            P(None, "ma"),
            P("ma", None),
            P(("grp", "gz", "dev"), None, None),
            P("grp"),
        ),
        out_specs=(
            P(("grp", "gz", "dev"), "ma"),
            P(("grp", "gz", "dev"), "ma"),
            P(("grp", "gz", "dev"), "ma"),
            P(("grp", "gz", "dev"), "ma"),
        ),
        check_vma=False,
    )
```

```python
import functools

import jax
import jax.numpy as jnp
from jax import lax
from jax.experimental import pallas as pl
from jax.experimental.pallas import tpu as pltpu
from jax.sharding import PartitionSpec as P

HD = 64
SLOT = 8
LANES = 128
F32 = jnp.float32
BF16 = jnp.bfloat16
CHUNK = 2
VMEM_LIMIT = 16 * 1024 * 1024


def dot(a, b, dims=((1,), (0,))):
    return lax.dot_general(a, b, (dims, ((), ())), preferred_element_type=F32)


BY_COLS = ((1,), (1,))
BY_ROWS = ((0,), (0,))


def normalize(values):
    row_mean = jnp.mean(values, axis=-1, keepdims=True)
    centred = values - row_mean
    variance = jnp.mean(centred * centred, axis=-1, keepdims=True)
    inv_std = lax.rsqrt(variance + 1e-05)
    return centred * inv_std, inv_std


def head_mask(slices, cols):
    shape = (slices * SLOT, cols)
    row = lax.broadcasted_iota(jnp.int32, shape, 0)
    col = lax.broadcasted_iota(jnp.int32, shape, 1)
    return row % SLOT == col // HD


def slot_rows(rows):
    slices, cols = rows.shape
    wide = jnp.broadcast_to(rows.astype(F32)[:, None, :], (slices, SLOT, cols))
    return wide.reshape(slices * SLOT, cols)


def expand(rows):
    wide = slot_rows(rows)
    return jnp.where(head_mask(rows.shape[0], rows.shape[1]), wide, 0.0).astype(BF16)


def collapse(full):
    rows, cols = full.shape
    kept = jnp.where(head_mask(rows // SLOT, cols), full, 0.0)
    return jnp.sum(kept.reshape(rows // SLOT, SLOT, cols), axis=1)


def in_vmem(shape, dtype):
    return pltpu.VMEM(shape, dtype)


def lane_blocks(rows):
    cols = rows.shape[1]
    spare = -cols % LANES
    if spare:
        rows = jnp.concatenate([rows, jnp.zeros((rows.shape[0], spare), rows.dtype)], axis=1)
    return jnp.concatenate(
        [rows[:, b : b + LANES] for b in range(0, cols + spare, LANES)], axis=0
    )


def from_lane_blocks(rows, cols):
    count = rows.shape[0] // pl.cdiv(cols, LANES)
    blocks = [rows[b : b + count] for b in range(0, rows.shape[0], count)]
    return jnp.concatenate(blocks, axis=1)[:, :cols]


def partner(here, shift, chips):
    return here ^ shift if chips & (chips - 1) == 0 else (here + shift) % chips


def forward_kernel(
    chunk,
    patches_hbm,
    w_query_hbm,
    w_key_hbm,
    w_value_hbm,
    w_out_hbm,
    cls_hbm,
    patches,
    w_key,
    w_value,
    w_out,
    probs,
    stats,
    cls_norm,
    head_terms,
    factor,
    pooled,
    cls_rows,
    w_query,
    query_keys,
    sems,
    patch_sems,
):
    slices, tokens, width = patches.shape
    scale = float(HD) ** (-0.5)

    def fetch(source, target, n):
        copy = pltpu.make_async_copy(source, target, sems.at[n])
        copy.start()
        return copy

    get_rows = fetch(cls_hbm, cls_rows, 4)
    get_query = fetch(w_query_hbm, w_query, 0)
    get_key = fetch(w_key_hbm, w_key, 1)
    get_patches = []
    for c in range(slices // chunk):
        part = pl.ds(c * chunk, chunk)
        copy = pltpu.make_async_copy(patches_hbm.at[part], patches.at[part], patch_sems.at[c])
        copy.start()
        get_patches.append(copy)
    get_value = fetch(w_value_hbm, w_value, 2)
    get_out = fetch(w_out_hbm, w_out, 3)

    def spread(z):
        wide = patches[z].astype(F32)
        first = wide[:, 0:1]
        squares = None
        for b in range(0, width, LANES):
            off = wide[:, b : b + LANES] - first
            squares = off * off if squares is None else squares + off * off
        return jnp.sum(squares.T, axis=0, keepdims=True)

    groups = [range(z, z + chunk) for z in range(0, slices, chunk)]
    get_rows.wait()
    rows = normalize(cls_rows[...].astype(F32))[0].astype(BF16)
    cls_norm[...] = rows
    get_query.wait()
    get_key.wait()
    get_patches[0].wait()
    totals = {z: spread(z) for z in groups[0]}
    q = dot(rows, w_query[...]).astype(BF16)
    keys = (dot(expand(q), w_key[...], BY_COLS) * scale).astype(BF16).astype(F32)
    key_sums = jnp.sum(keys, axis=-1, keepdims=True)
    place = lax.broadcasted_iota(jnp.int32, (SLOT, width), 0)
    entry = lax.broadcasted_iota(jnp.int32, (SLOT, width), 1)
    picks = jnp.where((place == 0) | ((place == 1) & (entry == 0)), 1.0, 0.0)
    for z in range(slices):
        query_keys[z] = jnp.concatenate(
            [keys[z * SLOT : (z + 1) * SLOT], picks], axis=0
        ).astype(BF16)

    def attend(z, raw, total):
        mean = raw[SLOT : SLOT + 1] * (1.0 / width)
        off = mean - raw[SLOT + 1 : SLOT + 2]
        inv_std = lax.rsqrt(jnp.maximum(total * (1.0 / width) - off * off, 0.0) + 1e-05)
        stats[z : z + 1] = mean
        stats[slices + z : slices + z + 1] = inv_std
        here = slice(z * SLOT, (z + 1) * SLOT)
        scores = inv_std * (raw[:SLOT] - mean * key_sums[here])
        powers = jnp.exp(scores - jnp.max(scores, axis=-1, keepdims=True))
        p = powers / jnp.sum(powers, axis=-1, keepdims=True)
        probs[z] = p
        weights = (p.astype(BF16).astype(F32) * inv_std).astype(BF16)
        shift = jnp.sum(weights.astype(F32) * mean, axis=-1, keepdims=True)
        return weights, shift

    def gather(z, weights, shift):
        factor[z * SLOT : (z + 1) * SLOT] = dot(weights, patches[z]) - shift

    waiting, weighted = [], []
    for g, group in enumerate(groups):
        if g + 1 < len(groups):
            get_patches[g + 1].wait()
        ready = [(z, dot(query_keys[z], patches[z], BY_COLS)) for z in group]
        if g + 1 < len(groups):
            totals.update({z: spread(z) for z in groups[g + 1]})
        for item in weighted:
            gather(*item)
        weighted = [(z,) + attend(z, raw, totals[z]) for z, raw in waiting]
        waiting = ready
    get_value.wait()
    get_out.wait()
    for item in weighted + [(z,) + attend(z, raw, totals[z]) for z, raw in waiting]:
        gather(*item)

    value_factor = factor[...]
    pool = collapse(dot(value_factor.astype(BF16), w_value[...])).astype(BF16)
    head_terms[...] = dot(pool, w_out[...]).astype(BF16)
    pooled[...] = jnp.concatenate([q.astype(F32), pool.astype(F32)], axis=0)


def encoder_forward(patches, cls_rows, w_query, w_key, w_value, w_out):
    slices, tokens, width = patches.shape
    cols = w_query.shape[1]
    chunk = CHUNK
    far = (patches, w_query, w_key, w_value, w_out, cls_rows)
    hbm = pl.BlockSpec(memory_space=pltpu.HBM)
    vmem = pl.BlockSpec(memory_space=pltpu.VMEM)
    out_shape = [
        in_vmem(patches.shape, BF16),
        in_vmem(w_key.shape, BF16),
        in_vmem(w_value.shape, BF16),
        in_vmem(w_out.shape, BF16),
        in_vmem((slices, SLOT, tokens), F32),
        in_vmem((2 * slices, tokens), F32),
        in_vmem((slices, width), BF16),
        in_vmem((slices, width), BF16),
        in_vmem((slices * SLOT, width), F32),
        in_vmem((2 * slices, cols), F32),
    ]
    return pl.pallas_call(
        functools.partial(forward_kernel, chunk),
        in_specs=[hbm] * len(far),
        out_specs=[vmem] * len(out_shape),
        out_shape=out_shape,
        scratch_shapes=[
            pltpu.VMEM(cls_rows.shape, BF16),
            pltpu.VMEM(w_query.shape, BF16),
            pltpu.VMEM((slices, 2 * SLOT, width), BF16),
            pltpu.SemaphoreType.DMA((5,)),
            pltpu.SemaphoreType.DMA((slices // chunk,)),
        ],
        compiler_params=pltpu.CompilerParams(vmem_limit_bytes=VMEM_LIMIT),
        name="encoder_forward",
    )(*[pltpu.with_memory_space_constraint(a, pltpu.HBM) for a in far])


def turn_kernel(patches, turned):
    for z in range(patches.shape[0]):
        turned[z] = patches[z].T


def turn_patches(patches):
    slices, tokens, width = patches.shape
    vmem = pl.BlockSpec(memory_space=pltpu.VMEM)
    return pl.pallas_call(
        turn_kernel,
        in_specs=[vmem],
        out_specs=vmem,
        out_shape=in_vmem((slices, width, tokens), BF16),
        compiler_params=pltpu.CompilerParams(vmem_limit_bytes=VMEM_LIMIT),
        name="turn_patches",
    )(patches)


def head_rows(x, heads):
    rows, cols = x.shape
    wide = (heads * rows, cols)
    mine = (
        lax.broadcasted_iota(jnp.int32, wide, 0) // rows
        == lax.broadcasted_iota(jnp.int32, wide, 1) // HD
    )
    tall = jnp.broadcast_to(x.astype(F32)[None], (heads, rows, cols)).reshape(wide)
    return jnp.where(mine, tall, 0.0).astype(BF16), mine


def prepare_kernel(heads, slices, ids, up, a_out, factor, pooled, d_wide, bias, turned, early):
    value_factor = factor[...]
    turned[...] = jnp.concatenate([jnp.zeros_like(value_factor), value_factor], axis=0).T
    early[...] = lane_blocks(pooled[...]).astype(BF16)
    rows = 2 * slices
    total = ids.shape[0]
    start = (lax.axis_index("gz") * lax.axis_size("dev") + lax.axis_index("dev")) * slices
    d_pooled = dot(up[...], a_out[...], BY_COLS).astype(BF16)
    d_wide[...] = head_rows(d_pooled, heads)[0]
    square = (heads * rows, rows)
    i_of = lax.broadcasted_iota(jnp.int32, square, 0) % rows
    j_of = lax.broadcasted_iota(jnp.int32, square, 1)
    id_i = jnp.full(square, -1, jnp.int32)
    id_j = jnp.full(square, -1, jnp.int32)
    for n in range(rows):
        place = start + n
        scan = jnp.where(place < total, ids[jnp.minimum(place, total - 1)], -1)
        id_i = jnp.where(i_of == n, scan, id_i)
        id_j = jnp.where(j_of == n, scan, id_j)
    allowed = ((id_i == id_j) & (id_j >= 0)) | (i_of == j_of)
    bias[...] = jnp.where(allowed, 1.0, 0.0)


def prepare_window(ids, up, a_out, factor, pooled, slices):
    cols = a_out.shape[0]
    width = a_out.shape[1]
    heads = cols // HD
    rows = 2 * slices
    vmem = pl.BlockSpec(memory_space=pltpu.VMEM)
    return pl.pallas_call(
        functools.partial(prepare_kernel, heads, slices),
        in_specs=[pl.BlockSpec(memory_space=pltpu.SMEM)] + [vmem] * 4,
        out_specs=[vmem] * 4,
        out_shape=[
            in_vmem((heads * rows, cols), BF16),
            in_vmem((heads * rows, rows), F32),
            in_vmem((width, 2 * slices * SLOT), F32),
            in_vmem((2 * slices * pl.cdiv(cols, LANES), LANES), BF16),
        ],
        compiler_params=pltpu.CompilerParams(vmem_limit_bytes=VMEM_LIMIT),
        name="prepare_window",
    )(ids, up, a_out, factor, pooled)


def choose(within, across, inside, edge):
    across = jnp.where(edge, 0.0, across.astype(F32))
    return jnp.where(inside, within.astype(F32), across)


def window_kernel(heads, own, within, across, a_query, a_key, a_value, d_wide, allowed, d_half):
    scale = float(HD) ** (-0.5)
    last = lax.axis_index("gz") == lax.axis_size("gz") - 1
    following = choose(within[...], across[...], lax.axis_index("dev") == 0, last)
    window = jnp.concatenate([own[...].astype(F32), following], axis=0)
    rows = window.shape[0]
    cols = a_query.shape[1]
    half = normalize(window)[0].astype(BF16)
    q_wide, mine = head_rows(dot(half, a_query[...]).astype(BF16), heads)
    k = dot(half, a_key[...]).astype(BF16)
    v = dot(half, a_value[...]).astype(BF16)
    scores = jnp.where(allowed[...] > 0.5, dot(q_wide, k, BY_COLS) * scale, -1e30)
    d_probs = dot(d_wide[...], v, BY_COLS)
    powers = jnp.exp(scores - jnp.max(scores, axis=-1, keepdims=True))
    probs = powers / jnp.sum(powers, axis=-1, keepdims=True)
    inner = jnp.sum(probs * d_probs, axis=-1, keepdims=True)
    d_scores = (probs * (d_probs - inner) * scale).astype(BF16)
    d_value = dot(probs.astype(BF16), d_wide[...], BY_ROWS).astype(BF16)
    d_query = jnp.where(mine, dot(d_scores, k), 0.0)
    d_query = jnp.sum(d_query.reshape(heads, rows, cols), axis=0).astype(BF16)
    d_key = dot(d_scores, q_wide, BY_ROWS).astype(BF16)
    terms = (
        dot(d_value, a_value[...], BY_COLS)
        + dot(d_query, a_query[...], BY_COLS)
        + dot(d_key, a_key[...], BY_COLS)
    )
    d_half[...] = terms.astype(BF16)


def window_gradients(own, within, across, a_query, a_key, a_value, d_wide, allowed):
    slices, width = own.shape
    heads = a_query.shape[1] // HD
    vmem = pl.BlockSpec(memory_space=pltpu.VMEM)
    return pl.pallas_call(
        functools.partial(window_kernel, heads),
        in_specs=[vmem] * 8,
        out_specs=vmem,
        out_shape=in_vmem((2 * slices, width), BF16),
        compiler_params=pltpu.CompilerParams(vmem_limit_bytes=VMEM_LIMIT),
        name="window_gradients",
    )(own, within, across, a_query, a_key, a_value, d_wide, allowed)


def backward_kernel(
    chips,
    patches,
    patches_turned,
    probs,
    stats,
    d_own,
    d_others,
    within,
    across,
    embedded,
    up,
    w_key,
    w_value,
    w_out,
    cls_norm,
    turned_value,
    early,
    *rest,
):
    outs, (turned, d_keys, factor) = rest[:chips], rest[chips:]
    scale = float(HD) ** (-0.5)
    slices = embedded.shape[0]

    carried = choose(
        within[...], across[...], lax.axis_index("dev") == 1, lax.axis_index("gz") == 0
    )
    win_norm, inv_std = normalize(embedded[...].astype(F32))
    d_normed = d_own[:slices].astype(F32) + carried[:slices]
    for n in range(d_others.shape[0]):
        d_normed = d_normed + d_others[n, :slices].astype(F32)
    centred = (
        d_normed
        - jnp.mean(d_normed, axis=-1, keepdims=True)
        - win_norm * jnp.mean(d_normed * win_norm, axis=-1, keepdims=True)
    )
    d_embed = up[:slices].astype(F32) + carried[slices:] + inv_std * centred
    d_embed = d_embed.astype(BF16)
    d_att = dot(d_embed, w_out[...], BY_COLS).astype(BF16)
    keys = dot(expand(d_att), w_value[...], BY_COLS).astype(BF16).astype(F32)
    key_sums = jnp.sum(keys, axis=-1, keepdims=True)
    d_keys[...] = keys

    def score(z):
        return dot(d_keys[z * SLOT : (z + 1) * SLOT].astype(BF16), patches_turned[z])

    def attend(z, raw):
        here = slice(z * SLOT, (z + 1) * SLOT)
        p = probs[z]
        mean = stats[z : z + 1]
        inv = stats[slices + z : slices + z + 1]
        d_probs = inv * (raw - mean * key_sums[here])
        inner = jnp.sum(p * d_probs, axis=-1, keepdims=True)
        d_scores = (p * (d_probs - inner) * scale).astype(BF16)
        weights = (d_scores.astype(F32) * inv).astype(BF16)
        shift = jnp.sum(weights.astype(F32) * mean, axis=-1, keepdims=True)
        factor[here] = dot(weights, patches[z]) - shift

    waiting = []
    for c in range(0, slices, CHUNK):
        ready = [(z, score(z)) for z in range(c, c + CHUNK)]
        for item in waiting:
            attend(*item)
        waiting = ready
    for item in waiting:
        attend(*item)

    key_factor = factor[...]
    d_query = collapse(dot(key_factor.astype(BF16), w_key[...])).astype(BF16)
    slot = lax.broadcasted_iota(jnp.int32, key_factor.shape, 0) % SLOT
    left = jnp.where(slot == SLOT - 2, slot_rows(cls_norm[...]), key_factor)
    left = jnp.where(slot == SLOT - 1, slot_rows(d_embed), left)
    right = jnp.concatenate([d_att.astype(F32), d_query.astype(F32)], axis=0)
    turned[...] = jnp.concatenate([left, jnp.zeros_like(left)], axis=0).T + turned_value[...]
    late = lane_blocks(right).astype(BF16)
    part = turned.shape[0] // chips
    middle = part + late.shape[0]
    here = lax.axis_index("gz")
    for shift in range(chips):
        first = pl.multiple_of(partner(here, shift, chips) * part, SLOT)
        outs[shift][:part] = turned[pl.ds(first, part), :].astype(BF16)
        outs[shift][part:middle] = late
        outs[shift][middle:] = early[...]


def encoder_backward(
    patches, patches_turned, probs, stats, d_own, d_others, within, across, embedded, up, w_key, w_value, w_out,
    cls_norm, turned_value, early, chips,
):
    slices, tokens, width = patches.shape
    cols = w_key.shape[1]
    vmem = pl.BlockSpec(memory_space=pltpu.VMEM)
    message = (width // chips + 4 * slices * pl.cdiv(cols, LANES), LANES)
    return pl.pallas_call(
        functools.partial(backward_kernel, chips),
        in_specs=[vmem] * 16,
        out_specs=[vmem] * chips,
        out_shape=[in_vmem(message, BF16)] * chips,
        scratch_shapes=[
            pltpu.VMEM((width, LANES), F32),
            pltpu.VMEM((slices * SLOT, width), F32),
            pltpu.VMEM((slices * SLOT, width), F32),
        ],
        compiler_params=pltpu.CompilerParams(vmem_limit_bytes=VMEM_LIMIT),
        name="encoder_backward",
    )(
        patches, patches_turned, probs, stats, d_own, d_others, within, across, embedded, up, w_key, w_value, w_out,
        cls_norm, turned_value, early,
    )


def assemble_kernel(slices, cols, part, chips, *refs):
    messages, (kept, sent) = refs[:chips], refs[chips:]
    mask = head_mask(slices, cols)
    slot = lax.broadcasted_iota(jnp.int32, mask.shape, 0) % SLOT
    depth = slices * SLOT
    rows = 2 * slices * pl.cdiv(cols, LANES)

    def stacked(columns):
        blocks = [m[:part, columns].astype(F32) for m in messages]
        return jnp.concatenate(blocks, axis=1).astype(BF16)

    first, second = [], []
    for m in messages:
        for start, into in ((part, second), (part + rows, first)):
            block = from_lane_blocks(m[start : start + rows].astype(F32), cols)
            into.append([slot_rows(block[:slices]), slot_rows(block[slices:])])
    left_key, left_value = stacked(slice(0, depth)), stacked(slice(depth, 2 * depth))

    def right(blocks):
        return jnp.concatenate(blocks, axis=0).astype(BF16)

    grads = [
        dot(left_key, right([jnp.where(slot == SLOT - 2, b[1], 0.0) for b in second])),
        dot(left_key, right([jnp.where(mask, b[0], 0.0) for b in first])),
        dot(left_value, right([jnp.where(mask, b[0], 0.0) for b in second])),
        dot(left_key, right([jnp.where(slot == SLOT - 1, b[1], 0.0) for b in first])),
    ]
    lower = lax.axis_index("dev") == 0
    half = part // 2
    for n, total in enumerate(grads):
        top, bottom = total[:half], total[half:]
        kept[n] = jnp.where(lower, top, bottom)
        sent[n] = jnp.where(lower, bottom, top).astype(BF16)


def assemble(messages, slices, cols, part):
    vmem = pl.BlockSpec(memory_space=pltpu.VMEM)
    shape = (4, part // 2, cols)
    return pl.pallas_call(
        functools.partial(assemble_kernel, slices, cols, part, len(messages)),
        in_specs=[vmem] * len(messages),
        out_specs=[vmem, vmem],
        out_shape=[in_vmem(shape, F32), in_vmem(shape, BF16)],
        compiler_params=pltpu.CompilerParams(vmem_limit_bytes=VMEM_LIMIT),
        name="assemble",
    )(*messages)


def finish_kernel(kept, arrived, *refs):
    outs, sums, sems = refs[:4], refs[4], refs[5]
    copies = []
    for n, out in enumerate(outs):
        sums[n] = kept[n] + arrived[n].astype(F32)
        copy = pltpu.make_async_copy(sums.at[n], out, sems.at[n])
        copy.start()
        copies.append(copy)
    for copy in copies:
        copy.wait()


def finish(kept, arrived):
    vmem = pl.BlockSpec(memory_space=pltpu.VMEM)
    return pl.pallas_call(
        finish_kernel,
        in_specs=[vmem, vmem],
        out_specs=[pl.BlockSpec(memory_space=pltpu.HBM)] * 4,
        out_shape=[pltpu.HBM(kept.shape[1:], F32)] * 4,
        scratch_shapes=[pltpu.VMEM(kept.shape, F32), pltpu.SemaphoreType.DMA((4,))],
        compiler_params=pltpu.CompilerParams(vmem_limit_bytes=VMEM_LIMIT),
        name="finish",
    )(kept, arrived)


def ring_shift(x, axis, distance):
    size = lax.axis_size(axis)
    return lax.ppermute(x, axis, [(i, (i + distance) % size) for i in range(size)])


def others(x):
    return [ring_shift(x, "ma", d) for d in range(1, lax.axis_size("ma"))]


def pair_route():
    chips, parts, cores = [lax.axis_size(a) for a in ("gz", "ma", "dev")]
    route = []
    for chip in range(chips):
        for part in range(parts):
            for core in range(cores):
                place = chip * cores + core
                other = place + 1 if core else place - 1
                at = part
                if not 0 <= other < chips * cores:
                    other, at = place, part ^ 1
                    if at >= parts:
                        continue
                source = (chip * parts + part) * cores + core
                route.append((source, (other // cores * parts + at) * cores + other % cores))
    return route


def neighbours(block):
    within = ring_shift(block, "dev", 1)
    return within, lax.ppermute(block, ("gz", "ma", "dev"), pair_route())


def exchanged(x, axis, shift):
    size = lax.axis_size(axis)
    return lax.ppermute(x, axis, [(i, partner(i, shift, size)) for i in range(size)])


def local(
    patches,
    cls_rows,
    w_query,
    w_key,
    w_value,
    w_out,
    a_query,
    a_key,
    a_value,
    a_out,
    upstream,
    slice_to_scan,
):
    slices, _, width = patches.shape
    cols = w_query.shape[1]
    chips = lax.axis_size("gz")
    up = upstream[0]
    (
        held, key_held, value_held, out_held, probs, stats, cls_norm, head_terms, factor, pooled
    ) = encoder_forward(patches, cls_rows, w_query, w_key, w_value, w_out)
    held_turned = turn_patches(held)
    d_wide, allowed, turned_value, early = prepare_window(
        slice_to_scan, up, a_out, factor, pooled, slices
    )
    total = head_terms.astype(F32)
    for term in others(head_terms):
        total = total + term.astype(F32)
    embedded = (cls_rows.astype(F32) + total).astype(BF16)
    following = neighbours(embedded)
    d_own = window_gradients(embedded, *following, a_query, a_key, a_value, d_wide, allowed)
    d_others = jnp.stack(others(d_own))
    lower = d_own[slices:].astype(F32)
    for n in range(d_others.shape[0]):
        lower = lower + d_others[n, slices:].astype(F32)
    carried = neighbours(jnp.concatenate([lower.astype(BF16), up[slices:]], axis=0))
    messages = encoder_backward(
        held, held_turned, probs, stats, d_own, d_others, *carried, embedded, up, key_held, value_held, out_held,
        cls_norm, turned_value, early, chips,
    )
    order = range(chips - 1, 0, -1)
    arrived = list(messages[:1]) + [exchanged(messages[n], "gz", n) for n in order]
    kept, sent = assemble(arrived, slices, cols, width // chips)
    return tuple(finish(kept, ring_shift(sent, "dev", 1)))


def solution(mesh):
    return jax.shard_map(
        local,
        mesh=mesh,
        in_specs=(
            P(("grp", "gz", "dev"), None, None),
            P(("grp", "gz", "dev"), None),
            P(None, "ma"),
            P(None, "ma"),
            P(None, "ma"),
            P("ma", None),
            P(None, "ma"),
            P(None, "ma"),
            P(None, "ma"),
            P("ma", None),
            P(("grp", "gz", "dev"), None, None),
            P("grp"),
        ),
        out_specs=(
            P(("grp", "gz", "dev"), "ma"),
            P(("grp", "gz", "dev"), "ma"),
            P(("grp", "gz", "dev"), "ma"),
            P(("grp", "gz", "dev"), "ma"),
        ),
        check_vma=False,
    )
```

```python
import functools

import jax
import jax.numpy as jnp
from jax import lax
from jax.experimental import pallas as pl
from jax.experimental.pallas import tpu as pltpu
from jax.sharding import PartitionSpec as P

HD = 64
SLOT = 8
LANES = 128
F32 = jnp.float32
BF16 = jnp.bfloat16
CHUNK = 2
VMEM_LIMIT = 16 * 1024 * 1024


def dot(a, b, dims=((1,), (0,))):
    return lax.dot_general(a, b, (dims, ((), ())), preferred_element_type=F32)


BY_COLS = ((1,), (1,))
BY_ROWS = ((0,), (0,))


def normalize(values):
    row_mean = jnp.mean(values, axis=-1, keepdims=True)
    centred = values - row_mean
    variance = jnp.mean(centred * centred, axis=-1, keepdims=True)
    inv_std = lax.rsqrt(variance + 1e-05)
    return centred * inv_std, inv_std


def head_mask(slices, cols):
    shape = (slices * SLOT, cols)
    row = lax.broadcasted_iota(jnp.int32, shape, 0)
    col = lax.broadcasted_iota(jnp.int32, shape, 1)
    return row % SLOT == col // HD


def slot_rows(rows):
    slices, cols = rows.shape
    wide = jnp.broadcast_to(rows.astype(F32)[:, None, :], (slices, SLOT, cols))
    return wide.reshape(slices * SLOT, cols)


def expand(rows):
    wide = slot_rows(rows)
    return jnp.where(head_mask(rows.shape[0], rows.shape[1]), wide, 0.0).astype(BF16)


def collapse(full):
    rows, cols = full.shape
    kept = jnp.where(head_mask(rows // SLOT, cols), full, 0.0)
    return jnp.sum(kept.reshape(rows // SLOT, SLOT, cols), axis=1)


def in_vmem(shape, dtype):
    return pltpu.VMEM(shape, dtype)


def lane_blocks(rows):
    cols = rows.shape[1]
    spare = -cols % LANES
    if spare:
        rows = jnp.concatenate([rows, jnp.zeros((rows.shape[0], spare), rows.dtype)], axis=1)
    return jnp.concatenate(
        [rows[:, b : b + LANES] for b in range(0, cols + spare, LANES)], axis=0
    )


def from_lane_blocks(rows, cols):
    count = rows.shape[0] // pl.cdiv(cols, LANES)
    blocks = [rows[b : b + count] for b in range(0, rows.shape[0], count)]
    return jnp.concatenate(blocks, axis=1)[:, :cols]


def partner(here, shift, chips):
    return here ^ shift if chips & (chips - 1) == 0 else (here + shift) % chips


def forward_kernel(
    chunk,
    patches_hbm,
    w_query_hbm,
    w_key_hbm,
    w_value_hbm,
    w_out_hbm,
    cls_hbm,
    patches,
    w_key,
    w_value,
    w_out,
    probs,
    stats,
    cls_norm,
    head_terms,
    factor,
    pooled,
    cls_rows,
    w_query,
    query_keys,
    sems,
    patch_sems,
):
    slices, tokens, width = patches.shape
    scale = float(HD) ** (-0.5)

    def fetch(source, target, n):
        copy = pltpu.make_async_copy(source, target, sems.at[n])
        copy.start()
        return copy

    get_rows = fetch(cls_hbm, cls_rows, 4)
    get_query = fetch(w_query_hbm, w_query, 0)
    get_key = fetch(w_key_hbm, w_key, 1)
    get_patches = []
    for c in range(slices // chunk):
        part = pl.ds(c * chunk, chunk)
        copy = pltpu.make_async_copy(patches_hbm.at[part], patches.at[part], patch_sems.at[c])
        copy.start()
        get_patches.append(copy)
    get_value = fetch(w_value_hbm, w_value, 2)
    get_out = fetch(w_out_hbm, w_out, 3)

    def spread(z):
        wide = patches[z].astype(F32)
        first = wide[:, 0:1]
        squares = None
        for b in range(0, width, LANES):
            off = wide[:, b : b + LANES] - first
            squares = off * off if squares is None else squares + off * off
        return jnp.sum(squares.T, axis=0, keepdims=True)

    groups = [range(z, z + chunk) for z in range(0, slices, chunk)]
    get_rows.wait()
    rows = normalize(cls_rows[...].astype(F32))[0].astype(BF16)
    cls_norm[...] = rows
    get_query.wait()
    get_key.wait()
    get_patches[0].wait()
    totals = {z: spread(z) for z in groups[0]}
    q = dot(rows, w_query[...]).astype(BF16)
    keys = (dot(expand(q), w_key[...], BY_COLS) * scale).astype(BF16).astype(F32)
    key_sums = jnp.sum(keys, axis=-1, keepdims=True)
    place = lax.broadcasted_iota(jnp.int32, (SLOT, width), 0)
    entry = lax.broadcasted_iota(jnp.int32, (SLOT, width), 1)
    picks = jnp.where((place == 0) | ((place == 1) & (entry == 0)), 1.0, 0.0)
    for z in range(slices):
        query_keys[z] = jnp.concatenate(
            [keys[z * SLOT : (z + 1) * SLOT], picks], axis=0
        ).astype(BF16)

    def attend(z, raw, total):
        mean = raw[SLOT : SLOT + 1] * (1.0 / width)
        off = mean - raw[SLOT + 1 : SLOT + 2]
        inv_std = lax.rsqrt(jnp.maximum(total * (1.0 / width) - off * off, 0.0) + 1e-05)
        stats[z : z + 1] = mean
        stats[slices + z : slices + z + 1] = inv_std
        here = slice(z * SLOT, (z + 1) * SLOT)
        scores = inv_std * (raw[:SLOT] - mean * key_sums[here])
        powers = jnp.exp(scores - jnp.max(scores, axis=-1, keepdims=True))
        p = powers / jnp.sum(powers, axis=-1, keepdims=True)
        probs[z] = p
        weights = (p.astype(BF16).astype(F32) * inv_std).astype(BF16)
        shift = jnp.sum(weights.astype(F32) * mean, axis=-1, keepdims=True)
        return weights, shift

    def gather(z, weights, shift):
        factor[z * SLOT : (z + 1) * SLOT] = dot(weights, patches[z]) - shift

    waiting, weighted = [], []
    for g, group in enumerate(groups):
        if g + 1 < len(groups):
            get_patches[g + 1].wait()
        ready = [(z, dot(query_keys[z], patches[z], BY_COLS)) for z in group]
        if g + 1 < len(groups):
            totals.update({z: spread(z) for z in groups[g + 1]})
        for item in weighted:
            gather(*item)
        weighted = [(z,) + attend(z, raw, totals[z]) for z, raw in waiting]
        waiting = ready
    get_value.wait()
    get_out.wait()
    for item in weighted + [(z,) + attend(z, raw, totals[z]) for z, raw in waiting]:
        gather(*item)

    value_factor = factor[...]
    pool = collapse(dot(value_factor.astype(BF16), w_value[...])).astype(BF16)
    head_terms[...] = dot(pool, w_out[...]).astype(BF16)
    pooled[...] = jnp.concatenate([q.astype(F32), pool.astype(F32)], axis=0)


def encoder_forward(patches, cls_rows, w_query, w_key, w_value, w_out):
    slices, tokens, width = patches.shape
    cols = w_query.shape[1]
    chunk = CHUNK
    far = (patches, w_query, w_key, w_value, w_out, cls_rows)
    hbm = pl.BlockSpec(memory_space=pltpu.HBM)
    vmem = pl.BlockSpec(memory_space=pltpu.VMEM)
    out_shape = [
        in_vmem(patches.shape, BF16),
        in_vmem(w_key.shape, BF16),
        in_vmem(w_value.shape, BF16),
        in_vmem(w_out.shape, BF16),
        in_vmem((slices, SLOT, tokens), F32),
        in_vmem((2 * slices, tokens), F32),
        in_vmem((slices, width), BF16),
        in_vmem((slices, width), BF16),
        in_vmem((slices * SLOT, width), F32),
        in_vmem((2 * slices, cols), F32),
    ]
    return pl.pallas_call(
        functools.partial(forward_kernel, chunk),
        in_specs=[hbm] * len(far),
        out_specs=[vmem] * len(out_shape),
        out_shape=out_shape,
        scratch_shapes=[
            pltpu.VMEM(cls_rows.shape, BF16),
            pltpu.VMEM(w_query.shape, BF16),
            pltpu.VMEM((slices, 2 * SLOT, width), BF16),
            pltpu.SemaphoreType.DMA((5,)),
            pltpu.SemaphoreType.DMA((slices // chunk,)),
        ],
        compiler_params=pltpu.CompilerParams(vmem_limit_bytes=VMEM_LIMIT),
        name="encoder_forward",
    )(*[pltpu.with_memory_space_constraint(a, pltpu.HBM) for a in far])


def turn_kernel(patches, turned):
    for z in range(patches.shape[0]):
        turned[z] = patches[z].T


def turn_patches(patches):
    slices, tokens, width = patches.shape
    vmem = pl.BlockSpec(memory_space=pltpu.VMEM)
    return pl.pallas_call(
        turn_kernel,
        in_specs=[vmem],
        out_specs=vmem,
        out_shape=in_vmem((slices, width, tokens), BF16),
        compiler_params=pltpu.CompilerParams(vmem_limit_bytes=VMEM_LIMIT),
        name="turn_patches",
    )(patches)


def head_rows(x, heads):
    rows, cols = x.shape
    wide = (heads * rows, cols)
    mine = (
        lax.broadcasted_iota(jnp.int32, wide, 0) // rows
        == lax.broadcasted_iota(jnp.int32, wide, 1) // HD
    )
    tall = jnp.broadcast_to(x.astype(F32)[None], (heads, rows, cols)).reshape(wide)
    return jnp.where(mine, tall, 0.0).astype(BF16), mine


def prepare_kernel(heads, slices, ids, up, a_out, factor, pooled, d_wide, bias, turned, early):
    value_factor = factor[...]
    turned[...] = jnp.concatenate([jnp.zeros_like(value_factor), value_factor], axis=0).T
    early[...] = lane_blocks(pooled[...]).astype(BF16)
    rows = 2 * slices
    total = ids.shape[0]
    start = (lax.axis_index("gz") * lax.axis_size("dev") + lax.axis_index("dev")) * slices
    d_pooled = dot(up[...], a_out[...], BY_COLS).astype(BF16)
    d_wide[...] = head_rows(d_pooled, heads)[0]
    square = (heads * rows, rows)
    i_of = lax.broadcasted_iota(jnp.int32, square, 0) % rows
    j_of = lax.broadcasted_iota(jnp.int32, square, 1)
    id_i = jnp.full(square, -1, jnp.int32)
    id_j = jnp.full(square, -1, jnp.int32)
    for n in range(rows):
        place = start + n
        scan = jnp.where(place < total, ids[jnp.minimum(place, total - 1)], -1)
        id_i = jnp.where(i_of == n, scan, id_i)
        id_j = jnp.where(j_of == n, scan, id_j)
    allowed = ((id_i == id_j) & (id_j >= 0)) | (i_of == j_of)
    bias[...] = jnp.where(allowed, 1.0, 0.0)


def prepare_window(ids, up, a_out, factor, pooled, slices):
    cols = a_out.shape[0]
    width = a_out.shape[1]
    heads = cols // HD
    rows = 2 * slices
    vmem = pl.BlockSpec(memory_space=pltpu.VMEM)
    return pl.pallas_call(
        functools.partial(prepare_kernel, heads, slices),
        in_specs=[pl.BlockSpec(memory_space=pltpu.SMEM)] + [vmem] * 4,
        out_specs=[vmem] * 4,
        out_shape=[
            in_vmem((heads * rows, cols), BF16),
            in_vmem((heads * rows, rows), F32),
            in_vmem((width, 2 * slices * SLOT), F32),
            in_vmem((2 * slices * pl.cdiv(cols, LANES), LANES), BF16),
        ],
        compiler_params=pltpu.CompilerParams(vmem_limit_bytes=VMEM_LIMIT),
        name="prepare_window",
    )(ids, up, a_out, factor, pooled)


def choose(within, across, inside, edge):
    across = jnp.where(edge, 0.0, across.astype(F32))
    return jnp.where(inside, within.astype(F32), across)


def window_kernel(heads, own, within, across, a_query, a_key, a_value, d_wide, allowed, d_half):
    scale = float(HD) ** (-0.5)
    last = lax.axis_index("gz") == lax.axis_size("gz") - 1
    following = choose(within[...], across[...], lax.axis_index("dev") == 0, last)
    window = jnp.concatenate([own[...].astype(F32), following], axis=0)
    rows = window.shape[0]
    cols = a_query.shape[1]
    half = normalize(window)[0].astype(BF16)
    q_wide, mine = head_rows(dot(half, a_query[...]).astype(BF16), heads)
    k = dot(half, a_key[...]).astype(BF16)
    v = dot(half, a_value[...]).astype(BF16)
    scores = jnp.where(allowed[...] > 0.5, dot(q_wide, k, BY_COLS) * scale, -1e30)
    d_probs = dot(d_wide[...], v, BY_COLS)
    powers = jnp.exp(scores - jnp.max(scores, axis=-1, keepdims=True))
    probs = powers / jnp.sum(powers, axis=-1, keepdims=True)
    inner = jnp.sum(probs * d_probs, axis=-1, keepdims=True)
    d_scores = (probs * (d_probs - inner) * scale).astype(BF16)
    d_value = dot(probs.astype(BF16), d_wide[...], BY_ROWS).astype(BF16)
    d_query = jnp.where(mine, dot(d_scores, k), 0.0)
    d_query = jnp.sum(d_query.reshape(heads, rows, cols), axis=0).astype(BF16)
    d_key = dot(d_scores, q_wide, BY_ROWS).astype(BF16)
    terms = (
        dot(d_value, a_value[...], BY_COLS)
        + dot(d_query, a_query[...], BY_COLS)
        + dot(d_key, a_key[...], BY_COLS)
    )
    d_half[...] = terms.astype(BF16)


def window_gradients(own, within, across, a_query, a_key, a_value, d_wide, allowed):
    slices, width = own.shape
    heads = a_query.shape[1] // HD
    vmem = pl.BlockSpec(memory_space=pltpu.VMEM)
    return pl.pallas_call(
        functools.partial(window_kernel, heads),
        in_specs=[vmem] * 8,
        out_specs=vmem,
        out_shape=in_vmem((2 * slices, width), BF16),
        compiler_params=pltpu.CompilerParams(vmem_limit_bytes=VMEM_LIMIT),
        name="window_gradients",
    )(own, within, across, a_query, a_key, a_value, d_wide, allowed)


def backward_kernel(
    chips,
    patches,
    patches_turned,
    probs,
    stats,
    d_own,
    d_others,
    within,
    across,
    embedded,
    up,
    w_key,
    w_value,
    w_out,
    cls_norm,
    turned_value,
    early,
    *rest,
):
    outs, (turned, d_keys, factor) = rest[:chips], rest[chips:]
    scale = float(HD) ** (-0.5)
    slices = embedded.shape[0]

    carried = choose(
        within[...], across[...], lax.axis_index("dev") == 1, lax.axis_index("gz") == 0
    )
    win_norm, inv_std = normalize(embedded[...].astype(F32))
    d_normed = d_own[:slices].astype(F32) + carried[:slices]
    for n in range(d_others.shape[0]):
        d_normed = d_normed + d_others[n, :slices].astype(F32)
    centred = (
        d_normed
        - jnp.mean(d_normed, axis=-1, keepdims=True)
        - win_norm * jnp.mean(d_normed * win_norm, axis=-1, keepdims=True)
    )
    d_embed = up[:slices].astype(F32) + carried[slices:] + inv_std * centred
    d_embed = d_embed.astype(BF16)
    d_att = dot(d_embed, w_out[...], BY_COLS).astype(BF16)
    keys = dot(expand(d_att), w_value[...], BY_COLS).astype(BF16).astype(F32)
    key_sums = jnp.sum(keys, axis=-1, keepdims=True)
    d_keys[...] = keys

    def score(z):
        return dot(d_keys[z * SLOT : (z + 1) * SLOT].astype(BF16), patches_turned[z])

    def attend(z, raw):
        here = slice(z * SLOT, (z + 1) * SLOT)
        p = probs[z]
        mean = stats[z : z + 1]
        inv = stats[slices + z : slices + z + 1]
        d_probs = inv * (raw - mean * key_sums[here])
        inner = jnp.sum(p * d_probs, axis=-1, keepdims=True)
        d_scores = (p * (d_probs - inner) * scale).astype(BF16)
        weights = (d_scores.astype(F32) * inv).astype(BF16)
        shift = jnp.sum(weights.astype(F32) * mean, axis=-1, keepdims=True)
        factor[here] = dot(weights, patches[z]) - shift

    waiting = []
    for c in range(0, slices, CHUNK):
        ready = [(z, score(z)) for z in range(c, c + CHUNK)]
        for item in waiting:
            attend(*item)
        waiting = ready
    for item in waiting:
        attend(*item)

    key_factor = factor[...]
    d_query = collapse(dot(key_factor.astype(BF16), w_key[...])).astype(BF16)
    slot = lax.broadcasted_iota(jnp.int32, key_factor.shape, 0) % SLOT
    left = jnp.where(slot == SLOT - 2, slot_rows(cls_norm[...]), key_factor)
    left = jnp.where(slot == SLOT - 1, slot_rows(d_embed), left)
    right = jnp.concatenate([d_att.astype(F32), d_query.astype(F32)], axis=0)
    turned[...] = jnp.concatenate([left, jnp.zeros_like(left)], axis=0).T + turned_value[...]
    late = lane_blocks(right).astype(BF16)
    part = turned.shape[0] // chips
    middle = part + late.shape[0]
    here = lax.axis_index("gz")
    for shift in range(chips):
        first = pl.multiple_of(partner(here, shift, chips) * part, SLOT)
        outs[shift][:part] = turned[pl.ds(first, part), :].astype(BF16)
        outs[shift][part:middle] = late
        outs[shift][middle:] = early[...]


def encoder_backward(
    patches, patches_turned, probs, stats, d_own, d_others, within, across, embedded, up, w_key, w_value, w_out,
    cls_norm, turned_value, early, chips,
):
    slices, tokens, width = patches.shape
    cols = w_key.shape[1]
    vmem = pl.BlockSpec(memory_space=pltpu.VMEM)
    message = (width // chips + 4 * slices * pl.cdiv(cols, LANES), LANES)
    return pl.pallas_call(
        functools.partial(backward_kernel, chips),
        in_specs=[vmem] * 16,
        out_specs=[vmem] * chips,
        out_shape=[in_vmem(message, BF16)] * chips,
        scratch_shapes=[
            pltpu.VMEM((width, LANES), F32),
            pltpu.VMEM((slices * SLOT, width), F32),
            pltpu.VMEM((slices * SLOT, width), F32),
        ],
        compiler_params=pltpu.CompilerParams(vmem_limit_bytes=VMEM_LIMIT),
        name="encoder_backward",
    )(
        patches, patches_turned, probs, stats, d_own, d_others, within, across, embedded, up, w_key, w_value, w_out,
        cls_norm, turned_value, early,
    )


def assemble_kernel(slices, cols, part, chips, *refs):
    messages, (kept, sent) = refs[:chips], refs[chips:]
    mask = head_mask(slices, cols)
    slot = lax.broadcasted_iota(jnp.int32, mask.shape, 0) % SLOT
    depth = slices * SLOT
    rows = 2 * slices * pl.cdiv(cols, LANES)

    def stacked(columns):
        blocks = [m[:part, columns].astype(F32) for m in messages]
        return jnp.concatenate(blocks, axis=1).astype(BF16)

    first, second = [], []
    for m in messages:
        for start, into in ((part, second), (part + rows, first)):
            block = from_lane_blocks(m[start : start + rows].astype(F32), cols)
            into.append([slot_rows(block[:slices]), slot_rows(block[slices:])])
    left_key, left_value = stacked(slice(0, depth)), stacked(slice(depth, 2 * depth))

    def right(blocks):
        return jnp.concatenate(blocks, axis=0).astype(BF16)

    grads = [
        dot(left_key, right([jnp.where(slot == SLOT - 2, b[1], 0.0) for b in second])),
        dot(left_key, right([jnp.where(mask, b[0], 0.0) for b in first])),
        dot(left_value, right([jnp.where(mask, b[0], 0.0) for b in second])),
        dot(left_key, right([jnp.where(slot == SLOT - 1, b[1], 0.0) for b in first])),
    ]
    lower = lax.axis_index("dev") == 0
    half = part // 2
    for n, total in enumerate(grads):
        top, bottom = total[:half], total[half:]
        kept[n] = jnp.where(lower, top, bottom)
        sent[n] = jnp.where(lower, bottom, top).astype(BF16)


def assemble(messages, slices, cols, part):
    vmem = pl.BlockSpec(memory_space=pltpu.VMEM)
    shape = (4, part // 2, cols)
    return pl.pallas_call(
        functools.partial(assemble_kernel, slices, cols, part, len(messages)),
        in_specs=[vmem] * len(messages),
        out_specs=[vmem, vmem],
        out_shape=[in_vmem(shape, F32), in_vmem(shape, BF16)],
        compiler_params=pltpu.CompilerParams(vmem_limit_bytes=VMEM_LIMIT),
        name="assemble",
    )(*messages)


def finish_kernel(kept, arrived, *refs):
    outs, sums, sems = refs[:4], refs[4], refs[5]
    copies = []
    for n, out in enumerate(outs):
        sums[n] = kept[n] + arrived[n].astype(F32)
        copy = pltpu.make_async_copy(sums.at[n], out, sems.at[n])
        copy.start()
        copies.append(copy)
    for copy in copies:
        copy.wait()


def finish(kept, arrived):
    vmem = pl.BlockSpec(memory_space=pltpu.VMEM)
    return pl.pallas_call(
        finish_kernel,
        in_specs=[vmem, vmem],
        out_specs=[pl.BlockSpec(memory_space=pltpu.HBM)] * 4,
        out_shape=[pltpu.HBM(kept.shape[1:], F32)] * 4,
        scratch_shapes=[pltpu.VMEM(kept.shape, F32), pltpu.SemaphoreType.DMA((4,))],
        compiler_params=pltpu.CompilerParams(vmem_limit_bytes=VMEM_LIMIT),
        name="finish",
    )(kept, arrived)


def ring_shift(x, axis, distance):
    size = lax.axis_size(axis)
    return lax.ppermute(x, axis, [(i, (i + distance) % size) for i in range(size)])


def others(x):
    return [ring_shift(x, "ma", d) for d in range(1, lax.axis_size("ma"))]


def pair_route():
    chips, parts, cores = [lax.axis_size(a) for a in ("gz", "ma", "dev")]
    route = []
    for chip in range(chips):
        for part in range(parts):
            for core in range(cores):
                place = chip * cores + core
                other = place + 1 if core else place - 1
                at = part
                if not 0 <= other < chips * cores:
                    other, at = place, part ^ 1
                    if at >= parts:
                        continue
                source = (chip * parts + part) * cores + core
                route.append((source, (other // cores * parts + at) * cores + other % cores))
    return route


def neighbours(block):
    within = ring_shift(block, "dev", 1)
    return within, lax.ppermute(block, ("gz", "ma", "dev"), pair_route())


def exchanged(x, axis, shift):
    size = lax.axis_size(axis)
    return lax.ppermute(x, axis, [(i, partner(i, shift, size)) for i in range(size)])


def local(
    patches,
    cls_rows,
    w_query,
    w_key,
    w_value,
    w_out,
    a_query,
    a_key,
    a_value,
    a_out,
    upstream,
    slice_to_scan,
):
    slices, _, width = patches.shape
    cols = w_query.shape[1]
    chips = lax.axis_size("gz")
    up = upstream[0]
    (
        held, key_held, value_held, out_held, probs, stats, cls_norm, head_terms, factor, pooled
    ) = encoder_forward(patches, cls_rows, w_query, w_key, w_value, w_out)
    held_turned = turn_patches(held)
    d_wide, allowed, turned_value, early = prepare_window(
        slice_to_scan, up, a_out, factor, pooled, slices
    )
    total = head_terms.astype(F32)
    arriving = others(head_terms)
    arriving, held_turned = lax.optimization_barrier((arriving, held_turned))
    for term in arriving:
        total = total + term.astype(F32)
    embedded = (cls_rows.astype(F32) + total).astype(BF16)
    following = neighbours(embedded)
    d_own = window_gradients(embedded, *following, a_query, a_key, a_value, d_wide, allowed)
    d_others = jnp.stack(others(d_own))
    lower = d_own[slices:].astype(F32)
    for n in range(d_others.shape[0]):
        lower = lower + d_others[n, slices:].astype(F32)
    carried = neighbours(jnp.concatenate([lower.astype(BF16), up[slices:]], axis=0))
    messages = encoder_backward(
        held, held_turned, probs, stats, d_own, d_others, *carried, embedded, up, key_held, value_held, out_held,
        cls_norm, turned_value, early, chips,
    )
    order = range(chips - 1, 0, -1)
    arrived = list(messages[:1]) + [exchanged(messages[n], "gz", n) for n in order]
    kept, sent = assemble(arrived, slices, cols, width // chips)
    return tuple(finish(kept, ring_shift(sent, "dev", 1)))


def solution(mesh):
    return jax.shard_map(
        local,
        mesh=mesh,
        in_specs=(
            P(("grp", "gz", "dev"), None, None),
            P(("grp", "gz", "dev"), None),
            P(None, "ma"),
            P(None, "ma"),
            P(None, "ma"),
            P("ma", None),
            P(None, "ma"),
            P(None, "ma"),
            P(None, "ma"),
            P("ma", None),
            P(("grp", "gz", "dev"), None, None),
            P("grp"),
        ),
        out_specs=(
            P(("grp", "gz", "dev"), "ma"),
            P(("grp", "gz", "dev"), "ma"),
            P(("grp", "gz", "dev"), "ma"),
            P(("grp", "gz", "dev"), "ma"),
        ),
        check_vma=False,
    )
```

```python
import functools

import jax
import jax.numpy as jnp
from jax import lax
from jax.experimental import pallas as pl
from jax.experimental.pallas import tpu as pltpu
from jax.sharding import PartitionSpec as P

HD = 64
SLOT = 8
LANES = 128
F32 = jnp.float32
BF16 = jnp.bfloat16
CHUNK = 2
VMEM_LIMIT = 16 * 1024 * 1024


def dot(a, b, dims=((1,), (0,))):
    return lax.dot_general(a, b, (dims, ((), ())), preferred_element_type=F32)


BY_COLS = ((1,), (1,))
BY_ROWS = ((0,), (0,))


def normalize(values):
    row_mean = jnp.mean(values, axis=-1, keepdims=True)
    centred = values - row_mean
    variance = jnp.mean(centred * centred, axis=-1, keepdims=True)
    inv_std = lax.rsqrt(variance + 1e-05)
    return centred * inv_std, inv_std


def head_mask(slices, cols):
    shape = (slices * SLOT, cols)
    row = lax.broadcasted_iota(jnp.int32, shape, 0)
    col = lax.broadcasted_iota(jnp.int32, shape, 1)
    return row % SLOT == col // HD


def slot_rows(rows):
    slices, cols = rows.shape
    wide = jnp.broadcast_to(rows.astype(F32)[:, None, :], (slices, SLOT, cols))
    return wide.reshape(slices * SLOT, cols)


def expand(rows):
    wide = slot_rows(rows)
    return jnp.where(head_mask(rows.shape[0], rows.shape[1]), wide, 0.0).astype(BF16)


def collapse(full):
    rows, cols = full.shape
    kept = jnp.where(head_mask(rows // SLOT, cols), full, 0.0)
    return jnp.sum(kept.reshape(rows // SLOT, SLOT, cols), axis=1)


def in_vmem(shape, dtype):
    return pltpu.VMEM(shape, dtype)


def lane_blocks(rows):
    cols = rows.shape[1]
    spare = -cols % LANES
    if spare:
        rows = jnp.concatenate([rows, jnp.zeros((rows.shape[0], spare), rows.dtype)], axis=1)
    return jnp.concatenate(
        [rows[:, b : b + LANES] for b in range(0, cols + spare, LANES)], axis=0
    )


def from_lane_blocks(rows, cols):
    count = rows.shape[0] // pl.cdiv(cols, LANES)
    blocks = [rows[b : b + count] for b in range(0, rows.shape[0], count)]
    return jnp.concatenate(blocks, axis=1)[:, :cols]


def partner(here, shift, chips):
    return here ^ shift if chips & (chips - 1) == 0 else (here + shift) % chips


def forward_kernel(
    chunk,
    patches_hbm,
    w_query_hbm,
    w_key_hbm,
    w_value_hbm,
    w_out_hbm,
    cls_hbm,
    patches,
    w_key,
    w_value,
    w_out,
    probs,
    stats,
    cls_norm,
    head_terms,
    factor,
    pooled,
    cls_rows,
    w_query,
    query_keys,
    sems,
    patch_sems,
):
    slices, tokens, width = patches.shape
    scale = float(HD) ** (-0.5)

    def fetch(source, target, n):
        copy = pltpu.make_async_copy(source, target, sems.at[n])
        copy.start()
        return copy

    get_rows = fetch(cls_hbm, cls_rows, 4)
    get_query = fetch(w_query_hbm, w_query, 0)
    get_key = fetch(w_key_hbm, w_key, 1)
    get_patches = []
    for c in range(slices // chunk):
        part = pl.ds(c * chunk, chunk)
        copy = pltpu.make_async_copy(patches_hbm.at[part], patches.at[part], patch_sems.at[c])
        copy.start()
        get_patches.append(copy)
    get_value = fetch(w_value_hbm, w_value, 2)
    get_out = fetch(w_out_hbm, w_out, 3)

    def spread(z):
        wide = patches[z].astype(F32)
        first = wide[:, 0:1]
        squares = None
        for b in range(0, width, LANES):
            off = wide[:, b : b + LANES] - first
            squares = off * off if squares is None else squares + off * off
        return jnp.sum(squares.T, axis=0, keepdims=True)

    groups = [range(z, z + chunk) for z in range(0, slices, chunk)]
    get_rows.wait()
    rows = normalize(cls_rows[...].astype(F32))[0].astype(BF16)
    cls_norm[...] = rows
    get_query.wait()
    get_key.wait()
    get_patches[0].wait()
    totals = {z: spread(z) for z in groups[0]}
    q = dot(rows, w_query[...]).astype(BF16)
    keys = (dot(expand(q), w_key[...], BY_COLS) * scale).astype(BF16).astype(F32)
    key_sums = jnp.sum(keys, axis=-1, keepdims=True)
    place = lax.broadcasted_iota(jnp.int32, (SLOT, width), 0)
    entry = lax.broadcasted_iota(jnp.int32, (SLOT, width), 1)
    picks = jnp.where((place == 0) | ((place == 1) & (entry == 0)), 1.0, 0.0)
    for z in range(slices):
        query_keys[z] = jnp.concatenate(
            [keys[z * SLOT : (z + 1) * SLOT], picks], axis=0
        ).astype(BF16)

    def attend(z, raw, total):
        mean = raw[SLOT : SLOT + 1] * (1.0 / width)
        off = mean - raw[SLOT + 1 : SLOT + 2]
        inv_std = lax.rsqrt(jnp.maximum(total * (1.0 / width) - off * off, 0.0) + 1e-05)
        stats[z : z + 1] = mean
        stats[slices + z : slices + z + 1] = inv_std
        here = slice(z * SLOT, (z + 1) * SLOT)
        scores = inv_std * (raw[:SLOT] - mean * key_sums[here])
        powers = jnp.exp(scores - jnp.max(scores, axis=-1, keepdims=True))
        p = powers / jnp.sum(powers, axis=-1, keepdims=True)
        probs[z] = p
        weights = (p.astype(BF16).astype(F32) * inv_std).astype(BF16)
        shift = jnp.sum(weights.astype(F32) * mean, axis=-1, keepdims=True)
        return weights, shift

    def gather(z, weights, shift):
        factor[z * SLOT : (z + 1) * SLOT] = dot(weights, patches[z]) - shift

    waiting, weighted = [], []
    for g, group in enumerate(groups):
        if g + 1 < len(groups):
            get_patches[g + 1].wait()
        ready = [(z, dot(query_keys[z], patches[z], BY_COLS)) for z in group]
        if g + 1 < len(groups):
            totals.update({z: spread(z) for z in groups[g + 1]})
        for item in weighted:
            gather(*item)
        weighted = [(z,) + attend(z, raw, totals[z]) for z, raw in waiting]
        waiting = ready
    get_value.wait()
    get_out.wait()
    for item in weighted + [(z,) + attend(z, raw, totals[z]) for z, raw in waiting]:
        gather(*item)

    value_factor = factor[...]
    pool = collapse(dot(value_factor.astype(BF16), w_value[...])).astype(BF16)
    head_terms[...] = dot(pool, w_out[...]).astype(BF16)
    pooled[...] = jnp.concatenate([q.astype(F32), pool.astype(F32)], axis=0)


def encoder_forward(patches, cls_rows, w_query, w_key, w_value, w_out):
    slices, tokens, width = patches.shape
    cols = w_query.shape[1]
    chunk = CHUNK
    far = (patches, w_query, w_key, w_value, w_out, cls_rows)
    hbm = pl.BlockSpec(memory_space=pltpu.HBM)
    vmem = pl.BlockSpec(memory_space=pltpu.VMEM)
    out_shape = [
        in_vmem(patches.shape, BF16),
        in_vmem(w_key.shape, BF16),
        in_vmem(w_value.shape, BF16),
        in_vmem(w_out.shape, BF16),
        in_vmem((slices, SLOT, tokens), F32),
        in_vmem((2 * slices, tokens), F32),
        in_vmem((slices, width), BF16),
        in_vmem((slices, width), BF16),
        in_vmem((slices * SLOT, width), F32),
        in_vmem((2 * slices, cols), F32),
    ]
    return pl.pallas_call(
        functools.partial(forward_kernel, chunk),
        in_specs=[hbm] * len(far),
        out_specs=[vmem] * len(out_shape),
        out_shape=out_shape,
        scratch_shapes=[
            pltpu.VMEM(cls_rows.shape, BF16),
            pltpu.VMEM(w_query.shape, BF16),
            pltpu.VMEM((slices, 2 * SLOT, width), BF16),
            pltpu.SemaphoreType.DMA((5,)),
            pltpu.SemaphoreType.DMA((slices // chunk,)),
        ],
        compiler_params=pltpu.CompilerParams(vmem_limit_bytes=VMEM_LIMIT),
        name="encoder_forward",
    )(*[pltpu.with_memory_space_constraint(a, pltpu.HBM) for a in far])


def sent_early(chips):
    return [chips // 2]


def halves(block):
    middle = block.shape[0] // 2
    return jnp.concatenate([block[:middle], block[middle:]], axis=1)


def from_halves(block):
    width = block.shape[1] // 2
    return jnp.concatenate([block[:, :width], block[:, width:]], axis=0)


def turn_kernel(patches, turned):
    for z in range(patches.shape[0]):
        turned[z] = patches[z].T


def turn_patches(patches):
    slices, tokens, width = patches.shape
    vmem = pl.BlockSpec(memory_space=pltpu.VMEM)
    return pl.pallas_call(
        turn_kernel,
        in_specs=[vmem],
        out_specs=vmem,
        out_shape=in_vmem((slices, width, tokens), BF16),
        compiler_params=pltpu.CompilerParams(vmem_limit_bytes=VMEM_LIMIT),
        name="turn_patches",
    )(patches)


def head_rows(x, heads):
    rows, cols = x.shape
    wide = (heads * rows, cols)
    mine = (
        lax.broadcasted_iota(jnp.int32, wide, 0) // rows
        == lax.broadcasted_iota(jnp.int32, wide, 1) // HD
    )
    tall = jnp.broadcast_to(x.astype(F32)[None], (heads, rows, cols)).reshape(wide)
    return jnp.where(mine, tall, 0.0).astype(BF16), mine


def prepare_kernel(
    heads, slices, chips, ids, up, a_out, factor, pooled, d_wide, bias, turned, early, *outs
):
    value_factor = factor[...]
    turned[...] = jnp.concatenate([jnp.zeros_like(value_factor), value_factor], axis=0).T
    rows_early = lane_blocks(pooled[...]).astype(BF16)
    early[...] = rows_early
    part = turned.shape[0] // chips
    here = lax.axis_index("gz")
    for shift, out in zip(sent_early(chips), outs):
        first = pl.multiple_of(partner(here, shift, chips) * part, SLOT)
        out[: part // 2] = halves(turned[pl.ds(first, part), slices * SLOT :]).astype(BF16)
        out[part // 2 :] = rows_early
    rows = 2 * slices
    total = ids.shape[0]
    start = (lax.axis_index("gz") * lax.axis_size("dev") + lax.axis_index("dev")) * slices
    d_pooled = dot(up[...], a_out[...], BY_COLS).astype(BF16)
    d_wide[...] = head_rows(d_pooled, heads)[0]
    square = (heads * rows, rows)
    i_of = lax.broadcasted_iota(jnp.int32, square, 0) % rows
    j_of = lax.broadcasted_iota(jnp.int32, square, 1)
    id_i = jnp.full(square, -1, jnp.int32)
    id_j = jnp.full(square, -1, jnp.int32)
    for n in range(rows):
        place = start + n
        scan = jnp.where(place < total, ids[jnp.minimum(place, total - 1)], -1)
        id_i = jnp.where(i_of == n, scan, id_i)
        id_j = jnp.where(j_of == n, scan, id_j)
    allowed = ((id_i == id_j) & (id_j >= 0)) | (i_of == j_of)
    bias[...] = jnp.where(allowed, 1.0, 0.0)


def prepare_window(ids, up, a_out, factor, pooled, slices, chips):
    cols = a_out.shape[0]
    width = a_out.shape[1]
    heads = cols // HD
    rows = 2 * slices
    below = rows * pl.cdiv(cols, LANES)
    vmem = pl.BlockSpec(memory_space=pltpu.VMEM)
    return pl.pallas_call(
        functools.partial(prepare_kernel, heads, slices, chips),
        in_specs=[pl.BlockSpec(memory_space=pltpu.SMEM)] + [vmem] * 4,
        out_specs=[vmem] * (4 + len(sent_early(chips))),
        out_shape=[
            in_vmem((heads * rows, cols), BF16),
            in_vmem((heads * rows, rows), F32),
            in_vmem((width, 2 * slices * SLOT), F32),
            in_vmem((below, LANES), BF16),
        ]
        + [in_vmem((width // chips // 2 + below, LANES), BF16)] * len(sent_early(chips)),
        compiler_params=pltpu.CompilerParams(vmem_limit_bytes=VMEM_LIMIT),
        name="prepare_window",
    )(ids, up, a_out, factor, pooled)


def choose(within, across, inside, edge):
    across = jnp.where(edge, 0.0, across.astype(F32))
    return jnp.where(inside, within.astype(F32), across)


def window_kernel(heads, own, within, across, a_query, a_key, a_value, d_wide, allowed, d_half):
    scale = float(HD) ** (-0.5)
    last = lax.axis_index("gz") == lax.axis_size("gz") - 1
    following = choose(within[...], across[...], lax.axis_index("dev") == 0, last)
    window = jnp.concatenate([own[...].astype(F32), following], axis=0)
    rows = window.shape[0]
    cols = a_query.shape[1]
    half = normalize(window)[0].astype(BF16)
    q_wide, mine = head_rows(dot(half, a_query[...]).astype(BF16), heads)
    k = dot(half, a_key[...]).astype(BF16)
    v = dot(half, a_value[...]).astype(BF16)
    scores = jnp.where(allowed[...] > 0.5, dot(q_wide, k, BY_COLS) * scale, -1e30)
    d_probs = dot(d_wide[...], v, BY_COLS)
    powers = jnp.exp(scores - jnp.max(scores, axis=-1, keepdims=True))
    probs = powers / jnp.sum(powers, axis=-1, keepdims=True)
    inner = jnp.sum(probs * d_probs, axis=-1, keepdims=True)
    d_scores = (probs * (d_probs - inner) * scale).astype(BF16)
    d_value = dot(probs.astype(BF16), d_wide[...], BY_ROWS).astype(BF16)
    d_query = jnp.where(mine, dot(d_scores, k), 0.0)
    d_query = jnp.sum(d_query.reshape(heads, rows, cols), axis=0).astype(BF16)
    d_key = dot(d_scores, q_wide, BY_ROWS).astype(BF16)
    terms = (
        dot(d_value, a_value[...], BY_COLS)
        + dot(d_query, a_query[...], BY_COLS)
        + dot(d_key, a_key[...], BY_COLS)
    )
    d_half[...] = terms.astype(BF16)


def window_gradients(own, within, across, a_query, a_key, a_value, d_wide, allowed):
    slices, width = own.shape
    heads = a_query.shape[1] // HD
    vmem = pl.BlockSpec(memory_space=pltpu.VMEM)
    return pl.pallas_call(
        functools.partial(window_kernel, heads),
        in_specs=[vmem] * 8,
        out_specs=vmem,
        out_shape=in_vmem((2 * slices, width), BF16),
        compiler_params=pltpu.CompilerParams(vmem_limit_bytes=VMEM_LIMIT),
        name="window_gradients",
    )(own, within, across, a_query, a_key, a_value, d_wide, allowed)


def backward_kernel(
    chips,
    patches,
    patches_turned,
    probs,
    stats,
    d_own,
    d_others,
    within,
    across,
    embedded,
    up,
    w_key,
    w_value,
    w_out,
    cls_norm,
    turned_value,
    early,
    *rest,
):
    outs, (turned, d_keys, factor) = rest[:chips], rest[chips:]
    scale = float(HD) ** (-0.5)
    slices = embedded.shape[0]

    carried = choose(
        within[...], across[...], lax.axis_index("dev") == 1, lax.axis_index("gz") == 0
    )
    win_norm, inv_std = normalize(embedded[...].astype(F32))
    d_normed = d_own[:slices].astype(F32) + carried[:slices]
    for n in range(d_others.shape[0]):
        d_normed = d_normed + d_others[n, :slices].astype(F32)
    centred = (
        d_normed
        - jnp.mean(d_normed, axis=-1, keepdims=True)
        - win_norm * jnp.mean(d_normed * win_norm, axis=-1, keepdims=True)
    )
    d_embed = up[:slices].astype(F32) + carried[slices:] + inv_std * centred
    d_embed = d_embed.astype(BF16)
    d_att = dot(d_embed, w_out[...], BY_COLS).astype(BF16)
    keys = dot(expand(d_att), w_value[...], BY_COLS).astype(BF16).astype(F32)
    key_sums = jnp.sum(keys, axis=-1, keepdims=True)
    d_keys[...] = keys

    def score(z):
        return dot(d_keys[z * SLOT : (z + 1) * SLOT].astype(BF16), patches_turned[z])

    def attend(z, raw):
        here = slice(z * SLOT, (z + 1) * SLOT)
        p = probs[z]
        mean = stats[z : z + 1]
        inv = stats[slices + z : slices + z + 1]
        d_probs = inv * (raw - mean * key_sums[here])
        inner = jnp.sum(p * d_probs, axis=-1, keepdims=True)
        d_scores = (p * (d_probs - inner) * scale).astype(BF16)
        weights = (d_scores.astype(F32) * inv).astype(BF16)
        shift = jnp.sum(weights.astype(F32) * mean, axis=-1, keepdims=True)
        factor[here] = dot(weights, patches[z]) - shift

    waiting = []
    for c in range(0, slices, CHUNK):
        ready = [(z, score(z)) for z in range(c, c + CHUNK)]
        for item in waiting:
            attend(*item)
        waiting = ready
    for item in waiting:
        attend(*item)

    key_factor = factor[...]
    d_query = collapse(dot(key_factor.astype(BF16), w_key[...])).astype(BF16)
    slot = lax.broadcasted_iota(jnp.int32, key_factor.shape, 0) % SLOT
    left = jnp.where(slot == SLOT - 2, slot_rows(cls_norm[...]), key_factor)
    left = jnp.where(slot == SLOT - 1, slot_rows(d_embed), left)
    right = jnp.concatenate([d_att.astype(F32), d_query.astype(F32)], axis=0)
    turned[...] = jnp.concatenate([left, jnp.zeros_like(left)], axis=0).T + turned_value[...]
    late = lane_blocks(right).astype(BF16)
    part = turned.shape[0] // chips
    middle = part + late.shape[0]
    here = lax.axis_index("gz")
    for shift in range(chips):
        first = pl.multiple_of(partner(here, shift, chips) * part, SLOT)
        if shift in sent_early(chips):
            keyed = turned[pl.ds(first, part), : slices * SLOT]
            outs[shift][: part // 2] = halves(keyed).astype(BF16)
            outs[shift][part // 2 :] = late
            continue
        outs[shift][:part] = turned[pl.ds(first, part), :].astype(BF16)
        outs[shift][part:middle] = late
        outs[shift][middle:] = early[...]


def encoder_backward(
    patches, patches_turned, probs, stats, d_own, d_others, within, across, embedded, up, w_key, w_value, w_out,
    cls_norm, turned_value, early, chips,
):
    slices, tokens, width = patches.shape
    cols = w_key.shape[1]
    vmem = pl.BlockSpec(memory_space=pltpu.VMEM)
    below = 2 * slices * pl.cdiv(cols, LANES)
    short, full = (width // chips // 2 + below, LANES), (width // chips + 2 * below, LANES)
    shapes = [short if shift in sent_early(chips) else full for shift in range(chips)]
    return pl.pallas_call(
        functools.partial(backward_kernel, chips),
        in_specs=[vmem] * 16,
        out_specs=[vmem] * chips,
        out_shape=[in_vmem(shape, BF16) for shape in shapes],
        scratch_shapes=[
            pltpu.VMEM((width, LANES), F32),
            pltpu.VMEM((slices * SLOT, width), F32),
            pltpu.VMEM((slices * SLOT, width), F32),
        ],
        compiler_params=pltpu.CompilerParams(vmem_limit_bytes=VMEM_LIMIT),
        name="encoder_backward",
    )(
        patches, patches_turned, probs, stats, d_own, d_others, within, across, embedded, up, w_key, w_value, w_out,
        cls_norm, turned_value, early,
    )


def assemble_kernel(slices, cols, part, chips, *refs):
    *messages, kept, sent = refs
    messages, early = messages[:chips], dict(zip(sent_early(chips), messages[chips:]))
    mask = head_mask(slices, cols)
    slot = lax.broadcasted_iota(jnp.int32, mask.shape, 0) % SLOT
    depth = slices * SLOT
    rows = 2 * slices * pl.cdiv(cols, LANES)
    keyed, valued, first, second = [], [], [], []
    for shift, m in enumerate(messages):
        if shift in early:
            e = early[shift]
            keyed.append(from_halves(m[: part // 2].astype(F32)))
            valued.append(from_halves(e[: part // 2].astype(F32)))
            ends = ((m, part // 2, second), (e, part // 2, first))
        else:
            keyed.append(m[:part, :depth].astype(F32))
            valued.append(m[:part, depth:].astype(F32))
            ends = ((m, part, second), (m, part + rows, first))
        for source, start, into in ends:
            block = from_lane_blocks(source[start : start + rows].astype(F32), cols)
            into.append([slot_rows(block[:slices]), slot_rows(block[slices:])])
    left_key = jnp.concatenate(keyed, axis=1).astype(BF16)
    left_value = jnp.concatenate(valued, axis=1).astype(BF16)

    def right(blocks):
        return jnp.concatenate(blocks, axis=0).astype(BF16)

    grads = [
        dot(left_key, right([jnp.where(slot == SLOT - 2, b[1], 0.0) for b in second])),
        dot(left_key, right([jnp.where(mask, b[0], 0.0) for b in first])),
        dot(left_value, right([jnp.where(mask, b[0], 0.0) for b in second])),
        dot(left_key, right([jnp.where(slot == SLOT - 1, b[1], 0.0) for b in first])),
    ]
    lower = lax.axis_index("dev") == 0
    half = part // 2
    for n, total in enumerate(grads):
        top, bottom = total[:half], total[half:]
        kept[n] = jnp.where(lower, top, bottom)
        sent[n] = jnp.where(lower, bottom, top).astype(BF16)


def assemble(messages, early, slices, cols, part):
    vmem = pl.BlockSpec(memory_space=pltpu.VMEM)
    shape = (4, part // 2, cols)
    return pl.pallas_call(
        functools.partial(assemble_kernel, slices, cols, part, len(messages)),
        in_specs=[vmem] * (len(messages) + len(early)),
        out_specs=[vmem, vmem],
        out_shape=[in_vmem(shape, F32), in_vmem(shape, BF16)],
        compiler_params=pltpu.CompilerParams(vmem_limit_bytes=VMEM_LIMIT),
        name="assemble",
    )(*messages, *early)


def finish_kernel(kept, arrived, *refs):
    outs, sums, sems = refs[:4], refs[4], refs[5]
    copies = []
    for n, out in enumerate(outs):
        sums[n] = kept[n] + arrived[n].astype(F32)
        copy = pltpu.make_async_copy(sums.at[n], out, sems.at[n])
        copy.start()
        copies.append(copy)
    for copy in copies:
        copy.wait()


def finish(kept, arrived):
    vmem = pl.BlockSpec(memory_space=pltpu.VMEM)
    return pl.pallas_call(
        finish_kernel,
        in_specs=[vmem, vmem],
        out_specs=[pl.BlockSpec(memory_space=pltpu.HBM)] * 4,
        out_shape=[pltpu.HBM(kept.shape[1:], F32)] * 4,
        scratch_shapes=[pltpu.VMEM(kept.shape, F32), pltpu.SemaphoreType.DMA((4,))],
        compiler_params=pltpu.CompilerParams(vmem_limit_bytes=VMEM_LIMIT),
        name="finish",
    )(kept, arrived)


def ring_shift(x, axis, distance):
    size = lax.axis_size(axis)
    return lax.ppermute(x, axis, [(i, (i + distance) % size) for i in range(size)])


def others(x):
    return [ring_shift(x, "ma", d) for d in range(1, lax.axis_size("ma"))]


def pair_route():
    chips, parts, cores = [lax.axis_size(a) for a in ("gz", "ma", "dev")]
    route = []
    for chip in range(chips):
        for part in range(parts):
            for core in range(cores):
                place = chip * cores + core
                other = place + 1 if core else place - 1
                at = part
                if not 0 <= other < chips * cores:
                    other, at = place, part ^ 1
                    if at >= parts:
                        continue
                source = (chip * parts + part) * cores + core
                route.append((source, (other // cores * parts + at) * cores + other % cores))
    return route


def neighbours(block):
    within = ring_shift(block, "dev", 1)
    return within, lax.ppermute(block, ("gz", "ma", "dev"), pair_route())


def exchanged(x, axis, shift):
    size = lax.axis_size(axis)
    return lax.ppermute(x, axis, [(i, partner(i, shift, size)) for i in range(size)])


def local(
    patches,
    cls_rows,
    w_query,
    w_key,
    w_value,
    w_out,
    a_query,
    a_key,
    a_value,
    a_out,
    upstream,
    slice_to_scan,
):
    slices, _, width = patches.shape
    cols = w_query.shape[1]
    chips = lax.axis_size("gz")
    up = upstream[0]
    (
        held, key_held, value_held, out_held, probs, stats, cls_norm, head_terms, factor, pooled
    ) = encoder_forward(patches, cls_rows, w_query, w_key, w_value, w_out)
    held_turned = turn_patches(held)
    d_wide, allowed, turned_value, early, *ahead = prepare_window(
        slice_to_scan, up, a_out, factor, pooled, slices, chips
    )
    ahead = [exchanged(m, "gz", n) for n, m in zip(sent_early(chips), ahead)]
    total = head_terms.astype(F32)
    arriving = others(head_terms)
    arriving, held_turned = lax.optimization_barrier((arriving, held_turned))
    for term in arriving:
        total = total + term.astype(F32)
    embedded = (cls_rows.astype(F32) + total).astype(BF16)
    following = neighbours(embedded)
    d_own = window_gradients(embedded, *following, a_query, a_key, a_value, d_wide, allowed)
    d_others = others(d_own)
    d_others, ahead = lax.optimization_barrier((d_others, ahead))
    d_others = jnp.stack(d_others)
    lower = d_own[slices:].astype(F32)
    for n in range(d_others.shape[0]):
        lower = lower + d_others[n, slices:].astype(F32)
    carried = neighbours(jnp.concatenate([lower.astype(BF16), up[slices:]], axis=0))
    messages = encoder_backward(
        held, held_turned, probs, stats, d_own, d_others, *carried, embedded, up, key_held, value_held, out_held,
        cls_norm, turned_value, early, chips,
    )
    order = range(chips - 1, 0, -1)
    arrived = list(messages[:1]) + [exchanged(messages[n], "gz", n) for n in order]
    kept, sent = assemble(arrived, ahead, slices, cols, width // chips)
    return tuple(finish(kept, ring_shift(sent, "dev", 1)))


def solution(mesh):
    return jax.shard_map(
        local,
        mesh=mesh,
        in_specs=(
            P(("grp", "gz", "dev"), None, None),
            P(("grp", "gz", "dev"), None),
            P(None, "ma"),
            P(None, "ma"),
            P(None, "ma"),
            P("ma", None),
            P(None, "ma"),
            P(None, "ma"),
            P(None, "ma"),
            P("ma", None),
            P(("grp", "gz", "dev"), None, None),
            P("grp"),
        ),
        out_specs=(
            P(("grp", "gz", "dev"), "ma"),
            P(("grp", "gz", "dev"), "ma"),
            P(("grp", "gz", "dev"), "ma"),
            P(("grp", "gz", "dev"), "ma"),
        ),
        check_vma=False,
    )
```

```python
import functools

import jax
import jax.numpy as jnp
from jax import lax
from jax.experimental import pallas as pl
from jax.experimental.pallas import tpu as pltpu
from jax.sharding import PartitionSpec as P

HD = 64
SLOT = 8
LANES = 128
F32 = jnp.float32
BF16 = jnp.bfloat16
CHUNK = 2
VMEM_LIMIT = 16 * 1024 * 1024


def dot(a, b, dims=((1,), (0,))):
    return lax.dot_general(a, b, (dims, ((), ())), preferred_element_type=F32)


BY_COLS = ((1,), (1,))
BY_ROWS = ((0,), (0,))


def normalize(values):
    row_mean = jnp.mean(values, axis=-1, keepdims=True)
    centred = values - row_mean
    variance = jnp.mean(centred * centred, axis=-1, keepdims=True)
    inv_std = lax.rsqrt(variance + 1e-05)
    return centred * inv_std, inv_std


def head_mask(slices, cols):
    shape = (slices * SLOT, cols)
    row = lax.broadcasted_iota(jnp.int32, shape, 0)
    col = lax.broadcasted_iota(jnp.int32, shape, 1)
    return row % SLOT == col // HD


def slot_rows(rows):
    slices, cols = rows.shape
    wide = jnp.broadcast_to(rows.astype(F32)[:, None, :], (slices, SLOT, cols))
    return wide.reshape(slices * SLOT, cols)


def expand(rows):
    wide = slot_rows(rows)
    return jnp.where(head_mask(rows.shape[0], rows.shape[1]), wide, 0.0).astype(BF16)


def collapse(full):
    rows, cols = full.shape
    kept = jnp.where(head_mask(rows // SLOT, cols), full, 0.0)
    return jnp.sum(kept.reshape(rows // SLOT, SLOT, cols), axis=1)


def in_vmem(shape, dtype):
    return pltpu.VMEM(shape, dtype)


def lane_blocks(rows):
    cols = rows.shape[1]
    spare = -cols % LANES
    if spare:
        rows = jnp.concatenate([rows, jnp.zeros((rows.shape[0], spare), rows.dtype)], axis=1)
    return jnp.concatenate(
        [rows[:, b : b + LANES] for b in range(0, cols + spare, LANES)], axis=0
    )


def from_lane_blocks(rows, cols):
    count = rows.shape[0] // pl.cdiv(cols, LANES)
    blocks = [rows[b : b + count] for b in range(0, rows.shape[0], count)]
    return jnp.concatenate(blocks, axis=1)[:, :cols]


def partner(here, shift, chips):
    return here ^ shift if chips & (chips - 1) == 0 else (here + shift) % chips


def forward_kernel(
    chunk,
    patches_hbm,
    w_query_hbm,
    w_key_hbm,
    w_value_hbm,
    w_out_hbm,
    cls_hbm,
    patches,
    w_key,
    w_value,
    w_out,
    probs,
    stats,
    cls_norm,
    head_terms,
    factor,
    pooled,
    cls_rows,
    w_query,
    query_keys,
    sems,
    patch_sems,
):
    slices, tokens, width = patches.shape
    scale = float(HD) ** (-0.5)

    def fetch(source, target, n):
        copy = pltpu.make_async_copy(source, target, sems.at[n])
        copy.start()
        return copy

    get_rows = fetch(cls_hbm, cls_rows, 4)
    get_query = fetch(w_query_hbm, w_query, 0)
    get_key = fetch(w_key_hbm, w_key, 1)
    get_patches = []
    for c in range(slices // chunk):
        part = pl.ds(c * chunk, chunk)
        copy = pltpu.make_async_copy(patches_hbm.at[part], patches.at[part], patch_sems.at[c])
        copy.start()
        get_patches.append(copy)
    get_value = fetch(w_value_hbm, w_value, 2)
    get_out = fetch(w_out_hbm, w_out, 3)

    def spread(z):
        wide = patches[z].astype(F32)
        first = wide[:, 0:1]
        squares = None
        for b in range(0, width, LANES):
            off = wide[:, b : b + LANES] - first
            squares = off * off if squares is None else squares + off * off
        return jnp.sum(squares.T, axis=0, keepdims=True)

    groups = [range(z, z + chunk) for z in range(0, slices, chunk)]
    get_rows.wait()
    rows = normalize(cls_rows[...].astype(F32))[0].astype(BF16)
    cls_norm[...] = rows
    get_query.wait()
    get_key.wait()
    get_patches[0].wait()
    totals = {z: spread(z) for z in groups[0]}
    q = dot(rows, w_query[...]).astype(BF16)
    keys = (dot(expand(q), w_key[...], BY_COLS) * scale).astype(BF16).astype(F32)
    key_sums = jnp.sum(keys, axis=-1, keepdims=True)
    place = lax.broadcasted_iota(jnp.int32, (SLOT, width), 0)
    entry = lax.broadcasted_iota(jnp.int32, (SLOT, width), 1)
    picks = jnp.where((place == 0) | ((place == 1) & (entry == 0)), 1.0, 0.0)
    for z in range(slices):
        query_keys[z] = jnp.concatenate(
            [keys[z * SLOT : (z + 1) * SLOT], picks], axis=0
        ).astype(BF16)

    def attend(z, raw, total):
        mean = raw[SLOT : SLOT + 1] * (1.0 / width)
        off = mean - raw[SLOT + 1 : SLOT + 2]
        inv_std = lax.rsqrt(jnp.maximum(total * (1.0 / width) - off * off, 0.0) + 1e-05)
        stats[z : z + 1] = mean
        stats[slices + z : slices + z + 1] = inv_std
        here = slice(z * SLOT, (z + 1) * SLOT)
        scores = inv_std * (raw[:SLOT] - mean * key_sums[here])
        powers = jnp.exp(scores - jnp.max(scores, axis=-1, keepdims=True))
        p = powers / jnp.sum(powers, axis=-1, keepdims=True)
        probs[z] = p
        weights = (p.astype(BF16).astype(F32) * inv_std).astype(BF16)
        shift = jnp.sum(weights.astype(F32) * mean, axis=-1, keepdims=True)
        return weights, shift

    def gather(z, weights, shift):
        factor[z * SLOT : (z + 1) * SLOT] = dot(weights, patches[z]) - shift

    waiting, weighted = [], []
    for g, group in enumerate(groups):
        if g + 1 < len(groups):
            get_patches[g + 1].wait()
        ready = [(z, dot(query_keys[z], patches[z], BY_COLS)) for z in group]
        if g + 1 < len(groups):
            totals.update({z: spread(z) for z in groups[g + 1]})
        for item in weighted:
            gather(*item)
        weighted = [(z,) + attend(z, raw, totals[z]) for z, raw in waiting]
        waiting = ready
    get_value.wait()
    get_out.wait()
    for item in weighted + [(z,) + attend(z, raw, totals[z]) for z, raw in waiting]:
        gather(*item)

    value_factor = factor[...]
    pool = collapse(dot(value_factor.astype(BF16), w_value[...])).astype(BF16)
    head_terms[...] = dot(pool, w_out[...]).astype(BF16)
    pooled[...] = jnp.concatenate([q.astype(F32), pool.astype(F32)], axis=0)


def encoder_forward(patches, cls_rows, w_query, w_key, w_value, w_out):
    slices, tokens, width = patches.shape
    cols = w_query.shape[1]
    chunk = CHUNK
    far = (patches, w_query, w_key, w_value, w_out, cls_rows)
    hbm = pl.BlockSpec(memory_space=pltpu.HBM)
    vmem = pl.BlockSpec(memory_space=pltpu.VMEM)
    out_shape = [
        in_vmem(patches.shape, BF16),
        in_vmem(w_key.shape, BF16),
        in_vmem(w_value.shape, BF16),
        in_vmem(w_out.shape, BF16),
        in_vmem((slices, SLOT, tokens), F32),
        in_vmem((2 * slices, tokens), F32),
        in_vmem((slices, width), BF16),
        in_vmem((slices, width), BF16),
        in_vmem((slices * SLOT, width), F32),
        in_vmem((2 * slices, cols), F32),
    ]
    return pl.pallas_call(
        functools.partial(forward_kernel, chunk),
        in_specs=[hbm] * len(far),
        out_specs=[vmem] * len(out_shape),
        out_shape=out_shape,
        scratch_shapes=[
            pltpu.VMEM(cls_rows.shape, BF16),
            pltpu.VMEM(w_query.shape, BF16),
            pltpu.VMEM((slices, 2 * SLOT, width), BF16),
            pltpu.SemaphoreType.DMA((5,)),
            pltpu.SemaphoreType.DMA((slices // chunk,)),
        ],
        compiler_params=pltpu.CompilerParams(vmem_limit_bytes=VMEM_LIMIT),
        name="encoder_forward",
    )(*[pltpu.with_memory_space_constraint(a, pltpu.HBM) for a in far])


def sent_early(chips):
    return [chips // 2]


def halves(block):
    middle = block.shape[0] // 2
    return jnp.concatenate([block[:middle], block[middle:]], axis=1)


def from_halves(block):
    width = block.shape[1] // 2
    return jnp.concatenate([block[:, :width], block[:, width:]], axis=0)


def turn_kernel(patches, turned):
    for z in range(patches.shape[0]):
        turned[z] = patches[z].T


def turn_patches(patches):
    slices, tokens, width = patches.shape
    vmem = pl.BlockSpec(memory_space=pltpu.VMEM)
    return pl.pallas_call(
        turn_kernel,
        in_specs=[vmem],
        out_specs=vmem,
        out_shape=in_vmem((slices, width, tokens), BF16),
        compiler_params=pltpu.CompilerParams(vmem_limit_bytes=VMEM_LIMIT),
        name="turn_patches",
    )(patches)


def head_rows(x, heads):
    rows, cols = x.shape
    wide = (heads * rows, cols)
    mine = (
        lax.broadcasted_iota(jnp.int32, wide, 0) // rows
        == lax.broadcasted_iota(jnp.int32, wide, 1) // HD
    )
    tall = jnp.broadcast_to(x.astype(F32)[None], (heads, rows, cols)).reshape(wide)
    return jnp.where(mine, tall, 0.0).astype(BF16), mine


def prepare_kernel(
    heads, slices, chips, ids, up, a_out, factor, pooled, d_wide, bias, turned, early, *outs
):
    value_factor = factor[...]
    turned[...] = jnp.concatenate([jnp.zeros_like(value_factor), value_factor], axis=0).T
    rows_early = lane_blocks(pooled[...]).astype(BF16)
    early[...] = rows_early
    part = turned.shape[0] // chips
    here = lax.axis_index("gz")
    for shift, out in zip(sent_early(chips), outs):
        first = pl.multiple_of(partner(here, shift, chips) * part, SLOT)
        out[: part // 2] = halves(turned[pl.ds(first, part), slices * SLOT :]).astype(BF16)
        out[part // 2 :] = rows_early
    rows = 2 * slices
    total = ids.shape[0]
    start = (lax.axis_index("gz") * lax.axis_size("dev") + lax.axis_index("dev")) * slices
    d_pooled = dot(up[...], a_out[...], BY_COLS).astype(BF16)
    d_wide[...] = head_rows(d_pooled, heads)[0]
    square = (heads * rows, rows)
    i_of = lax.broadcasted_iota(jnp.int32, square, 0) % rows
    j_of = lax.broadcasted_iota(jnp.int32, square, 1)
    id_i = jnp.full(square, -1, jnp.int32)
    id_j = jnp.full(square, -1, jnp.int32)
    for n in range(rows):
        place = start + n
        scan = jnp.where(place < total, ids[jnp.minimum(place, total - 1)], -1)
        id_i = jnp.where(i_of == n, scan, id_i)
        id_j = jnp.where(j_of == n, scan, id_j)
    allowed = ((id_i == id_j) & (id_j >= 0)) | (i_of == j_of)
    bias[...] = jnp.where(allowed, 1.0, 0.0)


def prepare_window(ids, up, a_out, factor, pooled, slices, chips):
    cols = a_out.shape[0]
    width = a_out.shape[1]
    heads = cols // HD
    rows = 2 * slices
    below = rows * pl.cdiv(cols, LANES)
    vmem = pl.BlockSpec(memory_space=pltpu.VMEM)
    return pl.pallas_call(
        functools.partial(prepare_kernel, heads, slices, chips),
        in_specs=[pl.BlockSpec(memory_space=pltpu.SMEM)] + [vmem] * 4,
        out_specs=[vmem] * (4 + len(sent_early(chips))),
        out_shape=[
            in_vmem((heads * rows, cols), BF16),
            in_vmem((heads * rows, rows), F32),
            in_vmem((width, 2 * slices * SLOT), F32),
            in_vmem((below, LANES), BF16),
        ]
        + [in_vmem((width // chips // 2 + below, LANES), BF16)] * len(sent_early(chips)),
        compiler_params=pltpu.CompilerParams(vmem_limit_bytes=VMEM_LIMIT),
        name="prepare_window",
    )(ids, up, a_out, factor, pooled)


def choose(within, across, inside, edge):
    across = jnp.where(edge, 0.0, across.astype(F32))
    return jnp.where(inside, within.astype(F32), across)


def window_kernel(heads, own, within, across, a_query, a_key, a_value, d_wide, allowed, d_half):
    scale = float(HD) ** (-0.5)
    last = lax.axis_index("gz") == lax.axis_size("gz") - 1
    following = choose(within[...], across[...], lax.axis_index("dev") == 0, last)
    window = jnp.concatenate([own[...].astype(F32), following], axis=0)
    rows = window.shape[0]
    cols = a_query.shape[1]
    half = normalize(window)[0].astype(BF16)
    q_wide, mine = head_rows(dot(half, a_query[...]).astype(BF16), heads)
    k = dot(half, a_key[...]).astype(BF16)
    v = dot(half, a_value[...]).astype(BF16)
    scores = jnp.where(allowed[...] > 0.5, dot(q_wide, k, BY_COLS) * scale, -1e30)
    d_probs = dot(d_wide[...], v, BY_COLS)
    powers = jnp.exp(scores - jnp.max(scores, axis=-1, keepdims=True))
    probs = powers / jnp.sum(powers, axis=-1, keepdims=True)
    inner = jnp.sum(probs * d_probs, axis=-1, keepdims=True)
    d_scores = (probs * (d_probs - inner) * scale).astype(BF16)
    d_value = dot(probs.astype(BF16), d_wide[...], BY_ROWS).astype(BF16)
    d_query = jnp.where(mine, dot(d_scores, k), 0.0)
    d_query = jnp.sum(d_query.reshape(heads, rows, cols), axis=0).astype(BF16)
    d_key = dot(d_scores, q_wide, BY_ROWS).astype(BF16)
    terms = (
        dot(d_value, a_value[...], BY_COLS)
        + dot(d_query, a_query[...], BY_COLS)
        + dot(d_key, a_key[...], BY_COLS)
    )
    d_half[...] = terms.astype(BF16)


def window_gradients(own, within, across, a_query, a_key, a_value, d_wide, allowed):
    slices, width = own.shape
    heads = a_query.shape[1] // HD
    vmem = pl.BlockSpec(memory_space=pltpu.VMEM)
    return pl.pallas_call(
        functools.partial(window_kernel, heads),
        in_specs=[vmem] * 8,
        out_specs=vmem,
        out_shape=in_vmem((2 * slices, width), BF16),
        compiler_params=pltpu.CompilerParams(vmem_limit_bytes=VMEM_LIMIT),
        name="window_gradients",
    )(own, within, across, a_query, a_key, a_value, d_wide, allowed)


def backward_kernel(
    chips,
    patches,
    patches_turned,
    probs,
    stats,
    d_own,
    d_others,
    within,
    across,
    embedded,
    up,
    w_key,
    w_value,
    w_out,
    cls_norm,
    turned_value,
    early,
    *rest,
):
    outs, (turned, d_keys, factor) = rest[:chips], rest[chips:]
    scale = float(HD) ** (-0.5)
    slices = embedded.shape[0]

    carried = choose(
        within[...], across[...], lax.axis_index("dev") == 1, lax.axis_index("gz") == 0
    )
    win_norm, inv_std = normalize(embedded[...].astype(F32))
    d_normed = d_own[:slices].astype(F32) + carried[:slices]
    for n in range(d_others.shape[0]):
        d_normed = d_normed + d_others[n, :slices].astype(F32)
    centred = (
        d_normed
        - jnp.mean(d_normed, axis=-1, keepdims=True)
        - win_norm * jnp.mean(d_normed * win_norm, axis=-1, keepdims=True)
    )
    d_embed = up[:slices].astype(F32) + carried[slices:] + inv_std * centred
    d_embed = d_embed.astype(BF16)
    d_att = dot(d_embed, w_out[...], BY_COLS).astype(BF16)
    keys = dot(expand(d_att), w_value[...], BY_COLS).astype(BF16).astype(F32)
    key_sums = jnp.sum(keys, axis=-1, keepdims=True)
    d_keys[...] = keys

    def score(z):
        return dot(d_keys[z * SLOT : (z + 1) * SLOT].astype(BF16), patches_turned[z])

    def attend(z, raw):
        here = slice(z * SLOT, (z + 1) * SLOT)
        p = probs[z]
        mean = stats[z : z + 1]
        inv = stats[slices + z : slices + z + 1]
        d_probs = inv * (raw - mean * key_sums[here])
        inner = jnp.sum(p * d_probs, axis=-1, keepdims=True)
        d_scores = (p * (d_probs - inner) * scale).astype(BF16)
        weights = (d_scores.astype(F32) * inv).astype(BF16)
        shift = jnp.sum(weights.astype(F32) * mean, axis=-1, keepdims=True)
        factor[here] = dot(weights, patches[z]) - shift

    waiting = []
    for c in range(0, slices, CHUNK):
        ready = [(z, score(z)) for z in range(c, c + CHUNK)]
        for item in waiting:
            attend(*item)
        waiting = ready
    for item in waiting:
        attend(*item)

    key_factor = factor[...]
    d_query = collapse(dot(key_factor.astype(BF16), w_key[...])).astype(BF16)
    slot = lax.broadcasted_iota(jnp.int32, key_factor.shape, 0) % SLOT
    left = jnp.where(slot == SLOT - 2, slot_rows(cls_norm[...]), key_factor)
    left = jnp.where(slot == SLOT - 1, slot_rows(d_embed), left)
    right = jnp.concatenate([d_att.astype(F32), d_query.astype(F32)], axis=0)
    turned[...] = jnp.concatenate([left, jnp.zeros_like(left)], axis=0).T + turned_value[...]
    late = lane_blocks(right).astype(BF16)
    part = turned.shape[0] // chips
    middle = part + late.shape[0]
    here = lax.axis_index("gz")
    for shift in range(chips):
        first = pl.multiple_of(partner(here, shift, chips) * part, SLOT)
        if shift in sent_early(chips):
            keyed = turned[pl.ds(first, part), : slices * SLOT]
            outs[shift][: part // 2] = halves(keyed).astype(BF16)
            outs[shift][part // 2 :] = late
            continue
        outs[shift][:part] = turned[pl.ds(first, part), :].astype(BF16)
        outs[shift][part:middle] = late
        outs[shift][middle:] = early[...]


def encoder_backward(
    patches, patches_turned, probs, stats, d_own, d_others, within, across, embedded, up, w_key, w_value, w_out,
    cls_norm, turned_value, early, chips,
):
    slices, tokens, width = patches.shape
    cols = w_key.shape[1]
    vmem = pl.BlockSpec(memory_space=pltpu.VMEM)
    below = 2 * slices * pl.cdiv(cols, LANES)
    short, full = (width // chips // 2 + below, LANES), (width // chips + 2 * below, LANES)
    shapes = [short if shift in sent_early(chips) else full for shift in range(chips)]
    return pl.pallas_call(
        functools.partial(backward_kernel, chips),
        in_specs=[vmem] * 16,
        out_specs=[vmem] * chips,
        out_shape=[in_vmem(shape, BF16) for shape in shapes],
        scratch_shapes=[
            pltpu.VMEM((width, LANES), F32),
            pltpu.VMEM((slices * SLOT, width), F32),
            pltpu.VMEM((slices * SLOT, width), F32),
        ],
        compiler_params=pltpu.CompilerParams(vmem_limit_bytes=VMEM_LIMIT),
        name="encoder_backward",
    )(
        patches, patches_turned, probs, stats, d_own, d_others, within, across, embedded, up, w_key, w_value, w_out,
        cls_norm, turned_value, early,
    )


def assemble_kernel(slices, cols, part, chips, *refs):
    *messages, kept, sent = refs
    messages, early = messages[:chips], dict(zip(sent_early(chips), messages[chips:]))
    mask = head_mask(slices, cols)
    slot = lax.broadcasted_iota(jnp.int32, mask.shape, 0) % SLOT
    depth = slices * SLOT
    rows = 2 * slices * pl.cdiv(cols, LANES)
    keyed, valued, first, second = [], [], [], []
    for shift, m in enumerate(messages):
        if shift in early:
            e = early[shift]
            keyed.append(from_halves(m[: part // 2].astype(F32)))
            valued.append(from_halves(e[: part // 2].astype(F32)))
            ends = ((m, part // 2, second), (e, part // 2, first))
        else:
            keyed.append(m[:part, :depth].astype(F32))
            valued.append(m[:part, depth:].astype(F32))
            ends = ((m, part, second), (m, part + rows, first))
        for source, start, into in ends:
            block = from_lane_blocks(source[start : start + rows].astype(F32), cols)
            into.append([slot_rows(block[:slices]), slot_rows(block[slices:])])
    left_key = jnp.concatenate(keyed, axis=1).astype(BF16)
    left_value = jnp.concatenate(valued, axis=1).astype(BF16)

    def right(blocks):
        return jnp.concatenate(blocks, axis=0).astype(BF16)

    grads = [
        dot(left_key, right([jnp.where(slot == SLOT - 2, b[1], 0.0) for b in second])),
        dot(left_key, right([jnp.where(mask, b[0], 0.0) for b in first])),
        dot(left_value, right([jnp.where(mask, b[0], 0.0) for b in second])),
        dot(left_key, right([jnp.where(slot == SLOT - 1, b[1], 0.0) for b in first])),
    ]
    lower = lax.axis_index("dev") == 0
    half = part // 2
    for n, total in enumerate(grads):
        top, bottom = total[:half], total[half:]
        kept[n] = jnp.where(lower, top, bottom)
        sent[n] = jnp.where(lower, bottom, top).astype(BF16)


def assemble(messages, early, slices, cols, part):
    vmem = pl.BlockSpec(memory_space=pltpu.VMEM)
    shape = (4, part // 2, cols)
    return pl.pallas_call(
        functools.partial(assemble_kernel, slices, cols, part, len(messages)),
        in_specs=[vmem] * (len(messages) + len(early)),
        out_specs=[vmem, vmem],
        out_shape=[in_vmem(shape, F32), in_vmem(shape, BF16)],
        compiler_params=pltpu.CompilerParams(vmem_limit_bytes=VMEM_LIMIT),
        name="assemble",
    )(*messages, *early)


def finish_kernel(kept, arrived, *refs):
    outs, sums, sems = refs[:4], refs[4], refs[5]
    copies = []
    for n, out in enumerate(outs):
        sums[n] = kept[n] + arrived[n].astype(F32)
        copy = pltpu.make_async_copy(sums.at[n], out, sems.at[n])
        copy.start()
        copies.append(copy)
    for copy in copies:
        copy.wait()


def finish(kept, arrived):
    vmem = pl.BlockSpec(memory_space=pltpu.VMEM)
    return pl.pallas_call(
        finish_kernel,
        in_specs=[vmem, vmem],
        out_specs=[pl.BlockSpec(memory_space=pltpu.HBM)] * 4,
        out_shape=[pltpu.HBM(kept.shape[1:], F32)] * 4,
        scratch_shapes=[pltpu.VMEM(kept.shape, F32), pltpu.SemaphoreType.DMA((4,))],
        compiler_params=pltpu.CompilerParams(vmem_limit_bytes=VMEM_LIMIT),
        name="finish",
    )(kept, arrived)


def ring_shift(x, axis, distance):
    size = lax.axis_size(axis)
    return lax.ppermute(x, axis, [(i, (i + distance) % size) for i in range(size)])


def others(x):
    return [ring_shift(x, "ma", d) for d in range(1, lax.axis_size("ma"))]


def pair_route():
    chips, parts, cores = [lax.axis_size(a) for a in ("gz", "ma", "dev")]
    route = []
    for chip in range(chips):
        for part in range(parts):
            for core in range(cores):
                place = chip * cores + core
                other = place + 1 if core else place - 1
                at = part
                if not 0 <= other < chips * cores:
                    other, at = place, part ^ 1
                    if at >= parts:
                        continue
                source = (chip * parts + part) * cores + core
                route.append((source, (other // cores * parts + at) * cores + other % cores))
    return route


def neighbours(block):
    within = ring_shift(block, "dev", 1)
    return within, lax.ppermute(block, ("gz", "ma", "dev"), pair_route())


def exchanged(x, axis, shift):
    size = lax.axis_size(axis)
    return lax.ppermute(x, axis, [(i, partner(i, shift, size)) for i in range(size)])


def local(
    patches,
    cls_rows,
    w_query,
    w_key,
    w_value,
    w_out,
    a_query,
    a_key,
    a_value,
    a_out,
    upstream,
    slice_to_scan,
):
    slices, _, width = patches.shape
    cols = w_query.shape[1]
    chips = lax.axis_size("gz")
    up = upstream[0]
    (
        held, key_held, value_held, out_held, probs, stats, cls_norm, head_terms, factor, pooled
    ) = encoder_forward(patches, cls_rows, w_query, w_key, w_value, w_out)
    held_turned = turn_patches(held)
    d_wide, allowed, turned_value, early, *ahead = prepare_window(
        slice_to_scan, up, a_out, factor, pooled, slices, chips
    )
    total = head_terms.astype(F32)
    arriving = others(head_terms)
    arriving, held_turned = lax.optimization_barrier((arriving, held_turned))
    for term in arriving:
        total = total + term.astype(F32)
    embedded = (cls_rows.astype(F32) + total).astype(BF16)
    following = neighbours(embedded)
    d_own = window_gradients(embedded, *following, a_query, a_key, a_value, d_wide, allowed)
    d_others = others(d_own)
    ahead, d_own = lax.optimization_barrier((ahead, d_own))
    ahead = [exchanged(m, "gz", n) for n, m in zip(sent_early(chips), ahead)]
    d_others = jnp.stack(d_others)
    lower = d_own[slices:].astype(F32)
    for n in range(d_others.shape[0]):
        lower = lower + d_others[n, slices:].astype(F32)
    carried = neighbours(jnp.concatenate([lower.astype(BF16), up[slices:]], axis=0))
    carried, ahead = lax.optimization_barrier((carried, ahead))
    messages = encoder_backward(
        held, held_turned, probs, stats, d_own, d_others, *carried, embedded, up, key_held, value_held, out_held,
        cls_norm, turned_value, early, chips,
    )
    order = range(chips - 1, 0, -1)
    arrived = list(messages[:1]) + [exchanged(messages[n], "gz", n) for n in order]
    kept, sent = assemble(arrived, ahead, slices, cols, width // chips)
    return tuple(finish(kept, ring_shift(sent, "dev", 1)))


def solution(mesh):
    return jax.shard_map(
        local,
        mesh=mesh,
        in_specs=(
            P(("grp", "gz", "dev"), None, None),
            P(("grp", "gz", "dev"), None),
            P(None, "ma"),
            P(None, "ma"),
            P(None, "ma"),
            P("ma", None),
            P(None, "ma"),
            P(None, "ma"),
            P(None, "ma"),
            P("ma", None),
            P(("grp", "gz", "dev"), None, None),
            P("grp"),
        ),
        out_specs=(
            P(("grp", "gz", "dev"), "ma"),
            P(("grp", "gz", "dev"), "ma"),
            P(("grp", "gz", "dev"), "ma"),
            P(("grp", "gz", "dev"), "ma"),
        ),
        check_vma=False,
    )
```
